32 devices in a mesh: seq: 8 (over y, x, core), head: 4 (over z).
Axes of the slice: x: 2, y: 2, z: 4, core: 2. Of those that a mesh axis runs over, the one named last changes fastest.
Arguments:
- attn_q: bfloat16 [8192, 5120], P('seq', 'head'), may hold values from -6 to 6
- attn_k: bfloat16 [8192, 5120], P('seq', 'head'), may hold values from -6 to 6
- attn_v: bfloat16 [8192, 5120], P('seq', 'head'), may hold values from -6 to 6
- fast_q: bfloat16 [8192, 5120], P('seq', 'head'), may hold values from -6 to 6
- fast_k: bfloat16 [8192, 5120], P('seq', 'head'), may hold values from -6 to 6
- fast_v: bfloat16 [8192, 5120], P('seq', 'head'), may hold values from -6 to 6
- rates: float32 [8192, 8], P('seq', 'head'), may hold values from 0.00022097086 to 0.0022097088
- fast_gate: float32 [8, 640, 640], P('head'), may hold values from -0.25 to 0.25
- fast_up: float32 [8, 640, 640], P('head'), may hold values from -0.25 to 0.25
- fast_down: float32 [8, 640, 640], P('head'), may hold values from -0.25 to 0.25
Outputs:
- mixed: bfloat16 [8192, 5120], P('seq', 'head')
The draws below stay inside these ranges and needn't reach their ends.
All inputs are finite; a program needn't handle non-finite values.
Results may differ from the reference program's by a relative error of at most 0.012.
Values may be sent and summed in bfloat16 or wider, within the bound.
No kernel may reach another device: no remote copies, remote signals or barrier semaphores. Data moves between devices by JAX's collectives and lax.ppermute only.
A program may use at most 192 MiB of HBM per device.

```python
import math
import jax
import jax.numpy as jnp
from jax import lax

HEADS = 40
HD = 128
FW_HEADS = 8
FWD = 640
WINDOW = 1024
TOK_DEV = 1024
TOKENS = 8192
D = 5120


def drawn_pair(key):
    base = jax.random.fold_in(key, 1234)
    key_query, key_keys = jax.random.split(base, 2)
    array_shape = (TOKENS, HEADS * HD)
    queries = jax.random.truncated_normal(key_query, -6.0, 6.0, array_shape, jnp.float32)
    key_rows = jax.random.truncated_normal(key_keys, -6.0, 6.0, array_shape, jnp.float32)
    return (queries, key_rows)


def draw_attn_q(key, part):
    return drawn_pair(key)[0].astype(jnp.bfloat16)


def draw_attn_k(key, part):
    return drawn_pair(key)[1].astype(jnp.bfloat16)


def levels(own_key, extent, cuts, least, high):
    def one(position, shards_of):
        heights = jax.random.uniform(jax.random.fold_in(jax.random.fold_in(own_key, 6), position), (shards_of,), jnp.float32, least / len(cuts), high / len(cuts))
        return jnp.repeat(jnp.exp(heights), extent[position] // shards_of).reshape((-1,) + (1,) * (len(extent) - position - 1))

    factor_of = one(*cuts[0])
    for cut in cuts[1:]:
        factor_of = factor_of * one(*cut)
    return factor_of


def normal_values(key, shape, deviation, limit, pieces=(), kind=jnp.bfloat16):
    values = deviation * jax.random.normal(key, shape, jnp.float32)
    if pieces:
        values = values * levels(key, shape, pieces, -0.22, 0.18)
    return jnp.clip(values, -limit, limit).astype(kind)


def setup_inputs(seed: int = 0) -> dict:
    arg_keys = jax.random.split(jax.random.key(seed), 11)
    attn_q = draw_attn_q(jax.random.fold_in(arg_keys[10], 71), 0)
    attn_k = draw_attn_k(jax.random.fold_in(arg_keys[10], 71), 0)
    attn_v = normal_values(arg_keys[2], (TOKENS, D), 1.0, 6.0, ((0, 8), (1, 4)))
    fast_q = normal_values(arg_keys[3], (TOKENS, D), 1.0, 6.0, ((0, 8), (1, 4)))
    fast_k = normal_values(arg_keys[4], (TOKENS, D), 1.0, 6.0, ((0, 8), (1, 4)))
    fast_v = normal_values(arg_keys[5], (TOKENS, D), 1.0, 6.0, ((0, 8), (1, 4)))
    rates = jnp.clip(jnp.exp(math.log(0.0022097088) - 2.3025852 * jax.random.uniform(arg_keys[6], (TOKENS, FW_HEADS), jnp.float32) ** levels(arg_keys[6], (TOKENS, FW_HEADS), ((0, 8), (1, 4)), -0.2, 0.2)), 0.00022097086, 0.0022097088)
    fast_gate = normal_values(arg_keys[7], (FW_HEADS, FWD, FWD), FWD ** -0.5, 0.25, ((0, 4),), jnp.float32)
    fast_up = normal_values(arg_keys[8], (FW_HEADS, FWD, FWD), FWD ** -0.5, 0.25, ((0, 4),), jnp.float32)
    fast_down = normal_values(arg_keys[9], (FW_HEADS, FWD, FWD), FWD ** -0.5, 0.25, ((0, 4),), jnp.float32)
    return dict(attn_q=attn_q, attn_k=attn_k, attn_v=attn_v, fast_q=fast_q, fast_k=fast_k, fast_v=fast_v, rates=rates, fast_gate=fast_gate, fast_up=fast_up, fast_down=fast_down)


epsilon = 1e-06

def attention(attn_q, attn_k, attn_v):
    block_rows = min(512, TOK_DEV)
    inverse_root = 1.0 / math.sqrt(HD)
    zero_rim = jnp.zeros((WINDOW, HEADS * HD), attn_k.dtype)
    ext_keys = jnp.concatenate([zero_rim, attn_k], axis=0)
    ext_values = jnp.concatenate([zero_rim, attn_v], axis=0)

    def one_block(block_index):
        first_row = (block_index * block_rows).astype(jnp.int32)
        query = lax.dynamic_slice_in_dim(attn_q, first_row, block_rows, 0).astype(jnp.float32).reshape(block_rows, HEADS, HD)
        key_block = lax.dynamic_slice_in_dim(ext_keys, first_row, WINDOW + block_rows, 0).astype(jnp.float32).reshape(WINDOW + block_rows, HEADS, HD)
        value_block = lax.dynamic_slice_in_dim(ext_values, first_row, WINDOW + block_rows, 0).astype(jnp.float32).reshape(WINDOW + block_rows, HEADS, HD)
        scores = jnp.einsum('qhd,khd->hqk', query, key_block, precision=lax.Precision.HIGHEST) * inverse_root
        query_pos = first_row + jnp.arange(block_rows, dtype=jnp.int32)
        key_pos = first_row - WINDOW + jnp.arange(WINDOW + block_rows, dtype=jnp.int32)
        distance = query_pos[:, None] - key_pos[None, :]
        allowed = (distance >= 0) & (distance <= WINDOW) & (key_pos[None, :] >= 0)
        scores = jnp.where(allowed[None], scores, -jnp.inf)
        row_max = lax.optimization_barrier(jnp.max(scores, axis=-1, keepdims=True))
        expo = jnp.exp(scores - row_max)
        weights = (expo / lax.optimization_barrier(jnp.sum(expo, axis=-1, keepdims=True))).astype(jnp.bfloat16)
        result = jnp.einsum('hqk,khd->qhd', weights.astype(jnp.float32), value_block, precision=lax.Precision.HIGHEST)
        return result.reshape(block_rows, HEADS * HD)
    blocks = lax.map(one_block, jnp.arange(TOKENS // block_rows, dtype=jnp.int32))
    return blocks.reshape(TOKENS, HEADS * HD)

def renorm(previous, gradient):
    updated = previous - gradient
    old_norm = jnp.sqrt(lax.optimization_barrier(jnp.sum(previous * previous, axis=-2, keepdims=True)))
    new_norm = jnp.sqrt(lax.optimization_barrier(jnp.sum(updated * updated, axis=-2, keepdims=True)) + epsilon)
    return updated * (old_norm / new_norm)

def reference(attn_q, attn_k, attn_v, fast_q, fast_k, fast_v, rates, fast_gate, fast_up, fast_down):
    attended = attention(attn_q, attn_k, attn_v)
    applied_list = []
    for head_index in range(FW_HEADS):
        cols = slice(head_index * FWD, (head_index + 1) * FWD)
        key_rows = fast_k[:, cols]
        gate_b = fast_gate[head_index].astype(jnp.bfloat16)
        up_b = fast_up[head_index].astype(jnp.bfloat16)
        down_b = fast_down[head_index].astype(jnp.bfloat16)
        pre_gate = jnp.dot(key_rows, gate_b, preferred_element_type=jnp.float32)
        pre_up = jnp.dot(key_rows, up_b, preferred_element_type=jnp.float32)
        activated = jax.nn.silu(pre_gate)
        hidden = (activated * pre_up).astype(jnp.bfloat16)
        out_grad = (-rates[:, head_index:head_index + 1] * fast_v[:, cols].astype(jnp.float32)).astype(jnp.bfloat16)
        hidden_grad = jnp.dot(out_grad, down_b.T, preferred_element_type=jnp.float32)
        sigma = jax.nn.sigmoid(pre_gate)
        gate_grad = (hidden_grad * pre_up * sigma * (1.0 + pre_gate * (1.0 - sigma))).astype(jnp.bfloat16)
        up_grad = (hidden_grad * activated).astype(jnp.bfloat16)
        grad_gate = jnp.dot(key_rows.T, gate_grad, preferred_element_type=jnp.float32)
        grad_up = jnp.dot(key_rows.T, up_grad, preferred_element_type=jnp.float32)
        grad_down = jnp.dot(hidden.T, out_grad, preferred_element_type=jnp.float32)
        new_gate = renorm(fast_gate[head_index], grad_gate).astype(jnp.bfloat16)
        new_up = renorm(fast_up[head_index], grad_up).astype(jnp.bfloat16)
        new_down = renorm(fast_down[head_index], grad_down).astype(jnp.bfloat16)
        query_rows = fast_q[:, cols]
        query_gate = jnp.dot(query_rows, new_gate, preferred_element_type=jnp.float32)
        query_up = jnp.dot(query_rows, new_up, preferred_element_type=jnp.float32)
        query_hidden = (jax.nn.silu(query_gate) * query_up).astype(jnp.bfloat16)
        applied_list.append(jnp.dot(query_hidden, new_down, preferred_element_type=jnp.float32))
    applied = jnp.concatenate(applied_list, axis=1)
    return (attended + applied).astype(jnp.bfloat16)
```

```python
import functools
import math

import jax
import jax.numpy as jnp
from jax import lax
from jax.experimental import pallas as pl
from jax.experimental.pallas import tpu as pltpu
from jax.sharding import PartitionSpec as P


HD = 128
WINDOW = 1024
EPS = 1e-06


def attn_kernel(first_ref, q_ref, kp_ref, vp_ref, ko_ref, vo_ref, o_ref, s0, s1, *, bq):
    rows, cols = q_ref.shape
    tiles = rows // bq
    c = math.log2(math.e) / math.sqrt(HD)
    ri = lax.broadcasted_iota(jnp.int32, (bq, bq), 0)
    ci = lax.broadcasted_iota(jnp.int32, (bq, bq), 1)
    first = first_ref[0] == 1
    bufs = (s0, s1)
    units = [(h, t) for h in range(cols // HD) for t in range(tiles)]

    def scores(i):
        h, t = units[i]
        hs = slice(h * HD, (h + 1) * HD)
        r0, r1 = t * bq, (t + 1) * bq
        before = rows - r0
        q = q_ref[r0:r1, hs]
        mul = lambda k: lax.dot_general(q, k, (((1,), (1,)), ((), ())), preferred_element_type=jnp.float32)
        sp = mul(kp_ref[r0:, hs])
        so = mul(ko_ref[:r1, hs])
        edge = jnp.where(ci >= ri, sp[:, :bq], -jnp.inf)
        sp = jnp.concatenate([edge, sp[:, bq:]], axis=1) if before > bq else edge
        diag = jnp.where(ci <= ri, so[:, r0:], -jnp.inf)
        so = jnp.concatenate([so[:, :r0], diag], axis=1) if t else diag
        bufs[i % 2][:, :before] = sp
        bufs[i % 2][:, before:] = so
        mp = jnp.max(sp, axis=1, keepdims=True)
        mo = jnp.max(so, axis=1, keepdims=True)
        m = jnp.maximum(mo, jnp.where(first, -jnp.inf, mp)) * c
        return jnp.where(first, 1e30, m), m

    def finish(i, mp, mo):
        h, t = units[i]
        hs = slice(h * HD, (h + 1) * HD)
        r0, r1 = t * bq, (t + 1) * bq
        before = rows - r0
        buf = bufs[i % 2]
        pp = jnp.exp2(buf[:, :before] * c - mp)
        po = jnp.exp2(buf[:, before:] * c - mo)
        total = jnp.sum(pp, axis=1, keepdims=True) + jnp.sum(po, axis=1, keepdims=True)
        o = jnp.dot(pp.astype(jnp.bfloat16), vp_ref[r0:, hs], preferred_element_type=jnp.float32)
        o = o + jnp.dot(po.astype(jnp.bfloat16), vo_ref[:r1, hs], preferred_element_type=jnp.float32)
        o_ref[r0:r1, hs] = (o / total).astype(o_ref.dtype)

    ms = scores(0)
    for i in range(len(units)):
        nxt = scores(i + 1) if i + 1 < len(units) else None
        finish(i, *ms)
        ms = nxt


def attention(first, group, width, q, halo, ko, vo, bq):
    rows = q.shape[0]
    w = width * HD
    here = pl.BlockSpec((rows, w), lambda i, f: (0, group))
    low = pl.BlockSpec((rows, w), lambda i, f: (0, 0))
    high = pl.BlockSpec((rows, w), lambda i, f: (0, 1))
    pairs = rows * (WINDOW + bq) * width
    return pl.pallas_call(
        functools.partial(attn_kernel, bq=bq),
        grid_spec=pltpu.PrefetchScalarGridSpec(
            num_scalar_prefetch=1,
            grid=(1,),
            in_specs=[here, low, high, here, here],
            out_specs=low,
            scratch_shapes=[pltpu.VMEM((bq, WINDOW + bq), jnp.float32)] * 2,
        ),
        out_shape=jax.ShapeDtypeStruct((rows, w), jnp.bfloat16),
        cost_estimate=pl.CostEstimate(
            flops=4 * pairs * HD, bytes_accessed=rows * w * 12, transcendentals=pairs
        ),
        name="attn",
    )(first, q, halo, halo, ko, vo)


def grad_kernel(h_ref,x_ref,v_ref,r_ref,w1_ref,w3_ref,w2_ref,g_ref,gu,hid,og):
    F=w1_ref.shape[2]
    rows=x_ref.shape[0]
    tm=256
    w1=w1_ref[0].astype(jnp.bfloat16); w3=w3_ref[0].astype(jnp.bfloat16); w2=w2_ref[0].astype(jnp.bfloat16)
    hi=h_ref[0]
    nh=r_ref.shape[1]
    def body(t,_):
        r=pl.ds(pl.multiple_of(t*tm,tm),tm)
        x=x_ref[r,:]
        pg=jnp.dot(x,w1,preferred_element_type=jnp.float32)
        pu=jnp.dot(x,w3,preferred_element_type=jnp.float32)
        rr=r_ref[r,:]
        lane=lax.broadcasted_iota(jnp.int32,(tm,nh),1)
        rate=jnp.sum(jnp.where(lane==hi,rr,0.0),axis=1,keepdims=True)
        o=(-rate*v_ref[r,:].astype(jnp.float32)).astype(jnp.bfloat16)
        hg=lax.dot_general(o,w2,(((1,),(1,)),((),())),preferred_element_type=jnp.float32)
        sg=jax.nn.sigmoid(pg)
        act=pg*sg
        gu[r,:F]=(hg*pu*sg*(1.0+pg*(1.0-sg))).astype(jnp.bfloat16)
        gu[r,F:]=(hg*act).astype(jnp.bfloat16)
        hid[r,:]=(act*pu).astype(jnp.bfloat16)
        og[r,:]=o
        return 0
    lax.fori_loop(0,rows//tm,body,0)
    tn=128
    def body2(j,_):
        cs=pl.ds(pl.multiple_of(j*tn,tn),tn)
        g_ref[cs,:]=lax.dot_general(gu[:,cs],x_ref[...],(((0,),(0,)),((),())),preferred_element_type=jnp.float32).astype(g_ref.dtype)
        return 0
    lax.fori_loop(0,2*F//tn,body2,0)
    def body3(j,_):
        cs=pl.ds(pl.multiple_of(j*tn,tn),tn)
        rs=pl.ds(pl.multiple_of(2*F+j*tn,tn),tn)
        g_ref[rs,:]=lax.dot_general(og[:,cs],hid[...],(((0,),(0,)),((),())),preferred_element_type=jnp.float32).astype(g_ref.dtype)
        return 0
    lax.fori_loop(0,F//tn,body3,0)


def gradients(h,fk,fv,rates,w1,w3,w2):
    rows=fk.shape[0]; F=w1.shape[1]; nh=rates.shape[1]
    col=pl.BlockSpec((rows,F),lambda i,h:(0,h[0]))
    wsp=pl.BlockSpec((1,F,F),lambda i,h:(h[0],0,0))
    return pl.pallas_call(grad_kernel,
        grid_spec=pltpu.PrefetchScalarGridSpec(num_scalar_prefetch=1,grid=(1,),
            in_specs=[col,col,pl.BlockSpec((rows,nh),lambda i,h:(0,0)),wsp,wsp,wsp],
            out_specs=pl.BlockSpec((3*F,F),lambda i,h:(0,0)),
            scratch_shapes=[pltpu.VMEM((rows,2*F),jnp.bfloat16),pltpu.VMEM((rows,F),jnp.bfloat16),pltpu.VMEM((rows,F),jnp.bfloat16)]),
        out_shape=jax.ShapeDtypeStruct((3*F,F),jnp.bfloat16),
        cost_estimate=pl.CostEstimate(flops=12*rows*F*F,bytes_accessed=rows*F*4+F*F*18,transcendentals=rows*F),
        name="grads")(h,fk,fv,rates,w1,w3,w2)


def apply_kernel(h_ref,q_ref,n_ref,a_ref,o_in,o_ref):
    F=n_ref.shape[1]
    h=lax.dot_general(q_ref[...],n_ref[:2*F,:],(((1,),(1,)),((),())),preferred_element_type=jnp.float32)
    g=h[:,:F]
    hid=(g*jax.nn.sigmoid(g)*h[:,F:]).astype(jnp.bfloat16)
    out=lax.dot_general(hid,n_ref[2*F:,:],(((1,),(1,)),((),())),preferred_element_type=jnp.float32)
    o_ref[...]=(a_ref[...].astype(jnp.float32)+out).astype(o_ref.dtype)


def apply_head(h,fq,n,att,out_in=None):
    rows,cols=fq.shape; F=n.shape[1]; tm=256
    col=pl.BlockSpec((tm,F),lambda i,h:(i,h[0]))
    args=[h,fq,n,att]
    ins=[col,pl.BlockSpec((3*F,F),lambda i,h:(0,0)),col]
    if out_in is not None:
        args.append(out_in); ins.append(pl.BlockSpec(memory_space=pl.ANY)); kern=apply_kernel; al={4:0}
    else:
        kern=lambda h,q,n,a,o: apply_kernel(h,q,n,a,None,o); al={}
    return pl.pallas_call(kern,
        grid_spec=pltpu.PrefetchScalarGridSpec(num_scalar_prefetch=1,grid=(rows//tm,),in_specs=ins,out_specs=col),
        out_shape=jax.ShapeDtypeStruct((rows,cols),jnp.bfloat16),input_output_aliases=al,
        cost_estimate=pl.CostEstimate(flops=6*rows*F*F,bytes_accessed=rows*F*6+F*F*6,transcendentals=rows*F),
        name="apply")(*args)


def exchange(block, bit):
    size = lax.axis_size("seq")
    return lax.ppermute(block, "seq", [(i, i ^ (1 << bit)) for i in range(size)])


def shifted(block):
    size = lax.axis_size("seq")
    return lax.ppermute(block, "seq", [(i, i + 1) for i in range(size - 1)])


def halve(total, bit, position):
    half = total.shape[0] // 2
    mine = (position >> bit) & 1
    away = lax.dynamic_slice_in_dim(total, (1 - mine) * half, half, 0).astype(jnp.bfloat16)
    kept = lax.dynamic_slice_in_dim(total, mine * half, half, 0)
    other = exchange(away, bit)
    return kept + other.astype(jnp.float32), mine * half


def double(part, bit, position):
    mine = (position >> bit) & 1
    other = exchange(part, bit)
    low = jnp.where(mine == 0, part, other)
    high = jnp.where(mine == 0, other, part)
    return jnp.concatenate([low, high], axis=0)


def renorm(old, grad):
    new = old - grad
    old_sq = jnp.sum(old * old, axis=-1, keepdims=True)
    new_sq = jnp.sum(new * new, axis=-1, keepdims=True)
    return (new * (jnp.sqrt(old_sq) / jnp.sqrt(new_sq + EPS))).astype(jnp.bfloat16)


def synced(total, old, bits, position):
    offset = 0
    for bit in bits:
        total, moved = halve(total, bit, position)
        offset = offset + moved
    part = renorm(lax.dynamic_slice_in_dim(old, offset, total.shape[0], 0), total)
    for bit in reversed(bits):
        part = double(part, bit, position)
    return part


def shards(attn_q, attn_k, attn_v, fast_q, fast_k, fast_v, rates, fast_gate, fast_up, fast_down):
    position = lax.axis_index("seq")
    count = lax.axis_size("seq")
    bits = list(range(count.bit_length() - 1))
    heads = fast_gate.shape[0]
    span = attn_q.shape[1] // HD
    width = 2 if span % 2 == 0 else 1
    w = width * HD
    halos = []
    for g in range(span // width):
        cols = slice(g * w, (g + 1) * w)
        packed = jnp.concatenate([attn_k[:, cols], attn_v[:, cols]], axis=1)
        halos.append(shifted(packed))
    scalar = lambda x: jnp.asarray(x, jnp.int32).reshape(1)
    grads = lambda h: gradients(scalar(h), fast_k, fast_v, rates, fast_gate, fast_up, fast_down)
    if heads == 2:
        own = position & 1
        theirs = grads(1 - own)
        received = exchange(theirs, 0)
        mine = grads(own)
        totals = [mine.astype(jnp.float32) + received.astype(jnp.float32)]
        order = [own]
        bits = bits[1:]
    else:
        order = list(range(heads))
        totals = [grads(h).astype(jnp.float32) for h in order]
    news = []
    for h, total in zip(order, totals):
        pick = lambda w: lax.dynamic_index_in_dim(w, h, 0, keepdims=False).T
        old = jnp.concatenate([pick(fast_gate), pick(fast_up), pick(fast_down)], axis=0)
        middle = total.shape[0] // 2
        top = synced(total[:middle], old[:middle], bits, position)
        bottom = synced(total[middle:], old[middle:], bits[::-1], position)
        news.append(jnp.concatenate([top, bottom], axis=0))
    if heads == 2:
        news.append(exchange(news[0], 0))
        order.append(1 - order[0])
    first = scalar(position == 0)
    bq = min(256, attn_q.shape[0])
    attended = []
    for g, halo in enumerate(halos):
        attended.append(attention(first, g, width, attn_q, halo, attn_k, attn_v, bq))
    attended = jnp.concatenate(attended, axis=1)
    mixed = None
    for h, new in zip(order, news):
        mixed = apply_head(scalar(h), fast_q, new, attended, mixed)
    return mixed


def solution(mesh):
    placed = (P("seq", "head"),) * 7 + (P("head", None, None),) * 3
    return jax.shard_map(shards, mesh=mesh, in_specs=placed, out_specs=P("seq", "head"), check_vma=False)
```

```python
import functools
import math

import jax
import jax.numpy as jnp
from jax import lax
from jax.experimental import pallas as pl
from jax.experimental.pallas import tpu as pltpu
from jax.sharding import PartitionSpec as P


HD = 128
WINDOW = 1024
EPS = 1e-06
NN = (((1,), (0,)), ((), ()))
NT = (((1,), (1,)), ((), ()))
TN = (((0,), (0,)), ((), ()))


def mm(a, b, dims=NN):
    return lax.dot_general(a, b, dims, preferred_element_type=jnp.float32)


def scalars(*values):
    return jnp.stack([jnp.asarray(v, jnp.int32) for v in values])


def attn_kernel(first_ref, q_ref, *refs, bq, tile0, tiles, parts):
    kps, vps = refs[:parts], refs[parts : 2 * parts]
    ko_ref, vo_ref = refs[2 * parts : 2 * parts + 2]
    o_ref, s0, s1 = refs[-3:]
    part_rows = kps[0].shape[0]
    cols = q_ref.shape[1]
    base = WINDOW - parts * part_rows
    c = math.log2(math.e) / math.sqrt(HD)
    ri = lax.broadcasted_iota(jnp.int32, (bq, bq), 0)
    ci = lax.broadcasted_iota(jnp.int32, (bq, bq), 1)
    first = first_ref[0] == 1
    bufs = (s0, s1)
    units = [(h, t) for h in range(cols // HD) for t in range(tile0, tile0 + tiles)]

    def pieces(t, prevs, own, hs):
        out = []
        at = 0
        for i, ref in enumerate(prevs):
            lo = max(t * bq - base - i * part_rows, 0)
            if lo < part_rows:
                out.append((ref[lo:, hs], at))
                at += part_rows - lo
        return out, (own[: (t + 1) * bq, hs], at)

    def scores(i):
        h, t = units[i]
        hs = slice(h * HD, (h + 1) * HD)
        r0 = t * bq
        before = WINDOW - r0
        buf = bufs[i % 2]
        q = q_ref[r0 - tile0 * bq : r0 - tile0 * bq + bq, hs]
        prev, (ko, at) = pieces(t, kps, ko_ref, hs)
        mp = None
        for k, start in prev:
            s = mm(q, k, NT)
            if start == 0:
                edge = jnp.where(ci >= ri, s[:, :bq], -jnp.inf)
                s = jnp.concatenate([edge, s[:, bq:]], axis=1) if s.shape[1] > bq else edge
            buf[:, start : start + s.shape[1]] = s
            top = jnp.max(s, axis=1, keepdims=True)
            mp = top if mp is None else jnp.maximum(mp, top)
        so = mm(q, ko, NT)
        diag = jnp.where(ci <= ri, so[:, r0:], -jnp.inf)
        so = jnp.concatenate([so[:, :r0], diag], axis=1) if t else diag
        buf[:, before:] = so
        mo = jnp.max(so, axis=1, keepdims=True)
        m = jnp.maximum(mo, jnp.where(first, -jnp.inf, mp)) * c
        return jnp.where(first, 1e30, m), m

    def finish(i, mp, mo):
        h, t = units[i]
        hs = slice(h * HD, (h + 1) * HD)
        buf = bufs[i % 2]
        prev, own = pieces(t, vps, vo_ref, hs)
        out = total = None
        for (v, start), m in [(p, mp) for p in prev] + [(own, mo)]:
            p = jnp.exp2(buf[:, start : start + v.shape[0]] * c - m)
            part = jnp.sum(p, axis=1, keepdims=True)
            o = mm(p.astype(jnp.bfloat16), v)
            total = part if total is None else total + part
            out = o if out is None else out + o
        r0 = (t - tile0) * bq
        o_ref[r0 : r0 + bq, hs] = (out / total).astype(o_ref.dtype)

    ms = scores(0)
    for i in range(len(units)):
        nxt = scores(i + 1) if i + 1 < len(units) else None
        finish(i, *ms)
        ms = nxt


def attention(first, half, q, halos, ko, vo, bq, width, into=None):
    rows, cols = q.shape
    w = width * HD
    part_rows = halos[0].shape[0] // 2
    parts = len(halos)
    mine = pl.BlockSpec((rows // 2, w), lambda g, f: (half, g))
    upper = pl.BlockSpec((part_rows, w), lambda g, f: (0, g))
    lower = pl.BlockSpec((part_rows, w), lambda g, f: (1, g))
    here = pl.BlockSpec((rows // 2 * (half + 1), w), lambda g, f: (0, g))
    tiles = rows // 2 // bq
    pairs = rows // 2 * (WINDOW + bq) * cols // HD
    args = [first, q, *halos, *halos, ko, vo]
    specs = [mine] + [upper] * parts + [lower] * parts + [here, here]
    kernel = functools.partial(attn_kernel, bq=bq, tile0=half * tiles, tiles=tiles, parts=parts)
    aliases = {}
    body = kernel
    if into is not None:
        aliases = {len(args): 0}
        args.append(into)
        specs.append(pl.BlockSpec(memory_space=pl.ANY))
    return pl.pallas_call(
        body,
        grid_spec=pltpu.PrefetchScalarGridSpec(
            num_scalar_prefetch=1,
            grid=(cols // w,),
            in_specs=specs,
            out_specs=mine,
            scratch_shapes=[pltpu.VMEM((bq, WINDOW + bq), jnp.float32)] * 2,
        ),
        out_shape=jax.ShapeDtypeStruct((rows, cols), jnp.bfloat16),
        input_output_aliases=aliases,
        cost_estimate=pl.CostEstimate(
            flops=4 * pairs * HD, bytes_accessed=rows * cols * 6, transcendentals=pairs
        ),
        name="attn",
    )(*args)


def grad_kernel(h_ref, x_ref, v_ref, r_ref, w1_ref, w3_ref, w2_ref, g_ref, w13, w2, gu, hid, og, *, tm, tn):
    F = w1_ref.shape[2]
    rows = x_ref.shape[0]
    w13[:, :F] = w1_ref[0].astype(jnp.bfloat16)
    w13[:, F:] = w3_ref[0].astype(jnp.bfloat16)
    w2[...] = w2_ref[0].astype(jnp.bfloat16)
    pick = lax.broadcasted_iota(jnp.int32, r_ref.shape, 0) == h_ref[0]
    rate = jnp.sum(jnp.where(pick, r_ref[...], 0.0), axis=0, keepdims=True)
    rate = jnp.transpose(jnp.broadcast_to(rate, (8, rows)))[:, :1]
    og[...] = (-rate * v_ref[...].astype(jnp.float32)).astype(jnp.bfloat16)
    n = rows // tm

    def products(i):
        r = slice(i * tm, (i + 1) * tm)
        return mm(x_ref[r, :], w13[...]), mm(og[r, :], w2[...], NT)

    def finish(i, pre, hg):
        r = slice(i * tm, (i + 1) * tm)
        pg, pu = pre[:, :F], pre[:, F:]
        sg = jax.nn.sigmoid(pg)
        act = pg * sg
        gu[r, :F] = (hg * pu * (sg * (1.0 + pg * (1.0 - sg)))).astype(jnp.bfloat16)
        gu[r, F:] = (hg * act).astype(jnp.bfloat16)
        hid[r, :] = (act * pu).astype(jnp.bfloat16)

    cur = products(0)
    for i in range(n):
        nxt = products(i + 1) if i + 1 < n else None
        finish(i, *cur)
        cur = nxt
    x = x_ref[...]
    for j in range(2 * F // tn):
        cs = slice(j * tn, (j + 1) * tn)
        g_ref[cs, :] = mm(gu[:, cs], x, TN).astype(g_ref.dtype)
    hd = hid[...]
    for j in range(F // HD):
        cs = slice(j * HD, (j + 1) * HD)
        g_ref[2 * F + j * HD : 2 * F + (j + 1) * HD, :] = mm(og[:, cs], hd, TN).astype(g_ref.dtype)


def gradients(h, fk, fv, rates_t, w1, w3, w2):
    rows = fk.shape[0]
    F = w1.shape[1]
    tm = min(256, rows)
    tn = 256 if 2 * F % 256 == 0 else HD
    col = pl.BlockSpec((rows, F), lambda i, h: (0, h[0]))
    weight = pl.BlockSpec((1, F, F), lambda i, h: (h[0], 0, 0))
    rate = pl.BlockSpec(rates_t.shape, lambda i, h: (0, 0))
    bf = jnp.bfloat16
    return pl.pallas_call(
        functools.partial(grad_kernel, tm=tm, tn=tn),
        grid_spec=pltpu.PrefetchScalarGridSpec(
            num_scalar_prefetch=1,
            grid=(1,),
            in_specs=[col, col, rate, weight, weight, weight],
            out_specs=pl.BlockSpec((3 * F, F), lambda i, h: (0, 0)),
            scratch_shapes=[
                pltpu.VMEM((F, 2 * F), bf),
                pltpu.VMEM((F, F), bf),
                pltpu.VMEM((rows, 2 * F), bf),
                pltpu.VMEM((rows, F), bf),
                pltpu.VMEM((rows, F), bf),
            ],
        ),
        out_shape=jax.ShapeDtypeStruct((3 * F, F), bf),
        cost_estimate=pl.CostEstimate(
            flops=12 * rows * F * F, bytes_accessed=rows * F * 4 + F * F * 18, transcendentals=rows * F
        ),
        name="grads",
    )(h, fk, fv, rates_t, w1, w3, w2)


def turn_kernel(h_ref, w1, w3, w2, o_ref):
    F = w1.shape[2]
    o_ref[:F, :] = w1[0].T
    o_ref[F : 2 * F, :] = w3[0].T
    o_ref[2 * F :, :] = w2[0].T


def turned(h, w1, w3, w2):
    F = w1.shape[1]
    weight = pl.BlockSpec((1, F, F), lambda i, h: (h[0], 0, 0))
    return pl.pallas_call(
        turn_kernel,
        grid_spec=pltpu.PrefetchScalarGridSpec(
            num_scalar_prefetch=1,
            grid=(1,),
            in_specs=[weight] * 3,
            out_specs=pl.BlockSpec((3 * F, F), lambda i, h: (0, 0)),
        ),
        out_shape=jax.ShapeDtypeStruct((3 * F, F), jnp.float32),
        cost_estimate=pl.CostEstimate(flops=3 * F * F, bytes_accessed=24 * F * F, transcendentals=0),
        name="turned",
    )(h, w1, w3, w2)


def renormed(old, grad):
    new = old - grad
    old_sq = jnp.sum(old * old, axis=-1, keepdims=True)
    new_sq = jnp.sum(new * new, axis=-1, keepdims=True)
    return (new * (jnp.sqrt(old_sq) / jnp.sqrt(new_sq + EPS))).astype(jnp.bfloat16)


def fold_kernel(s_ref, *refs, counts):
    outs = refs[sum(counts) :]
    at = 0
    for count, out in zip(counts, outs):
        blocks = refs[at : at + count]
        at += count
        total = blocks[0][...].astype(jnp.float32)
        for block in blocks[1:]:
            total = total + block[...].astype(jnp.float32)
        out[...] = total.astype(out.dtype)


def renorm_kernel(s_ref, *refs, counts):
    out = refs[-1]
    at = row = 0
    for count in counts:
        blocks = refs[at : at + count]
        at += count
        grad = blocks[1][...].astype(jnp.float32)
        for block in blocks[2:]:
            grad = grad + block[...].astype(jnp.float32)
        n = grad.shape[0]
        out[row : row + n, :] = renormed(blocks[0][...], grad)
        row += n


def blockwise(kernel, where, groups, size, outs):
    F = groups[0][0][0].shape[1]
    flat = [pair for group in groups for pair in group]
    spec = lambda slot: pl.BlockSpec((size, F), lambda i, s: (s[slot], 0))
    whole = lambda shape: pl.BlockSpec(shape, lambda i, s: (0, 0))
    moved = len(flat) * size * F * 2
    return pl.pallas_call(
        functools.partial(kernel, counts=[len(group) for group in groups]),
        grid_spec=pltpu.PrefetchScalarGridSpec(
            num_scalar_prefetch=1,
            grid=(1,),
            in_specs=[spec(slot) for _, slot in flat],
            out_specs=[whole(o) for o in outs],
        ),
        out_shape=[jax.ShapeDtypeStruct(o, jnp.bfloat16) for o in outs],
        cost_estimate=pl.CostEstimate(flops=moved, bytes_accessed=moved, transcendentals=0),
    )(where, *[array for array, _ in flat])


def apply_kernel(s_ref, q_ref, a_ref, *rest, tm, pieces, unit):
    n_ref, o_ref = rest[-1], rest[-2]
    F = n_ref.shape[1]

    @pl.when(pl.program_id(0) == 0)
    def _():
        slot = 1
        for ref in rest[:pieces]:
            for r in range(ref.shape[0] // unit):
                to = pl.multiple_of(s_ref[slot] * unit, unit)
                n_ref[pl.ds(to, unit), :] = ref[r * unit : (r + 1) * unit, :]
                slot += 1

    n = q_ref.shape[0] // tm

    def first(i):
        return mm(q_ref[i * tm : (i + 1) * tm, :], n_ref[: 2 * F, :], NT)

    def second(i, h):
        g = h[:, :F]
        hid = (g * jax.nn.sigmoid(g) * h[:, F:]).astype(jnp.bfloat16)
        out = mm(hid, n_ref[2 * F :, :], NT)
        r = slice(i * tm, (i + 1) * tm)
        o_ref[r, :] = (a_ref[r, :].astype(jnp.float32) + out).astype(o_ref.dtype)

    cur = first(0)
    for i in range(n):
        nxt = first(i + 1) if i + 1 < n else None
        second(i, cur)
        cur = nxt


def apply_head(where, fq, pieces, unit, att, into=None):
    rows, cols = fq.shape
    F = pieces[0].shape[1]
    steps = 2
    col = pl.BlockSpec((rows // steps, F), lambda i, s: (i, s[0]))
    args = [where, fq, att, *pieces]
    specs = [col, col] + [pl.BlockSpec(p.shape, lambda i, s: (0, 0)) for p in pieces]
    aliases = {}
    if into is not None:
        aliases = {len(args): 0}
        args.append(into)
        specs.append(pl.BlockSpec(memory_space=pl.ANY))
    return pl.pallas_call(
        functools.partial(apply_kernel, tm=min(256, rows // steps), pieces=len(pieces), unit=unit),
        grid_spec=pltpu.PrefetchScalarGridSpec(
            num_scalar_prefetch=1,
            grid=(steps,),
            in_specs=specs,
            out_specs=col,
            scratch_shapes=[pltpu.VMEM((3 * F, F), jnp.bfloat16)],
        ),
        out_shape=jax.ShapeDtypeStruct((rows, cols), jnp.bfloat16),
        input_output_aliases=aliases,
        cost_estimate=pl.CostEstimate(
            flops=6 * rows * F * F, bytes_accessed=rows * F * 6 + F * F * 6, transcendentals=rows * F
        ),
        name="apply",
    )(*args)


def exchange(block, bit):
    size = lax.axis_size("seq")
    return lax.ppermute(block, "seq", [(i, i ^ (1 << bit)) for i in range(size)])


def shifted(block):
    size = lax.axis_size("seq")
    return lax.ppermute(block, "seq", [(i, i + 1) for i in range(size - 1)])


def synced(total, old, bits, position):
    offset = 0
    for bit in bits:
        half = total.shape[0] // 2
        mine = (position >> bit) & 1
        away = lax.dynamic_slice_in_dim(total, (1 - mine) * half, half, 0).astype(jnp.bfloat16)
        kept = lax.dynamic_slice_in_dim(total, mine * half, half, 0)
        total = kept + exchange(away, bit).astype(jnp.float32)
        offset = offset + mine * half
    part = renormed(lax.dynamic_slice_in_dim(old, offset, total.shape[0], 0), total)
    for bit in reversed(bits):
        mine = (position >> bit) & 1
        other = exchange(part, bit)
        part = jnp.concatenate(
            [jnp.where(mine == 0, part, other), jnp.where(mine == 0, other, part)], axis=0
        )
    return part


def synced_square(mine, received, old):
    position = lax.axis_index("seq")
    x, y = (position >> 1) & 1, (position >> 2) & 1
    F = mine.shape[1]
    quarter = mine.shape[0] // 4
    unit = quarter // 2
    both = lambda slot: [(mine, slot), (received, slot)]
    top, bottom = blockwise(fold_kernel, scalars(1 - x, 3 - y), [both(0), both(1)], quarter, [(quarter, F)] * 2)
    top0, bottom0 = exchange(top, 1), exchange(bottom, 2)
    where = scalars(2 * x + 1 - y, 4 + 2 * y + 1 - x, 1 - y, 1 - x)
    top, bottom = blockwise(
        fold_kernel, where, [both(0) + [(top0, 2)], both(1) + [(bottom0, 3)]], unit, [(unit, F)] * 2
    )
    top1, bottom1 = exchange(top, 2), exchange(bottom, 1)
    where = scalars(2 * x + y, 4 + 2 * y + x, y, x, 0)
    (part,) = blockwise(
        renorm_kernel,
        where,
        [
            [(old, 0)] + both(0) + [(top0, 2), (top1, 4)],
            [(old, 1)] + both(1) + [(bottom0, 3), (bottom1, 4)],
        ],
        unit,
        [(quarter, F)],
    )
    over_x, over_y = exchange(part, 1), exchange(part, 2)
    top2, bottom2 = exchange(over_y[:unit], 1), exchange(over_x[unit:], 2)
    place = lambda x, y: (2 * x + y, 4 + 2 * y + x)
    slots = (*place(x, y), *place(1 - x, y), *place(x, 1 - y), *place(1 - x, 1 - y))
    return [part, over_x, over_y, top2, bottom2], slots, unit


def shards(attn_q, attn_k, attn_v, fast_q, fast_k, fast_v, rates, fast_gate, fast_up, fast_down):
    position = lax.axis_index("seq")
    count = lax.axis_size("seq")
    heads = fast_gate.shape[0]
    rows = attn_q.shape[0]
    width = 2 if attn_q.shape[1] // HD % 2 == 0 else 1
    pack = lambda r: jnp.concatenate([attn_k[r], attn_v[r]], axis=0)
    near = shifted(pack(slice(rows // 2, rows)))
    far = shifted(pack(slice(0, rows // 2)))
    rates_t = rates.T

    def grads(h):
        return gradients(scalars(h), fast_k, fast_v, rates_t, fast_gate, fast_up, fast_down)

    if heads == 2 and count == 8:
        own = position & 1
        received = exchange(grads(1 - own), 0)
        mine = grads(own)
        old = turned(scalars(own), fast_gate, fast_up, fast_down)
        pieces, slots, unit = synced_square(mine, received, old)
        other = [exchange(p, 0) for p in pieces]
        news = [(own, pieces, slots, unit), (1 - own, other, slots, unit)]
    else:
        news = []
        bits = list(range(count.bit_length() - 1))
        for h in range(heads):
            old = turned(scalars(h), fast_gate, fast_up, fast_down)
            new = synced(grads(h).astype(jnp.float32), old, bits, position)
            news.append((h, [new], (0,), new.shape[0]))
    first = scalars(position == 0)
    bq = min(256, rows // 2)
    attended = attention(first, 1, attn_q, [near], attn_k, attn_v, bq, width)
    attended = attention(first, 0, attn_q, [far, near], attn_k, attn_v, bq, width, attended)
    mixed = None
    for h, pieces, slots, unit in news:
        mixed = apply_head(scalars(h, *slots), fast_q, pieces, unit, attended, mixed)
    return mixed


def solution(mesh):
    placed = (P("seq", "head"),) * 7 + (P("head", None, None),) * 3
    return jax.shard_map(shards, mesh=mesh, in_specs=placed, out_specs=P("seq", "head"), check_vma=False)
```

```python
import functools
import math

import jax
import jax.numpy as jnp
from jax import lax
from jax.experimental import pallas as pl
from jax.experimental.pallas import tpu as pltpu
from jax.sharding import PartitionSpec as P


HD = 128
EPS = 1e-06
NN = (((1,), (0,)), ((), ()))
NT = (((1,), (1,)), ((), ()))
TN = (((0,), (0,)), ((), ()))


def mm(a, b, dims=NN):
    return lax.dot_general(a, b, dims, preferred_element_type=jnp.float32)


def attn_kernel(position_ref, *refs, bq, jobs, sources, log_stride):
    queries = refs[: len(jobs)]
    keys = refs[len(jobs) : len(jobs) + sources]
    values = refs[len(jobs) + sources : len(jobs) + 2 * sources]
    rest = list(refs[len(jobs) + 2 * sources :])
    outs = []
    for _, sums in jobs:
        outs.append((rest.pop(0), rest.pop(0) if sums == 1 else None))
    bufs = (rest.pop(0), rest.pop(0))
    logs = [rest.pop(0) if sums else None for _, sums in jobs]
    group = pl.program_id(0)
    heads = queries[0].shape[1] // HD
    c = math.log2(math.e) / math.sqrt(HD)
    ri = lax.broadcasted_iota(jnp.int32, (bq, bq), 0)
    ci = lax.broadcasted_iota(jnp.int32, (bq, bq), 1)
    absent = position_ref[0] == 0
    units = [(h, j, t) for h in range(heads) for j in range(len(jobs)) for t in range(len(jobs[j][0]))]

    def scores(i):
        h, j, t = units[i]
        hs = slice(h * HD, (h + 1) * HD)
        buf = bufs[i % 2]
        q = queries[j][t * bq : (t + 1) * bq, hs]
        tops = []
        at = 0
        for source, lo, hi, edge in jobs[j][0][t]:
            s = mm(q, keys[source][lo:hi, hs], NT)
            n = hi - lo
            if edge == 1:
                kept = jnp.where(ci >= ri, s[:, :bq], -jnp.inf)
                s = jnp.concatenate([kept, s[:, bq:]], axis=1) if n > bq else kept
            elif edge == -1:
                kept = jnp.where(ci <= ri, s[:, n - bq :], -jnp.inf)
                s = jnp.concatenate([s[:, : n - bq], kept], axis=1) if n > bq else kept
            buf[:, at : at + n] = s
            tops.append(jnp.max(s, axis=1, keepdims=True))
            at += n
        if len(tops) == 1:
            return [tops[0] * c]
        m = jnp.maximum(tops[1], jnp.where(absent, -jnp.inf, tops[0])) * c
        return [jnp.where(absent, 1e30, m), m]

    def finish(i, ms):
        h, j, t = units[i]
        plan, sums = jobs[j]
        hs = slice(h * HD, (h + 1) * HD)
        buf = bufs[i % 2]
        out = total = None
        at = 0
        for (source, lo, hi, _), m in zip(plan[t], ms):
            p = jnp.exp2(buf[:, at : at + hi - lo] * c - m)
            part = jnp.sum(p, axis=1, keepdims=True)
            o = mm(p.astype(jnp.bfloat16), values[source][lo:hi, hs])
            total = part if total is None else total + part
            out = o if out is None else out + o
            at += hi - lo
        rows = slice(t * bq, (t + 1) * bq)
        out = (out / total).astype(jnp.bfloat16)
        head = group * heads + h
        if sums == 2:
            outs[j][0][rows, pl.ds(pl.multiple_of(head * HD, HD), HD)] = out
        else:
            outs[j][0][rows, hs] = out
        if sums:
            lane = lax.broadcasted_iota(jnp.int32, (bq, HD), 1)
            log = ms[-1] + jnp.log(total) * math.log2(math.e)
            logs[j][rows, :] = jnp.where(lane == head, log, logs[j][rows, :])

    if any(sums for _, sums in jobs):

        @pl.when(group == 0)
        def _():
            for log in logs:
                if log is not None:
                    log[...] = jnp.zeros(log.shape, log.dtype)

    ms = scores(0)
    for i in range(len(units)):
        nxt = scores(i + 1) if i + 1 < len(units) else None
        finish(i, ms)
        ms = nxt
    if any(sums for _, sums in jobs):

        @pl.when(group == pl.num_programs(0) - 1)
        def _():
            for (_, sums), (out, log_out), log in zip(jobs, outs, logs):
                if sums == 1:
                    log_out[...] = log[...]
                if sums == 2:
                    x = log[...]
                    a = x.astype(jnp.bfloat16).astype(jnp.float32)
                    b = (x - a).astype(jnp.bfloat16).astype(jnp.float32)
                    x = a + pltpu.roll(b, log_stride, 1) + pltpu.roll(x - a - b, 2 * log_stride, 1)
                    out[:, out.shape[1] - HD :] = x.astype(jnp.bfloat16)


def log_stride_of(cols):
    return 16 * pl.cdiv(cols // HD, 16)


def attention(position, jobs, sources, bq, width):
    cols = jobs[0][0].shape[1]
    w = width * HD
    ranges = [r for _, _, plan, _ in jobs for tile in plan for r in tile]
    span = max(sum(hi - lo for _, lo, hi, _ in tile) for _, _, plan, _ in jobs for tile in plan)
    pairs = bq * sum(hi - lo for _, lo, hi, _ in ranges) * cols // HD
    block = lambda n, at: pl.BlockSpec((n, w), lambda g, f: (at, g))
    whole = lambda *shape: pl.BlockSpec(shape, lambda g, f: (0, 0))
    outs, out_specs, logs = [], [], []
    for _, _, plan, sums in jobs:
        rows = len(plan) * bq
        if sums == 2:
            outs.append(jax.ShapeDtypeStruct((rows, cols + HD), jnp.bfloat16))
            out_specs.append(whole(rows, cols + HD))
        else:
            outs.append(jax.ShapeDtypeStruct((rows, cols), jnp.bfloat16))
            out_specs.append(block(rows, 0))
        if sums == 1:
            outs.append(jax.ShapeDtypeStruct((rows, HD), jnp.float32))
            out_specs.append(whole(rows, HD))
        if sums:
            logs.append(pltpu.VMEM((rows, HD), jnp.float32))
    specs = [block(len(plan) * bq, at) for _, at, plan, _ in jobs]
    specs += [block(n, at) for _, at, _, _, n in sources] + [block(n, at) for _, _, _, at, n in sources]
    kernel = functools.partial(
        attn_kernel,
        bq=bq,
        jobs=[(plan, sums) for _, _, plan, sums in jobs],
        sources=len(sources),
        log_stride=log_stride_of(cols),
    )
    return pl.pallas_call(
        kernel,
        grid_spec=pltpu.PrefetchScalarGridSpec(
            num_scalar_prefetch=1,
            grid=(cols // w,),
            in_specs=specs,
            out_specs=out_specs,
            scratch_shapes=[pltpu.VMEM((bq, span), jnp.float32)] * 2 + logs,
        ),
        out_shape=outs,
        cost_estimate=pl.CostEstimate(
            flops=4 * pairs * HD, bytes_accessed=8 * bq * cols * len(ranges), transcendentals=pairs
        ),
    )(position, *[job[0] for job in jobs], *[x[0] for x in sources], *[x[2] for x in sources])


def grad_kernel(s_ref, x_ref, v_ref, r_ref, w1_ref, w3_ref, w2_ref, *refs, head, tm, tn, split):
    w13, w2, gu, hid, og = refs[-5:]
    F = w1_ref.shape[2]
    rows = x_ref.shape[0]
    w13[:, :F] = w1_ref[0].astype(jnp.bfloat16)
    w13[:, F:] = w3_ref[0].astype(jnp.bfloat16)
    w2[...] = w2_ref[0].astype(jnp.bfloat16)
    pick = lax.broadcasted_iota(jnp.int32, r_ref.shape, 0) == head(s_ref)
    rate = jnp.sum(jnp.where(pick, r_ref[...], 0.0), axis=0, keepdims=True)
    rate = jnp.transpose(jnp.broadcast_to(rate, (8, rows)))[:, :1]
    og[...] = (-rate * v_ref[...].astype(jnp.float32)).astype(jnp.bfloat16)
    n = rows // tm

    def products(i):
        r = slice(i * tm, (i + 1) * tm)
        return mm(x_ref[r, :], w13[...]), mm(og[r, :], w2[...], NT)

    def finish(i, pre, hg):
        r = slice(i * tm, (i + 1) * tm)
        pg, pu = pre[:, :F], pre[:, F:]
        sg = jax.nn.sigmoid(pg)
        act = pg * sg
        gu[r, :F] = (hg * pu * (sg * (1.0 + pg * (1.0 - sg)))).astype(jnp.bfloat16)
        gu[r, F:] = (hg * act).astype(jnp.bfloat16)
        hid[r, :] = (act * pu).astype(jnp.bfloat16)

    cur = products(0)
    for i in range(n):
        nxt = products(i + 1) if i + 1 < n else None
        finish(i, *cur)
        cur = nxt
    x = x_ref[...]
    hd = hid[...]
    quarter = 3 * F // 4
    x1, y1 = (s_ref[0] >> 1) & 1, (s_ref[0] >> 2) & 1

    def put(lo, grad):
        if not split:
            refs[0][lo : lo + grad.shape[0], :] = grad.astype(refs[0].dtype)
            return
        grad = grad + refs[0][lo : lo + grad.shape[0], :].astype(jnp.float32)
        at = 0
        while at < grad.shape[0]:
            block, row = divmod(lo + at, quarter)
            n = min(grad.shape[0] - at, quarter - row)
            coordinate = x1 if block < 2 else y1
            slot = jnp.where(coordinate == block % 2, 0, 1)
            refs[1 + block // 2][slot, row : row + n, :] = grad[at : at + n].astype(jnp.bfloat16)
            at += n

    for j in range(2 * F // tn):
        put(j * tn, mm(gu[:, j * tn : (j + 1) * tn], x, TN))
    for j in range(F // HD):
        put(2 * F + j * HD, mm(og[:, j * HD : (j + 1) * HD], hd, TN))
    if split:
        for o in range(2):
            refs[3 + 2 * o][...] = refs[1 + o][0]
            refs[4 + 2 * o][...] = refs[1 + o][1]


def gradients(position, head, fk, fv, rates_t, w1, w3, w2, received=None):
    rows = fk.shape[0]
    F = w1.shape[1]
    tm = min(256, rows)
    tn = 256 if 2 * F % 256 == 0 else HD
    col = pl.BlockSpec((rows, F), lambda i, s: (0, head(s)))
    weight = pl.BlockSpec((1, F, F), lambda i, s: (head(s), 0, 0))
    whole = lambda *shape: pl.BlockSpec(shape, lambda i, s: (0,) * len(shape))
    bf = jnp.bfloat16
    args = [position, fk, fv, rates_t, w1, w3, w2]
    specs = [col, col, whole(*rates_t.shape), weight, weight, weight]
    scratch = [
        pltpu.VMEM((F, 2 * F), bf),
        pltpu.VMEM((F, F), bf),
        pltpu.VMEM((rows, 2 * F), bf),
        pltpu.VMEM((rows, F), bf),
        pltpu.VMEM((rows, F), bf),
    ]
    if received is None:
        shapes = [(3 * F, F)]
    else:
        shapes = [(3 * F // 4, F)] * 4
        args.append(received)
        specs.append(whole(3 * F, F))
        scratch = [pltpu.VMEM((2, 3 * F // 4, F), bf)] * 2 + scratch
    kernel = functools.partial(grad_kernel, head=head, tm=tm, tn=tn, split=received is not None)

    def body(*refs):
        if received is None:
            return kernel(*refs)
        ins, outs, halves, rest = refs[:8], refs[8:12], refs[12:14], refs[14:]
        return kernel(*ins, *halves, *outs, *rest)

    return pl.pallas_call(
        body,
        grid_spec=pltpu.PrefetchScalarGridSpec(
            num_scalar_prefetch=1,
            grid=(1,),
            in_specs=specs,
            out_specs=[whole(*shape) for shape in shapes],
            scratch_shapes=scratch,
        ),
        out_shape=[jax.ShapeDtypeStruct(shape, bf) for shape in shapes],
        cost_estimate=pl.CostEstimate(
            flops=12 * rows * F * F, bytes_accessed=rows * F * 4 + F * F * 18, transcendentals=rows * F
        ),
        name="grads",
    )(*args)


def turn_kernel(s_ref, w1, w3, w2, o_ref, *scratch, units):
    F = w1.shape[2]
    all_ref = scratch[0] if scratch else o_ref
    all_ref[:F, :] = w1[0].T
    all_ref[F : 2 * F, :] = w3[0].T
    all_ref[2 * F :, :] = w2[0].T
    if scratch:
        n = o_ref.shape[0] // len(units)
        for i, unit in enumerate(units):
            start = pl.multiple_of(unit(s_ref) * n, 8)
            o_ref[i * n : (i + 1) * n, :] = all_ref[pl.ds(start, n), :]


def turned(position, head, w1, w3, w2, size=None, units=()):
    F = w1.shape[1]
    weight = pl.BlockSpec((1, F, F), lambda i, s: (head(s), 0, 0))
    shape = (size * len(units), F) if units else (3 * F, F)
    return pl.pallas_call(
        functools.partial(turn_kernel, units=units),
        grid_spec=pltpu.PrefetchScalarGridSpec(
            num_scalar_prefetch=1,
            grid=(1,),
            in_specs=[weight] * 3,
            out_specs=pl.BlockSpec(shape, lambda i, s: (0, 0)),
            scratch_shapes=[pltpu.VMEM((3 * F, F), jnp.float32)] if units else [],
        ),
        out_shape=jax.ShapeDtypeStruct(shape, jnp.float32),
        cost_estimate=pl.CostEstimate(flops=3 * F * F, bytes_accessed=24 * F * F, transcendentals=0),
        name="turned",
    )(position, w1, w3, w2)


def renormed(old, grad):
    new = old - grad
    old_sq = jnp.sum(old * old, axis=-1, keepdims=True)
    new_sq = jnp.sum(new * new, axis=-1, keepdims=True)
    return (new * (jnp.sqrt(old_sq) / jnp.sqrt(new_sq + EPS))).astype(jnp.bfloat16)


def renorm_kernel(s_ref, old_ref, *refs):
    out = refs[-1]
    n = out.shape[0] // 2
    for i in range(2):
        a, b, c = (ref[...].astype(jnp.float32) for ref in refs[3 * i : 3 * i + 3])
        out[i * n : (i + 1) * n, :] = renormed(old_ref[i * n : (i + 1) * n, :], a + b + c)


def renorm_units(position, old, upper, lower):
    unit, F = upper[2][0].shape
    flat = upper + lower
    spec = lambda at: pl.BlockSpec((unit, F), lambda i, s: (at(s), 0))
    whole = pl.BlockSpec((2 * unit, F), lambda i, s: (0, 0))
    return pl.pallas_call(
        renorm_kernel,
        grid_spec=pltpu.PrefetchScalarGridSpec(
            num_scalar_prefetch=1,
            grid=(1,),
            in_specs=[whole] + [spec(at) for _, at in flat],
            out_specs=whole,
        ),
        out_shape=jax.ShapeDtypeStruct((2 * unit, F), jnp.bfloat16),
        cost_estimate=pl.CostEstimate(flops=20 * unit * F, bytes_accessed=24 * unit * F, transcendentals=0),
        name="renorm",
    )(position, old, *[array for array, _ in flat])


def apply_kernel(s_ref, q_ref, high_ref, own_ref, far_ref, own_log, far_log, *rest, head, tm, places, unit, pieces, stride):
    n_ref, a_ref, o_ref = rest[-2], rest[-1], rest[-3]
    F = n_ref.shape[1]
    step = pl.program_id(0)

    @pl.when(step == 0)
    def _():
        slot = 0
        for ref in rest[:pieces]:
            for r in range(ref.shape[0] // unit):
                to = pl.multiple_of(places[slot](s_ref) * unit, min(unit, 16))
                n_ref[pl.ds(to, unit), :] = ref[r * unit : (r + 1) * unit, :]
                slot += 1
        lane = lax.broadcasted_iota(jnp.int32, own_log.shape, 1)
        for j in range(F // HD):
            cs = slice(j * HD, (j + 1) * HD)
            at = head(s_ref) * (F // HD) + j
            pick = lambda ref, of: jnp.sum(
                jnp.where(of, ref[...].astype(jnp.float32), 0.0), axis=1, keepdims=True
            )
            own = pick(own_log, lane == at)
            far = pick(far_log, (lane == at) | (lane == at + stride) | (lane == at + 2 * stride))
            far = jnp.where(s_ref[0] == 0, -jnp.inf, far)
            top = jnp.maximum(own, far)
            own, far = jnp.exp2(own - top), jnp.exp2(far - top)
            share = own / (own + far)
            a, b = own_ref[:, cs].astype(jnp.float32), far_ref[:, cs].astype(jnp.float32)
            a_ref[:, cs] = a * share + b * (1.0 - share)

    @pl.when(step == 1)
    def _():
        a_ref[...] = high_ref[...].astype(jnp.float32)

    n = q_ref.shape[0] // tm

    def first(i):
        return mm(q_ref[i * tm : (i + 1) * tm, :], n_ref[: 2 * F, :], NT)

    def second(i, h):
        g = h[:, :F]
        hid = (g * jax.nn.sigmoid(g) * h[:, F:]).astype(jnp.bfloat16)
        r = slice(i * tm, (i + 1) * tm)
        o_ref[r, :] = (a_ref[r, :] + mm(hid, n_ref[2 * F :, :], NT)).astype(o_ref.dtype)

    cur = first(0)
    for i in range(n):
        nxt = first(i + 1) if i + 1 < n else None
        second(i, cur)
        cur = nxt


def apply_head(position, head, fq, pieces, places, unit, attended, into=None):
    rows, cols = fq.shape
    F = pieces[0].shape[1]
    half = rows // 2
    col = pl.BlockSpec((half, F), lambda i, s: (i, head(s)))
    part = pl.BlockSpec((half, F), lambda i, s: (0, head(s)))
    whole = lambda a: pl.BlockSpec(a.shape, lambda i, s: (0, 0))
    high, own, far, own_log = attended
    far_log = pl.BlockSpec((half, HD), lambda i, s: (0, cols // HD))
    args = [position, fq, high, own, far, own_log, far, *pieces]
    specs = [col, part, part, part, whole(own_log), far_log] + [whole(p) for p in pieces]
    aliases = {}
    if into is not None:
        aliases = {len(args): 0}
        args.append(into)
        specs.append(pl.BlockSpec(memory_space=pl.ANY))
    kernel = functools.partial(
        apply_kernel, head=head, tm=min(256, half), places=places, unit=unit, pieces=len(pieces), stride=log_stride_of(cols)
    )
    return pl.pallas_call(
        kernel,
        grid_spec=pltpu.PrefetchScalarGridSpec(
            num_scalar_prefetch=1,
            grid=(2,),
            in_specs=specs,
            out_specs=col,
            scratch_shapes=[pltpu.VMEM((3 * F, F), jnp.bfloat16), pltpu.VMEM((half, F), jnp.float32)],
        ),
        out_shape=jax.ShapeDtypeStruct((rows, cols), jnp.bfloat16),
        input_output_aliases=aliases,
        cost_estimate=pl.CostEstimate(
            flops=6 * rows * F * F, bytes_accessed=rows * F * 6 + F * F * 6, transcendentals=rows * F
        ),
        name="apply",
    )(*args)


def exchange(block, bit):
    size = lax.axis_size("seq")
    return lax.ppermute(block, "seq", [(i, i ^ (1 << bit)) for i in range(size)])


def shifted(block, by):
    size = lax.axis_size("seq")
    return lax.ppermute(block, "seq", [(i, i + by) for i in range(size) if 0 <= i + by < size])


def synced(total, old, bits, position):
    offset = 0
    for bit in bits:
        half = total.shape[0] // 2
        mine = (position >> bit) & 1
        away = lax.dynamic_slice_in_dim(total, (1 - mine) * half, half, 0).astype(jnp.bfloat16)
        kept = lax.dynamic_slice_in_dim(total, mine * half, half, 0)
        total = kept + exchange(away, bit).astype(jnp.float32)
        offset = offset + mine * half
    part = renormed(lax.dynamic_slice_in_dim(old, offset, total.shape[0], 0), total)
    for bit in reversed(bits):
        mine = (position >> bit) & 1
        other = exchange(part, bit)
        part = jnp.concatenate(
            [jnp.where(mine == 0, part, other), jnp.where(mine == 0, other, part)], axis=0
        )
    return part


def synced_square(position, quarters, old):
    x, y = (position[0] >> 1) & 1, (position[0] >> 2) & 1
    keep_x, send_x, keep_y, send_y = quarters
    unit = keep_x.shape[0] // 2
    top0, bottom0 = exchange(send_x, 1), exchange(send_y, 2)

    def fold(a, b, at):
        a, b = (lax.dynamic_slice_in_dim(v, at * unit, unit, 0).astype(jnp.float32) for v in (a, b))
        return (a + b).astype(jnp.bfloat16)

    top1 = exchange(fold(keep_x, top0, 1 - y), 2)
    bottom1 = exchange(fold(keep_y, bottom0, 1 - x), 1)
    zero = lambda s: 0
    part = renorm_units(
        position,
        old,
        [(keep_x, at_y), (top0, at_y), (top1, zero)],
        [(keep_y, at_x), (bottom0, at_x), (bottom1, zero)],
    )
    over_x, over_y = exchange(part, 1), exchange(part, 2)
    top2, bottom2 = exchange(over_y[:unit], 1), exchange(over_x[unit:], 2)
    return [part, over_x, over_y, top2, bottom2], unit


def at_x(s):
    return (s[0] >> 1) & 1


def at_y(s):
    return (s[0] >> 2) & 1


def place(flip_x, flip_y):
    x = lambda s: at_x(s) ^ flip_x
    y = lambda s: at_y(s) ^ flip_y
    return [lambda s: 2 * x(s) + y(s), lambda s: 4 + 2 * y(s) + x(s)]


def shards(attn_q, attn_k, attn_v, fast_q, fast_k, fast_v, rates, fast_gate, fast_up, fast_down):
    position = lax.axis_index("seq").astype(jnp.int32).reshape(1)
    count = lax.axis_size("seq")
    heads = fast_gate.shape[0]
    rows = attn_q.shape[0]
    half = rows // 2
    width = 2 if attn_q.shape[1] // HD % 2 == 0 else 1
    prev = shifted(jnp.concatenate([attn_k[half:], attn_v[half:]], axis=0), 1)
    guests = shifted(attn_q[:half], -1)
    rates_t = rates.T
    weights = (fast_gate, fast_up, fast_down)

    def grads(head, received=None):
        return gradients(position, head, fast_k, fast_v, rates_t, *weights, received)

    if heads == 2 and count == 8:
        near, far = (lambda s: s[0] & 1), (lambda s: 1 - (s[0] & 1))
        received = exchange(grads(far)[0], 0)
        old = turned(position, near, *weights, size=3 * fast_gate.shape[1] // 8, units=tuple(place(0, 0)))
        quarters = grads(near, received)
        pieces, unit = synced_square(position, quarters, old)
        other = [exchange(p, 0) for p in pieces]
        places = place(0, 0) + place(1, 0) + place(0, 1)
        places += [place(1, 1)[0], place(1, 1)[1]]
        news = [(near, pieces, places, unit), (far, other, places, unit)]
    else:
        news = []
        bits = list(range(count.bit_length() - 1))
        for h in range(heads):
            head = lambda s, h=h: h
            old = turned(position, head, *weights)
            new = synced(grads(head)[0].astype(jnp.float32), old, bits, position[0])
            news.append((head, [new], [lambda s: 0], new.shape[0]))
    bq = min(256, half)
    tiles = half // bq
    late = [
        [(0, t * bq, half, 1), (1, 0, half + (t + 1) * bq, -1)] for t in range(tiles)
    ]
    early = [[(0, 0, (t + 1) * bq, -1)] for t in range(tiles)]
    guest = [[(0, t * bq, rows, 1)] for t in range(tiles)]
    here = (attn_k, 0, attn_v, 0, rows)
    returned, own_out, own_log = attention(position, [(guests, 0, guest, 2), (attn_q, 0, early, 1)], [here], bq, width)
    far_out = shifted(returned, 1)
    (high,) = attention(position, [(attn_q, 1, late, 0)], [(prev, 0, prev, 1, half), here], bq, width)
    attended = (high, own_out, far_out, own_log)
    mixed = None
    for head, pieces, places, unit in news:
        mixed = apply_head(position, head, fast_q, pieces, places, unit, attended, mixed)
    return mixed


def solution(mesh):
    placed = (P("seq", "head"),) * 7 + (P("head", None, None),) * 3
    return jax.shard_map(shards, mesh=mesh, in_specs=placed, out_specs=P("seq", "head"), check_vma=False)
```

```python
import functools
import math

import jax
import jax.numpy as jnp
from jax import lax
from jax.experimental import pallas as pl
from jax.experimental.pallas import tpu as pltpu
from jax.sharding import PartitionSpec as P


HD = 128
EPS = 1e-06
NN = (((1,), (0,)), ((), ()))
NT = (((1,), (1,)), ((), ()))
TN = (((0,), (0,)), ((), ()))


def mm(a, b, dims=NN):
    return lax.dot_general(a, b, dims, preferred_element_type=jnp.float32)


def attn_kernel(position_ref, *refs, bq, jobs, sources, log_stride):
    queries = refs[: len(jobs)]
    keys = refs[len(jobs) : len(jobs) + sources]
    values = refs[len(jobs) + sources : len(jobs) + 2 * sources]
    rest = list(refs[len(jobs) + 2 * sources :])
    outs = []
    for _, sums in jobs:
        outs.append((rest.pop(0), rest.pop(0) if sums == 1 else None))
    bufs = (rest.pop(0), rest.pop(0))
    logs = [rest.pop(0) if sums else None for _, sums in jobs]
    group = pl.program_id(0)
    heads = queries[0].shape[1] // HD
    c = math.log2(math.e) / math.sqrt(HD)
    ri = lax.broadcasted_iota(jnp.int32, (bq, bq), 0)
    ci = lax.broadcasted_iota(jnp.int32, (bq, bq), 1)
    absent = position_ref[0] == 0
    units = [(h, j, t) for h in range(heads) for j in range(len(jobs)) for t in range(len(jobs[j][0]))]

    def scores(i):
        h, j, t = units[i]
        hs = slice(h * HD, (h + 1) * HD)
        buf = bufs[i % 2]
        q = queries[j][t * bq : (t + 1) * bq, hs]
        tops = []
        at = 0
        for source, lo, hi, edge in jobs[j][0][t]:
            s = mm(q, keys[source][lo:hi, hs], NT)
            n = hi - lo
            if edge == 1:
                kept = jnp.where(ci >= ri, s[:, :bq], -jnp.inf)
                s = jnp.concatenate([kept, s[:, bq:]], axis=1) if n > bq else kept
            elif edge == -1:
                kept = jnp.where(ci <= ri, s[:, n - bq :], -jnp.inf)
                s = jnp.concatenate([s[:, : n - bq], kept], axis=1) if n > bq else kept
            buf[:, at : at + n] = s
            tops.append(jnp.max(s, axis=1, keepdims=True))
            at += n
        if len(tops) == 1:
            return [tops[0] * c]
        m = jnp.maximum(tops[1], jnp.where(absent, -jnp.inf, tops[0])) * c
        return [jnp.where(absent, 1e30, m), m]

    def finish(i, ms):
        h, j, t = units[i]
        plan, sums = jobs[j]
        hs = slice(h * HD, (h + 1) * HD)
        buf = bufs[i % 2]
        out = total = None
        at = 0
        for (source, lo, hi, _), m in zip(plan[t], ms):
            p = jnp.exp2(buf[:, at : at + hi - lo] * c - m)
            part = jnp.sum(p, axis=1, keepdims=True)
            o = mm(p.astype(jnp.bfloat16), values[source][lo:hi, hs])
            total = part if total is None else total + part
            out = o if out is None else out + o
            at += hi - lo
        rows = slice(t * bq, (t + 1) * bq)
        out = (out / total).astype(jnp.bfloat16)
        head = group * heads + h
        if sums == 2:
            outs[j][0][rows, pl.ds(pl.multiple_of(head * HD, HD), HD)] = out
        else:
            outs[j][0][rows, hs] = out
        if sums:
            lane = lax.broadcasted_iota(jnp.int32, (bq, HD), 1)
            log = ms[-1] + jnp.log(total) * math.log2(math.e)
            logs[j][rows, :] = jnp.where(lane == head, log, logs[j][rows, :])

    if any(sums for _, sums in jobs):

        @pl.when(group == 0)
        def _():
            for log in logs:
                if log is not None:
                    log[...] = jnp.zeros(log.shape, log.dtype)

    ms = scores(0)
    for i in range(len(units)):
        nxt = scores(i + 1) if i + 1 < len(units) else None
        finish(i, ms)
        ms = nxt
    if any(sums for _, sums in jobs):

        @pl.when(group == pl.num_programs(0) - 1)
        def _():
            for (_, sums), (out, log_out), log in zip(jobs, outs, logs):
                if sums == 1:
                    log_out[...] = log[...]
                if sums == 2:
                    x = log[...]
                    a = x.astype(jnp.bfloat16).astype(jnp.float32)
                    b = (x - a).astype(jnp.bfloat16).astype(jnp.float32)
                    x = a + pltpu.roll(b, log_stride, 1) + pltpu.roll(x - a - b, 2 * log_stride, 1)
                    out[:, out.shape[1] - HD :] = x.astype(jnp.bfloat16)


def log_stride_of(cols):
    return 16 * pl.cdiv(cols // HD, 16)


def attention(position, jobs, sources, bq, width):
    cols = jobs[0][0].shape[1]
    w = width * HD
    ranges = [r for _, _, plan, _ in jobs for tile in plan for r in tile]
    span = max(sum(hi - lo for _, lo, hi, _ in tile) for _, _, plan, _ in jobs for tile in plan)
    pairs = bq * sum(hi - lo for _, lo, hi, _ in ranges) * cols // HD
    block = lambda n, at: pl.BlockSpec((n, w), lambda g, f: (at, g))
    whole = lambda *shape: pl.BlockSpec(shape, lambda g, f: (0, 0))
    outs, out_specs, logs = [], [], []
    for _, _, plan, sums in jobs:
        rows = len(plan) * bq
        if sums == 2:
            outs.append(jax.ShapeDtypeStruct((rows, cols + HD), jnp.bfloat16))
            out_specs.append(whole(rows, cols + HD))
        else:
            outs.append(jax.ShapeDtypeStruct((rows, cols), jnp.bfloat16))
            out_specs.append(block(rows, 0))
        if sums == 1:
            outs.append(jax.ShapeDtypeStruct((rows, HD), jnp.float32))
            out_specs.append(whole(rows, HD))
        if sums:
            logs.append(pltpu.VMEM((rows, HD), jnp.float32))
    specs = [block(len(plan) * bq, at) for _, at, plan, _ in jobs]
    specs += [block(n, at) for _, at, _, _, n in sources] + [block(n, at) for _, _, _, at, n in sources]
    kernel = functools.partial(
        attn_kernel,
        bq=bq,
        jobs=[(plan, sums) for _, _, plan, sums in jobs],
        sources=len(sources),
        log_stride=log_stride_of(cols),
    )
    return pl.pallas_call(
        kernel,
        grid_spec=pltpu.PrefetchScalarGridSpec(
            num_scalar_prefetch=1,
            grid=(cols // w,),
            in_specs=specs,
            out_specs=out_specs,
            scratch_shapes=[pltpu.VMEM((bq, span), jnp.float32)] * 2 + logs,
        ),
        out_shape=outs,
        cost_estimate=pl.CostEstimate(
            flops=4 * pairs * HD, bytes_accessed=8 * bq * cols * len(ranges), transcendentals=pairs
        ),
    )(position, *[job[0] for job in jobs], *[x[0] for x in sources], *[x[2] for x in sources])


def grad_kernel(s_ref, x_ref, v_ref, r_ref, w1_ref, w3_ref, w2_ref, *refs, head, tm, tn, split):
    w13, w2, gu, hid, og = refs[-5:]
    F = w1_ref.shape[2]
    rows = x_ref.shape[0]
    w13[:, :F] = w1_ref[0].astype(jnp.bfloat16)
    w13[:, F:] = w3_ref[0].astype(jnp.bfloat16)
    w2[...] = w2_ref[0].astype(jnp.bfloat16)
    pick = lax.broadcasted_iota(jnp.int32, r_ref.shape, 0) == head(s_ref)
    rate = jnp.sum(jnp.where(pick, r_ref[...], 0.0), axis=0, keepdims=True)
    rate = jnp.transpose(jnp.broadcast_to(rate, (8, rows)))[:, :1]
    og[...] = (-rate * v_ref[...].astype(jnp.float32)).astype(jnp.bfloat16)
    n = rows // tm

    def products(i):
        r = slice(i * tm, (i + 1) * tm)
        return mm(x_ref[r, :], w13[...]), mm(og[r, :], w2[...], NT)

    def finish(i, pre, hg):
        r = slice(i * tm, (i + 1) * tm)
        pg, pu = pre[:, :F], pre[:, F:]
        sg = jax.nn.sigmoid(pg)
        act = pg * sg
        gu[r, :F] = (hg * pu * (sg * (1.0 + pg * (1.0 - sg)))).astype(jnp.bfloat16)
        gu[r, F:] = (hg * act).astype(jnp.bfloat16)
        hid[r, :] = (act * pu).astype(jnp.bfloat16)

    cur = products(0)
    for i in range(n):
        nxt = products(i + 1) if i + 1 < n else None
        finish(i, *cur)
        cur = nxt
    x = x_ref[...]
    hd = hid[...]
    x1, y1 = (s_ref[0] >> 1) & 1, (s_ref[0] >> 2) & 1

    def put(lo, grad):
        if not split:
            refs[0][lo : lo + grad.shape[0], :] = grad.astype(refs[0].dtype)
            return
        grad = grad + refs[0][lo : lo + grad.shape[0], :].astype(jnp.float32)
        edges = [0, F // 2, F, 2 * F, 3 * F]
        for block in range(4):
            a, b = max(lo, edges[block]), min(lo + grad.shape[0], edges[block + 1])
            if a < b:
                slot = jnp.where((x1 if block < 2 else y1) == block % 2, 0, 1)
                rows_at = slice(a - edges[block], b - edges[block])
                refs[1 + block // 2][slot, rows_at, :] = grad[a - lo : b - lo].astype(jnp.bfloat16)

    for j in range(2 * F // tn):
        put(j * tn, mm(gu[:, j * tn : (j + 1) * tn], x, TN))
    for j in range(F // HD):
        put(2 * F + j * HD, mm(og[:, j * HD : (j + 1) * HD], hd, TN))
    if split:
        for o in range(2):
            refs[3 + 2 * o][...] = refs[1 + o][0]
            refs[4 + 2 * o][...] = refs[1 + o][1]


def gradients(position, head, fk, fv, rates_t, w1, w3, w2, received=None):
    rows = fk.shape[0]
    F = w1.shape[1]
    tm = min(256, rows)
    tn = 256 if 2 * F % 256 == 0 else HD
    col = pl.BlockSpec((rows, F), lambda i, s: (0, head(s)))
    weight = pl.BlockSpec((1, F, F), lambda i, s: (head(s), 0, 0))
    whole = lambda *shape: pl.BlockSpec(shape, lambda i, s: (0,) * len(shape))
    bf = jnp.bfloat16
    args = [position, fk, fv, rates_t, w1, w3, w2]
    specs = [col, col, whole(*rates_t.shape), weight, weight, weight]
    scratch = [
        pltpu.VMEM((F, 2 * F), bf),
        pltpu.VMEM((F, F), bf),
        pltpu.VMEM((rows, 2 * F), bf),
        pltpu.VMEM((rows, F), bf),
        pltpu.VMEM((rows, F), bf),
    ]
    if received is None:
        shapes = [(3 * F, F)]
    else:
        shapes = [(F // 2, F)] * 2 + [(F, F)] * 2
        args.append(received)
        specs.append(whole(3 * F, F))
        scratch = [pltpu.VMEM((2, F // 2, F), bf), pltpu.VMEM((2, F, F), bf)] + scratch
    kernel = functools.partial(grad_kernel, head=head, tm=tm, tn=tn, split=received is not None)

    def body(*refs):
        if received is None:
            return kernel(*refs)
        ins, outs, halves, rest = refs[:8], refs[8:12], refs[12:14], refs[14:]
        return kernel(*ins, *halves, *outs, *rest)

    return pl.pallas_call(
        body,
        grid_spec=pltpu.PrefetchScalarGridSpec(
            num_scalar_prefetch=1,
            grid=(1,),
            in_specs=specs,
            out_specs=[whole(*shape) for shape in shapes],
            scratch_shapes=scratch,
        ),
        out_shape=[jax.ShapeDtypeStruct(shape, bf) for shape in shapes],
        cost_estimate=pl.CostEstimate(
            flops=12 * rows * F * F, bytes_accessed=rows * F * 4 + F * F * 18, transcendentals=rows * F
        ),
        name="grads",
    )(*args)


def turn_kernel(s_ref, w1, w3, w2, o_ref, *scratch, parts):
    F = w1.shape[2]
    all_ref = scratch[0] if scratch else o_ref
    all_ref[:F, :] = w1[0].T
    all_ref[F : 2 * F, :] = w3[0].T
    all_ref[2 * F :, :] = w2[0].T
    at = 0
    for n, start in parts:
        o_ref[at : at + n, :] = all_ref[pl.ds(pl.multiple_of(start(s_ref), 8), n), :]
        at += n


def turned(position, head, w1, w3, w2, parts=()):
    F = w1.shape[1]
    weight = pl.BlockSpec((1, F, F), lambda i, s: (head(s), 0, 0))
    shape = (sum(n for n, _ in parts), F) if parts else (3 * F, F)
    return pl.pallas_call(
        functools.partial(turn_kernel, parts=parts),
        grid_spec=pltpu.PrefetchScalarGridSpec(
            num_scalar_prefetch=1,
            grid=(1,),
            in_specs=[weight] * 3,
            out_specs=pl.BlockSpec(shape, lambda i, s: (0, 0)),
            scratch_shapes=[pltpu.VMEM((3 * F, F), jnp.float32)] if parts else [],
        ),
        out_shape=jax.ShapeDtypeStruct(shape, jnp.float32),
        cost_estimate=pl.CostEstimate(flops=3 * F * F, bytes_accessed=24 * F * F, transcendentals=0),
        name="turned",
    )(position, w1, w3, w2)


def renormed(old, grad):
    new = old - grad
    old_sq = jnp.sum(old * old, axis=-1, keepdims=True)
    new_sq = jnp.sum(new * new, axis=-1, keepdims=True)
    return (new * (jnp.sqrt(old_sq) / jnp.sqrt(new_sq + EPS))).astype(jnp.bfloat16)


def renorm_kernel(s_ref, old_ref, *refs):
    out = refs[-1]
    at = 0
    for i in range(2):
        a, b, c = (ref[...].astype(jnp.float32) for ref in refs[3 * i : 3 * i + 3])
        rows = slice(at, at + a.shape[0])
        out[rows, :] = renormed(old_ref[rows, :], a + b + c)
        at += a.shape[0]


def renorm_units(position, old, upper, lower):
    rows, F = old.shape
    specs = [pl.BlockSpec((rows, F), lambda i, s: (0, 0))]
    for group in (upper, lower):
        size = group[2][0].shape[0]
        specs += [pl.BlockSpec((size, F), lambda i, s, at=at: (at(s), 0)) for _, at in group]
    return pl.pallas_call(
        renorm_kernel,
        grid_spec=pltpu.PrefetchScalarGridSpec(
            num_scalar_prefetch=1,
            grid=(1,),
            in_specs=specs,
            out_specs=pl.BlockSpec((rows, F), lambda i, s: (0, 0)),
        ),
        out_shape=jax.ShapeDtypeStruct((rows, F), jnp.bfloat16),
        cost_estimate=pl.CostEstimate(flops=10 * rows * F, bytes_accessed=12 * rows * F, transcendentals=0),
        name="renorm",
    )(position, old, *[array for array, _ in upper + lower])


def merge_kernel(s_ref, own_ref, far_ref, own_log, far_log, o_ref, *, stride):
    lane = lax.broadcasted_iota(jnp.int32, own_log.shape, 1)
    heads = o_ref.shape[1] // HD
    for j in range(heads):
        cs = slice(j * HD, (j + 1) * HD)
        at = pl.program_id(0) * heads + j
        pick = lambda ref, of: jnp.sum(
            jnp.where(of, ref[...].astype(jnp.float32), 0.0), axis=1, keepdims=True
        )
        own = pick(own_log, lane == at)
        far = pick(far_log, (lane == at) | (lane == at + stride) | (lane == at + 2 * stride))
        far = jnp.where(s_ref[0] == 0, -jnp.inf, far)
        top = jnp.maximum(own, far)
        own, far = jnp.exp2(own - top), jnp.exp2(far - top)
        share = own / (own + far)
        a, b = own_ref[:, cs].astype(jnp.float32), far_ref[:, cs].astype(jnp.float32)
        o_ref[:, cs] = (a * share + b * (1.0 - share)).astype(o_ref.dtype)


def merged(position, own, far, own_log, width):
    rows, cols = own.shape
    w = width * HD
    col = pl.BlockSpec((rows, w), lambda g, s: (0, g))
    log = lambda at: pl.BlockSpec((rows, HD), lambda g, s: (0, at))
    return pl.pallas_call(
        functools.partial(merge_kernel, stride=log_stride_of(cols)),
        grid_spec=pltpu.PrefetchScalarGridSpec(
            num_scalar_prefetch=1,
            grid=(cols // w,),
            in_specs=[col, col, log(0), log(cols // HD)],
            out_specs=col,
        ),
        out_shape=jax.ShapeDtypeStruct((rows, cols), jnp.bfloat16),
        cost_estimate=pl.CostEstimate(
            flops=8 * rows * cols, bytes_accessed=6 * rows * cols, transcendentals=rows * cols // HD
        ),
        name="merge",
    )(position, own, far, own_log, far)


def apply_kernel(s_ref, q_ref, high_ref, low_ref, *rest, tm, parts):
    n_ref, a_ref, o_ref = rest[-2], rest[-1], rest[-3]
    F = n_ref.shape[1]
    step = pl.program_id(0)

    @pl.when(step == 0)
    def _():
        for piece, row, n, start in parts:
            to = pl.multiple_of(start(s_ref), 16)
            n_ref[pl.ds(to, n), :] = rest[piece][row : row + n, :]
        a_ref[...] = low_ref[...]

    @pl.when(step == 1)
    def _():
        a_ref[...] = high_ref[...]

    n = q_ref.shape[0] // tm

    def first(i):
        return mm(q_ref[i * tm : (i + 1) * tm, :], n_ref[: 2 * F, :], NT)

    def second(i, h):
        g = h[:, :F]
        hid = (g * jax.nn.sigmoid(g) * h[:, F:]).astype(jnp.bfloat16)
        r = slice(i * tm, (i + 1) * tm)
        o_ref[r, :] = (a_ref[r, :].astype(jnp.float32) + mm(hid, n_ref[2 * F :, :], NT)).astype(o_ref.dtype)

    cur = first(0)
    for i in range(n):
        nxt = first(i + 1) if i + 1 < n else None
        second(i, cur)
        cur = nxt


def apply_head(position, head, fq, pieces, parts, high, low, into=None):
    rows, cols = fq.shape
    F = pieces[0].shape[1]
    half = rows // 2
    col = pl.BlockSpec((half, F), lambda i, s: (i, head(s)))
    part = pl.BlockSpec((half, F), lambda i, s: (0, head(s)))
    whole = lambda a: pl.BlockSpec(a.shape, lambda i, s: (0, 0))
    args = [position, fq, high, low, *pieces]
    specs = [col, part, part] + [whole(p) for p in pieces]
    aliases = {}
    if into is not None:
        aliases = {len(args): 0}
        args.append(into)
        specs.append(pl.BlockSpec(memory_space=pl.ANY))
    return pl.pallas_call(
        functools.partial(apply_kernel, tm=min(256, half), parts=parts),
        grid_spec=pltpu.PrefetchScalarGridSpec(
            num_scalar_prefetch=1,
            grid=(2,),
            in_specs=specs,
            out_specs=col,
            scratch_shapes=[pltpu.VMEM((3 * F, F), jnp.bfloat16), pltpu.VMEM((half, F), jnp.bfloat16)],
        ),
        out_shape=jax.ShapeDtypeStruct((rows, cols), jnp.bfloat16),
        input_output_aliases=aliases,
        cost_estimate=pl.CostEstimate(
            flops=6 * rows * F * F, bytes_accessed=rows * F * 6 + F * F * 6, transcendentals=rows * F
        ),
        name="apply",
    )(*args)


def exchange(block, bit):
    size = lax.axis_size("seq")
    return lax.ppermute(block, "seq", [(i, i ^ (1 << bit)) for i in range(size)])


def shifted(block, by):
    size = lax.axis_size("seq")
    return lax.ppermute(block, "seq", [(i, i + by) for i in range(size) if 0 <= i + by < size])


def synced(total, old, bits, position):
    offset = 0
    for bit in bits:
        half = total.shape[0] // 2
        mine = (position >> bit) & 1
        away = lax.dynamic_slice_in_dim(total, (1 - mine) * half, half, 0).astype(jnp.bfloat16)
        kept = lax.dynamic_slice_in_dim(total, mine * half, half, 0)
        total = kept + exchange(away, bit).astype(jnp.float32)
        offset = offset + mine * half
    part = renormed(lax.dynamic_slice_in_dim(old, offset, total.shape[0], 0), total)
    for bit in reversed(bits):
        mine = (position >> bit) & 1
        other = exchange(part, bit)
        part = jnp.concatenate(
            [jnp.where(mine == 0, part, other), jnp.where(mine == 0, other, part)], axis=0
        )
    return part


def synced_square(position, blocks, old):
    x, y = (position[0] >> 1) & 1, (position[0] >> 2) & 1
    keep_x, send_x, keep_y, send_y = blocks
    top0, bottom0 = exchange(send_x, 1), exchange(send_y, 2)

    def fold(a, b, at):
        n = a.shape[0] // 2
        a, b = (lax.dynamic_slice_in_dim(v, at * n, n, 0).astype(jnp.float32) for v in (a, b))
        return (a + b).astype(jnp.bfloat16)

    top1 = exchange(fold(keep_x, top0, 1 - y), 2)
    bottom1 = exchange(fold(keep_y, bottom0, 1 - x), 1)
    zero = lambda s: 0
    part = renorm_units(
        position,
        old,
        [(keep_x, at_y), (top0, at_y), (top1, zero)],
        [(keep_y, at_x), (bottom0, at_x), (bottom1, zero)],
    )
    n = top1.shape[0]
    over_x, over_y = exchange(part, 1), exchange(part, 2)
    top2, bottom2 = exchange(over_y[:n], 1), exchange(over_x[n:], 2)
    return [part, over_x, over_y, top2, bottom2]


def at_x(s):
    return (s[0] >> 1) & 1


def at_y(s):
    return (s[0] >> 2) & 1


def place(F, flip_x, flip_y):
    x = lambda s: at_x(s) ^ flip_x
    y = lambda s: at_y(s) ^ flip_y
    return lambda s: (2 * x(s) + y(s)) * (F // 4), lambda s: F + (2 * y(s) + x(s)) * (F // 2)


def shards(attn_q, attn_k, attn_v, fast_q, fast_k, fast_v, rates, fast_gate, fast_up, fast_down):
    position = lax.axis_index("seq").astype(jnp.int32).reshape(1)
    count = lax.axis_size("seq")
    heads = fast_gate.shape[0]
    rows = attn_q.shape[0]
    half = rows // 2
    width = 2 if attn_q.shape[1] // HD % 2 == 0 else 1
    prev = shifted(jnp.concatenate([attn_k[half:], attn_v[half:]], axis=0), 1)
    guests = shifted(attn_q[:half], -1)
    rates_t = rates.T
    weights = (fast_gate, fast_up, fast_down)

    def grads(head, received=None):
        return gradients(position, head, fast_k, fast_v, rates_t, *weights, received)

    if heads == 2 and count == 8:
        near, far = (lambda s: s[0] & 1), (lambda s: 1 - (s[0] & 1))
        received = exchange(grads(far)[0], 0)
        F = fast_gate.shape[1]
        n, m = F // 4, F // 2
        upper, lower = place(F, 0, 0)
        old = turned(position, near, *weights, parts=((n, upper), (m, lower)))
        blocks = grads(near, received)
        pieces = synced_square(position, blocks, old)
        other = [exchange(p, 0) for p in pieces]
        parts = []
        for piece, (flip_x, flip_y) in enumerate([(0, 0), (1, 0), (0, 1)]):
            upper, lower = place(F, flip_x, flip_y)
            parts += [(piece, 0, n, upper), (piece, n, m, lower)]
        upper, lower = place(F, 1, 1)
        parts += [(3, 0, n, upper), (4, 0, m, lower)]
        news = [(near, pieces, parts), (far, other, parts)]
    else:
        news = []
        bits = list(range(count.bit_length() - 1))
        for h in range(heads):
            head = lambda s, h=h: h
            old = turned(position, head, *weights)
            new = synced(grads(head)[0].astype(jnp.float32), old, bits, position[0])
            news.append((head, [new], [(0, 0, new.shape[0], lambda s: 0)]))
    bq = min(256, half)
    tiles = half // bq
    late = [
        [(0, t * bq, half, 1), (1, 0, half + (t + 1) * bq, -1)] for t in range(tiles)
    ]
    early = [[(0, 0, (t + 1) * bq, -1)] for t in range(tiles)]
    guest = [[(0, t * bq, rows, 1)] for t in range(tiles)]
    here = (attn_k, 0, attn_v, 0, rows)
    returned, own_out, own_log = attention(position, [(guests, 0, guest, 2), (attn_q, 0, early, 1)], [here], bq, width)
    far_out = shifted(returned, 1)
    (high,) = attention(position, [(attn_q, 1, late, 0)], [(prev, 0, prev, 1, half), here], bq, width)
    low = merged(position, own_out, far_out, own_log, width)
    mixed = None
    for head, pieces, parts in news:
        mixed = apply_head(position, head, fast_q, pieces, parts, high, low, mixed)
    return mixed


def solution(mesh):
    placed = (P("seq", "head"),) * 7 + (P("head", None, None),) * 3
    return jax.shard_map(shards, mesh=mesh, in_specs=placed, out_specs=P("seq", "head"), check_vma=False)
```

```python
import functools
import math

import jax
import jax.numpy as jnp
from jax import lax
from jax.experimental import pallas as pl
from jax.experimental.pallas import tpu as pltpu
from jax.sharding import PartitionSpec as P


HD = 128
EPS = 1e-06
NN = (((1,), (0,)), ((), ()))
NT = (((1,), (1,)), ((), ()))
TN = (((0,), (0,)), ((), ()))


def mm(a, b, dims=NN):
    return lax.dot_general(a, b, dims, preferred_element_type=jnp.float32)


def attn_kernel(position_ref, *refs, bq, jobs, sources, log_stride):
    queries = refs[: len(jobs)]
    keys = refs[len(jobs) : len(jobs) + sources]
    values = refs[len(jobs) + sources : len(jobs) + 2 * sources]
    rest = list(refs[len(jobs) + 2 * sources :])
    outs = []
    for _, sums in jobs:
        outs.append((rest.pop(0), rest.pop(0) if sums == 1 else None))
    bufs = (rest.pop(0), rest.pop(0))
    logs = [rest.pop(0) if sums else None for _, sums in jobs]
    group = pl.program_id(0)
    heads = queries[0].shape[1] // HD
    c = math.log2(math.e) / math.sqrt(HD)
    ri = lax.broadcasted_iota(jnp.int32, (bq, bq), 0)
    ci = lax.broadcasted_iota(jnp.int32, (bq, bq), 1)
    absent = position_ref[0] == 0
    units = [(h, j, t) for h in range(heads) for j in range(len(jobs)) for t in range(len(jobs[j][0]))]

    def scores(i):
        h, j, t = units[i]
        hs = slice(h * HD, (h + 1) * HD)
        buf = bufs[i % 2]
        q = queries[j][t * bq : (t + 1) * bq, hs]
        tops = []
        at = 0
        for source, lo, hi, edge in jobs[j][0][t]:
            s = mm(q, keys[source][lo:hi, hs], NT)
            n = hi - lo
            if edge == 1:
                kept = jnp.where(ci >= ri, s[:, :bq], -jnp.inf)
                s = jnp.concatenate([kept, s[:, bq:]], axis=1) if n > bq else kept
            elif edge == -1:
                kept = jnp.where(ci <= ri, s[:, n - bq :], -jnp.inf)
                s = jnp.concatenate([s[:, : n - bq], kept], axis=1) if n > bq else kept
            buf[:, at : at + n] = s
            tops.append(jnp.max(s, axis=1, keepdims=True))
            at += n
        if len(tops) == 1:
            return [tops[0] * c]
        m = jnp.maximum(tops[1], jnp.where(absent, -jnp.inf, tops[0])) * c
        return [jnp.where(absent, 1e30, m), m]

    def finish(i, ms):
        h, j, t = units[i]
        plan, sums = jobs[j]
        hs = slice(h * HD, (h + 1) * HD)
        buf = bufs[i % 2]
        out = total = None
        at = 0
        for (source, lo, hi, _), m in zip(plan[t], ms):
            p = jnp.exp2(buf[:, at : at + hi - lo] * c - m)
            part = jnp.sum(p, axis=1, keepdims=True)
            o = mm(p.astype(jnp.bfloat16), values[source][lo:hi, hs])
            total = part if total is None else total + part
            out = o if out is None else out + o
            at += hi - lo
        rows = slice(t * bq, (t + 1) * bq)
        out = (out / total).astype(jnp.bfloat16)
        head = group * heads + h
        if sums == 2:
            outs[j][0][rows, pl.ds(pl.multiple_of(head * HD, HD), HD)] = out
        else:
            outs[j][0][rows, hs] = out
        if sums:
            lane = lax.broadcasted_iota(jnp.int32, (bq, HD), 1)
            log = ms[-1] + jnp.log(total) * math.log2(math.e)
            logs[j][rows, :] = jnp.where(lane == head, log, logs[j][rows, :])

    if any(sums for _, sums in jobs):

        @pl.when(group == 0)
        def _():
            for log in logs:
                if log is not None:
                    log[...] = jnp.zeros(log.shape, log.dtype)

    ms = scores(0)
    for i in range(len(units)):
        nxt = scores(i + 1) if i + 1 < len(units) else None
        finish(i, ms)
        ms = nxt
    if any(sums for _, sums in jobs):

        @pl.when(group == pl.num_programs(0) - 1)
        def _():
            for (_, sums), (out, log_out), log in zip(jobs, outs, logs):
                if sums == 1:
                    log_out[...] = log[...]
                if sums == 2:
                    x = log[...]
                    a = x.astype(jnp.bfloat16).astype(jnp.float32)
                    b = (x - a).astype(jnp.bfloat16).astype(jnp.float32)
                    x = a + pltpu.roll(b, log_stride, 1) + pltpu.roll(x - a - b, 2 * log_stride, 1)
                    out[:, out.shape[1] - HD :] = x.astype(jnp.bfloat16)


def log_stride_of(cols):
    return 16 * pl.cdiv(cols // HD, 16)


def attention(position, jobs, sources, bq, width):
    cols = jobs[0][0].shape[1]
    w = width * HD
    ranges = [r for _, _, plan, _ in jobs for tile in plan for r in tile]
    span = max(sum(hi - lo for _, lo, hi, _ in tile) for _, _, plan, _ in jobs for tile in plan)
    pairs = bq * sum(hi - lo for _, lo, hi, _ in ranges) * cols // HD
    block = lambda n, at: pl.BlockSpec((n, w), lambda g, f: (at, g))
    whole = lambda *shape: pl.BlockSpec(shape, lambda g, f: (0, 0))
    outs, out_specs, logs = [], [], []
    for _, _, plan, sums in jobs:
        rows = len(plan) * bq
        if sums == 2:
            outs.append(jax.ShapeDtypeStruct((rows, cols + HD), jnp.bfloat16))
            out_specs.append(whole(rows, cols + HD))
        else:
            outs.append(jax.ShapeDtypeStruct((rows, cols), jnp.bfloat16))
            out_specs.append(block(rows, 0))
        if sums == 1:
            outs.append(jax.ShapeDtypeStruct((rows, HD), jnp.float32))
            out_specs.append(whole(rows, HD))
        if sums:
            logs.append(pltpu.VMEM((rows, HD), jnp.float32))
    specs = [block(len(plan) * bq, at) for _, at, plan, _ in jobs]
    specs += [block(n, at) for _, at, _, _, n in sources] + [block(n, at) for _, _, _, at, n in sources]
    kernel = functools.partial(
        attn_kernel,
        bq=bq,
        jobs=[(plan, sums) for _, _, plan, sums in jobs],
        sources=len(sources),
        log_stride=log_stride_of(cols),
    )
    return pl.pallas_call(
        kernel,
        grid_spec=pltpu.PrefetchScalarGridSpec(
            num_scalar_prefetch=1,
            grid=(cols // w,),
            in_specs=specs,
            out_specs=out_specs,
            scratch_shapes=[pltpu.VMEM((bq, span), jnp.float32)] * 2 + logs,
        ),
        out_shape=outs,
        cost_estimate=pl.CostEstimate(
            flops=4 * pairs * HD, bytes_accessed=8 * bq * cols * len(ranges), transcendentals=pairs
        ),
    )(position, *[job[0] for job in jobs], *[x[0] for x in sources], *[x[2] for x in sources])


def owned_rows(F):
    n, m, half = F // 4, F // 8, 3 * F // 2
    unit = 3 * F // 8
    segments = []
    for k in range(4):
        upper, lower = k * unit, half + (2 * (k % 2) + k // 2) * unit
        segments += [
            (k * n, (k + 1) * n, upper),
            (F + k * n, F + k * n + m, upper + n),
            (F + k * n + m, F + (k + 1) * n, lower),
            (2 * F + k * n, 2 * F + (k + 1) * n, lower + m),
        ]
    return segments


def at_x(s):
    return (s[0] >> 1) & 1


def at_y(s):
    return (s[0] >> 2) & 1


def grad_kernel(s_ref, x_ref, v_ref, r_ref, w1_ref, w3_ref, w2_ref, *refs, head, tm, tn, split):
    w13, w2, gu, hid, og = refs[-5:]
    F = w1_ref.shape[2]
    rows = x_ref.shape[0]
    w13[:, :F] = w1_ref[0].astype(jnp.bfloat16)
    w13[:, F:] = w3_ref[0].astype(jnp.bfloat16)
    w2[...] = w2_ref[0].astype(jnp.bfloat16)
    pick = lax.broadcasted_iota(jnp.int32, r_ref.shape, 0) == head(s_ref)
    rate = jnp.sum(jnp.where(pick, r_ref[...], 0.0), axis=0, keepdims=True)
    rate = jnp.transpose(jnp.broadcast_to(rate, (8, rows)))[:, :1]
    og[...] = (-rate * v_ref[...].astype(jnp.float32)).astype(jnp.bfloat16)
    n = rows // tm

    def products(i):
        r = slice(i * tm, (i + 1) * tm)
        return mm(x_ref[r, :], w13[...]), mm(og[r, :], w2[...], NT)

    def finish(i, pre, hg):
        r = slice(i * tm, (i + 1) * tm)
        pg, pu = pre[:, :F], pre[:, F:]
        sg = jax.nn.sigmoid(pg)
        act = pg * sg
        gu[r, :F] = (hg * pu * (sg * (1.0 + pg * (1.0 - sg)))).astype(jnp.bfloat16)
        gu[r, F:] = (hg * act).astype(jnp.bfloat16)
        hid[r, :] = (act * pu).astype(jnp.bfloat16)

    cur = products(0)
    for i in range(n):
        nxt = products(i + 1) if i + 1 < n else None
        finish(i, *cur)
        cur = nxt
    x = x_ref[...]
    hd = hid[...]
    x1, y1 = at_x(s_ref), at_y(s_ref)
    block_rows = 3 * F // 4
    segments = owned_rows(F) if split else []

    def put(lo, grad):
        if not split:
            refs[0][lo : lo + grad.shape[0], :] = grad.astype(refs[0].dtype)
            return
        grad = grad + refs[0][lo : lo + grad.shape[0], :].astype(jnp.float32)
        for a, b, to in segments:
            a, b, to = max(lo, a), min(lo + grad.shape[0], b), to + max(lo - a, 0)
            if a < b:
                block, row = divmod(to, block_rows)
                slot = jnp.where((x1 if block < 2 else y1) == block % 2, 0, 1)
                part = grad[a - lo : b - lo].astype(jnp.bfloat16)
                refs[1 + block // 2][slot, row : row + b - a, :] = part

    for j in range(2 * F // tn):
        put(j * tn, mm(gu[:, j * tn : (j + 1) * tn], x, TN))
    for j in range(F // HD):
        put(2 * F + j * HD, mm(og[:, j * HD : (j + 1) * HD], hd, TN))
    if split:
        for o in range(2):
            refs[3 + 2 * o][...] = refs[1 + o][0]
            refs[4 + 2 * o][...] = refs[1 + o][1]


def gradients(position, head, fk, fv, rates_t, w1, w3, w2, received=None):
    rows = fk.shape[0]
    F = w1.shape[1]
    tm = min(256, rows)
    tn = 256 if 2 * F % 256 == 0 else HD
    col = pl.BlockSpec((rows, F), lambda i, s: (0, head(s)))
    weight = pl.BlockSpec((1, F, F), lambda i, s: (head(s), 0, 0))
    whole = lambda *shape: pl.BlockSpec(shape, lambda i, s: (0,) * len(shape))
    bf = jnp.bfloat16
    args = [position, fk, fv, rates_t, w1, w3, w2]
    specs = [col, col, whole(*rates_t.shape), weight, weight, weight]
    scratch = [
        pltpu.VMEM((F, 2 * F), bf),
        pltpu.VMEM((F, F), bf),
        pltpu.VMEM((rows, 2 * F), bf),
        pltpu.VMEM((rows, F), bf),
        pltpu.VMEM((rows, F), bf),
    ]
    if received is None:
        shapes = [(3 * F, F)]
    else:
        shapes = [(3 * F // 4, F)] * 4
        args.append(received)
        specs.append(whole(3 * F, F))
        scratch = [pltpu.VMEM((2, 3 * F // 4, F), bf)] * 2 + scratch
    kernel = functools.partial(grad_kernel, head=head, tm=tm, tn=tn, split=received is not None)

    def body(*refs):
        if received is None:
            return kernel(*refs)
        ins, outs, halves, rest = refs[:8], refs[8:12], refs[12:14], refs[14:]
        return kernel(*ins, *halves, *outs, *rest)

    return pl.pallas_call(
        body,
        grid_spec=pltpu.PrefetchScalarGridSpec(
            num_scalar_prefetch=1,
            grid=(1,),
            in_specs=specs,
            out_specs=[whole(*shape) for shape in shapes],
            scratch_shapes=scratch,
        ),
        out_shape=[jax.ShapeDtypeStruct(shape, bf) for shape in shapes],
        cost_estimate=pl.CostEstimate(
            flops=12 * rows * F * F, bytes_accessed=rows * F * 4 + F * F * 18, transcendentals=rows * F
        ),
        name="grads",
    )(*args)


def turn_kernel(s_ref, w1, w3, w2, o_ref, *scratch, parts):
    F = w1.shape[2]
    all_ref = scratch[0] if scratch else o_ref
    all_ref[:F, :] = w1[0].T
    all_ref[F : 2 * F, :] = w3[0].T
    all_ref[2 * F :, :] = w2[0].T
    at = 0
    for n, start in parts:
        o_ref[at : at + n, :] = all_ref[pl.ds(pl.multiple_of(start(s_ref), 8), n), :]
        at += n


def turned(position, head, w1, w3, w2, parts=()):
    F = w1.shape[1]
    weight = pl.BlockSpec((1, F, F), lambda i, s: (head(s), 0, 0))
    shape = (sum(n for n, _ in parts), F) if parts else (3 * F, F)
    return pl.pallas_call(
        functools.partial(turn_kernel, parts=parts),
        grid_spec=pltpu.PrefetchScalarGridSpec(
            num_scalar_prefetch=1,
            grid=(1,),
            in_specs=[weight] * 3,
            out_specs=pl.BlockSpec(shape, lambda i, s: (0, 0)),
            scratch_shapes=[pltpu.VMEM((3 * F, F), jnp.float32)] if parts else [],
        ),
        out_shape=jax.ShapeDtypeStruct(shape, jnp.float32),
        cost_estimate=pl.CostEstimate(flops=3 * F * F, bytes_accessed=24 * F * F, transcendentals=0),
        name="turned",
    )(position, w1, w3, w2)


def renormed(old, grad):
    new = old - grad
    old_sq = jnp.sum(old * old, axis=-1, keepdims=True)
    new_sq = jnp.sum(new * new, axis=-1, keepdims=True)
    return (new * (jnp.sqrt(old_sq) / jnp.sqrt(new_sq + EPS))).astype(jnp.bfloat16)


def renorm_kernel(s_ref, old_ref, *refs):
    out = refs[-1]
    at = 0
    for i in range(2):
        a, b, c = (ref[...].astype(jnp.float32) for ref in refs[3 * i : 3 * i + 3])
        rows = slice(at, at + a.shape[0])
        out[rows, :] = renormed(old_ref[rows, :], a + b + c)
        at += a.shape[0]


def renorm_units(position, old, upper, lower):
    rows, F = old.shape
    specs = [pl.BlockSpec((rows, F), lambda i, s: (0, 0))]
    for group in (upper, lower):
        size = group[2][0].shape[0]
        specs += [pl.BlockSpec((size, F), lambda i, s, at=at: (at(s), 0)) for _, at in group]
    return pl.pallas_call(
        renorm_kernel,
        grid_spec=pltpu.PrefetchScalarGridSpec(
            num_scalar_prefetch=1,
            grid=(1,),
            in_specs=specs,
            out_specs=pl.BlockSpec((rows, F), lambda i, s: (0, 0)),
        ),
        out_shape=jax.ShapeDtypeStruct((rows, F), jnp.bfloat16),
        cost_estimate=pl.CostEstimate(flops=10 * rows * F, bytes_accessed=12 * rows * F, transcendentals=0),
        name="renorm",
    )(position, old, *[array for array, _ in upper + lower])


def merge_kernel(s_ref, own_ref, far_ref, own_log, far_log, o_ref, *, stride):
    lane = lax.broadcasted_iota(jnp.int32, own_log.shape, 1)
    heads = o_ref.shape[1] // HD
    for j in range(heads):
        cs = slice(j * HD, (j + 1) * HD)
        at = pl.program_id(0) * heads + j
        pick = lambda ref, of: jnp.sum(
            jnp.where(of, ref[...].astype(jnp.float32), 0.0), axis=1, keepdims=True
        )
        own = pick(own_log, lane == at)
        far = pick(far_log, (lane == at) | (lane == at + stride) | (lane == at + 2 * stride))
        far = jnp.where(s_ref[0] == 0, -jnp.inf, far)
        top = jnp.maximum(own, far)
        own, far = jnp.exp2(own - top), jnp.exp2(far - top)
        share = own / (own + far)
        a, b = own_ref[:, cs].astype(jnp.float32), far_ref[:, cs].astype(jnp.float32)
        o_ref[:, cs] = (a * share + b * (1.0 - share)).astype(o_ref.dtype)


def merged(position, own, far, own_log, width):
    rows, cols = own.shape
    w = width * HD
    col = pl.BlockSpec((rows, w), lambda g, s: (0, g))
    log = lambda at: pl.BlockSpec((rows, HD), lambda g, s: (0, at))
    return pl.pallas_call(
        functools.partial(merge_kernel, stride=log_stride_of(cols)),
        grid_spec=pltpu.PrefetchScalarGridSpec(
            num_scalar_prefetch=1,
            grid=(cols // w,),
            in_specs=[col, col, log(0), log(cols // HD)],
            out_specs=col,
        ),
        out_shape=jax.ShapeDtypeStruct((rows, cols), jnp.bfloat16),
        cost_estimate=pl.CostEstimate(
            flops=8 * rows * cols, bytes_accessed=6 * rows * cols, transcendentals=rows * cols // HD
        ),
        name="merge",
    )(position, own, far, own_log, far)


def gated(h, n):
    g = h[:, :n]
    return (g * jax.nn.sigmoid(g) * h[:, n:]).astype(jnp.bfloat16)


def staggered(n, first, second):
    cur = first(0)
    for i in range(n):
        nxt = first(i + 1) if i + 1 < n else None
        second(i, cur)
        cur = nxt


def put_quarter(s_ref, ref, rows, values, flip_x, flip_y):
    n = ref.shape[1] // 4
    chip = 2 * (at_x(s_ref) ^ flip_x) + (at_y(s_ref) ^ flip_y)
    for k in range(4):

        @pl.when(chip == k)
        def _():
            ref[rows, k * n : (k + 1) * n] = values


def hidden_kernel(s_ref, q_ref, own_ref, over_x, over_y, o_ref, w_ref, v_ref, *, tm):
    F = q_ref.shape[1]
    n = F // 4

    @pl.when(pl.program_id(0) == 0)
    def _():
        for i, ref in enumerate((own_ref, over_x, over_y)):
            w_ref[i * n : (i + 1) * n, :] = ref[:n, :]
            w_ref[(3 + i) * n : (4 + i) * n, :] = ref[n : 2 * n, :]

    def first(i):
        return mm(q_ref[i * tm : (i + 1) * tm, :], w_ref[...], NT)

    def second(i, h):
        v_ref[i * tm : (i + 1) * tm, : 3 * n] = gated(h, 3 * n)

    staggered(q_ref.shape[0] // tm, first, second)
    every = slice(0, q_ref.shape[0])
    for i, flips in enumerate(((0, 0), (1, 0), (0, 1))):
        put_quarter(s_ref, o_ref, every, v_ref[:, i * n : (i + 1) * n], *flips)


def hidden_part(position, head, fq, pieces):
    rows = fq.shape[0]
    F = pieces[0].shape[1]
    half = rows // 2
    whole = pl.BlockSpec(pieces[0].shape, lambda i, s: (0, 0))
    bf = jnp.bfloat16
    return pl.pallas_call(
        functools.partial(hidden_kernel, tm=min(256, half)),
        grid_spec=pltpu.PrefetchScalarGridSpec(
            num_scalar_prefetch=1,
            grid=(2,),
            in_specs=[pl.BlockSpec((half, F), lambda i, s: (i, head(s)))] + [whole] * 3,
            out_specs=pl.BlockSpec((half, F), lambda i, s: (i, 0)),
            scratch_shapes=[pltpu.VMEM((3 * F // 2, F), bf), pltpu.VMEM((half, F), bf)],
        ),
        out_shape=jax.ShapeDtypeStruct((rows, F), bf),
        cost_estimate=pl.CostEstimate(
            flops=3 * rows * F * F, bytes_accessed=rows * F * 4 + F * F * 3, transcendentals=rows * F
        ),
        name="hidden",
    )(position, fq, *pieces[:3])


def apply_kernel(s_ref, q_ref, high_ref, low_ref, *rest, tm, split):
    n_ref, w_ref, h_ref, a_ref = rest[-4:]
    o_ref = rest[-5]
    F = q_ref.shape[1]
    n, m = F // 4, F // 8
    step = pl.program_id(0)

    @pl.when(step == 0)
    def _():
        if split:
            own, over_x, over_y, upper, lower = rest[1:6]
            for ref, row, flips in (
                (own, 2 * n, (0, 0)),
                (over_x, 2 * n, (1, 0)),
                (over_y, 2 * n, (0, 1)),
                (lower, m, (1, 1)),
            ):
                to = pl.multiple_of(quarter(F, *flips)(s_ref), 16)
                n_ref[pl.ds(to, n), :] = ref[row : row + n, :]
            w_ref[: n + m, :] = upper[...]
            w_ref[n + m :, :] = lower[:m, :]
        else:
            w_ref[...] = rest[0][: 2 * F, :]
            n_ref[...] = rest[0][2 * F :, :]
        a_ref[...] = low_ref[...]

    @pl.when(step == 1)
    def _():
        a_ref[...] = high_ref[...]

    def first(i):
        return mm(q_ref[i * tm : (i + 1) * tm, :], w_ref[...], NT)

    def second(i, h):
        r = slice(i * tm, (i + 1) * tm)
        if split:
            h_ref[r, :] = rest[0][r, :]
            put_quarter(s_ref, h_ref, r, gated(h, n), 1, 1)
            hid = h_ref[r, :]
        else:
            hid = gated(h, F)
        o_ref[r, :] = (a_ref[r, :].astype(jnp.float32) + mm(hid, n_ref[...], NT)).astype(o_ref.dtype)

    staggered(q_ref.shape[0] // tm, first, second)


def apply_head(position, head, fq, hidden, pieces, high, low, into=None):
    rows, cols = fq.shape
    F = pieces[0].shape[1]
    half = rows // 2
    split = hidden is not None
    col = pl.BlockSpec((half, F), lambda i, s: (i, head(s)))
    part = pl.BlockSpec((half, F), lambda i, s: (0, head(s)))
    whole = lambda a: pl.BlockSpec(a.shape, lambda i, s: (0, 0))
    args = [position, fq, high, low]
    specs = [col, part, part]
    if split:
        args.append(hidden)
        specs.append(pl.BlockSpec((half, F), lambda i, s: (i, 0)))
    args += pieces
    specs += [whole(p) for p in pieces]
    aliases = {}
    if into is not None:
        aliases = {len(args): 0}
        args.append(into)
        specs.append(pl.BlockSpec(memory_space=pl.ANY))
    bf = jnp.bfloat16
    return pl.pallas_call(
        functools.partial(apply_kernel, tm=min(256, half), split=split),
        grid_spec=pltpu.PrefetchScalarGridSpec(
            num_scalar_prefetch=1,
            grid=(2,),
            in_specs=specs,
            out_specs=col,
            scratch_shapes=[
                pltpu.VMEM((F, F), bf),
                pltpu.VMEM((F // 2 if split else 2 * F, F), bf),
                pltpu.VMEM((half, F), bf),
                pltpu.VMEM((half, F), bf),
            ],
        ),
        out_shape=jax.ShapeDtypeStruct((rows, cols), bf),
        input_output_aliases=aliases,
        cost_estimate=pl.CostEstimate(
            flops=3 * rows * F * F, bytes_accessed=rows * F * 8 + F * F * 6, transcendentals=rows * F
        ),
        name="apply",
    )(*args)


def exchange(block, bit):
    size = lax.axis_size("seq")
    return lax.ppermute(block, "seq", [(i, i ^ (1 << bit)) for i in range(size)])


def shifted(block, by):
    size = lax.axis_size("seq")
    return lax.ppermute(block, "seq", [(i, i + by) for i in range(size) if 0 <= i + by < size])


def synced(total, old, bits, position):
    offset = 0
    for bit in bits:
        half = total.shape[0] // 2
        mine = (position >> bit) & 1
        away = lax.dynamic_slice_in_dim(total, (1 - mine) * half, half, 0).astype(jnp.bfloat16)
        kept = lax.dynamic_slice_in_dim(total, mine * half, half, 0)
        total = kept + exchange(away, bit).astype(jnp.float32)
        offset = offset + mine * half
    part = renormed(lax.dynamic_slice_in_dim(old, offset, total.shape[0], 0), total)
    for bit in reversed(bits):
        mine = (position >> bit) & 1
        other = exchange(part, bit)
        part = jnp.concatenate(
            [jnp.where(mine == 0, part, other), jnp.where(mine == 0, other, part)], axis=0
        )
    return part


def synced_square(position, blocks, old):
    x, y = (position[0] >> 1) & 1, (position[0] >> 2) & 1
    keep_x, send_x, keep_y, send_y = blocks
    top0, bottom0 = exchange(send_x, 1), exchange(send_y, 2)

    def fold(a, b, at):
        n = a.shape[0] // 2
        a, b = (lax.dynamic_slice_in_dim(v, at * n, n, 0).astype(jnp.float32) for v in (a, b))
        return (a + b).astype(jnp.bfloat16)

    top1 = exchange(fold(keep_x, top0, 1 - y), 2)
    bottom1 = exchange(fold(keep_y, bottom0, 1 - x), 1)
    zero = lambda s: 0
    part = renorm_units(
        position,
        old,
        [(keep_x, at_y), (top0, at_y), (top1, zero)],
        [(keep_y, at_x), (bottom0, at_x), (bottom1, zero)],
    )
    n = top1.shape[0]
    over_x, over_y = exchange(part, 1), exchange(part, 2)
    top2, bottom2 = exchange(over_y[:n], 1), exchange(over_x[n:], 2)
    return [part, over_x, over_y, top2, bottom2]


def quarter(F, flip_x=0, flip_y=0):
    return lambda s: (2 * (at_x(s) ^ flip_x) + (at_y(s) ^ flip_y)) * (F // 4)


def shards(attn_q, attn_k, attn_v, fast_q, fast_k, fast_v, rates, fast_gate, fast_up, fast_down):
    position = lax.axis_index("seq").astype(jnp.int32).reshape(1)
    count = lax.axis_size("seq")
    heads = fast_gate.shape[0]
    rows = attn_q.shape[0]
    half = rows // 2
    width = 2 if attn_q.shape[1] // HD % 2 == 0 else 1
    prev = shifted(jnp.concatenate([attn_k[half:], attn_v[half:]], axis=0), 1)
    guests = shifted(attn_q[:half], -1)
    rates_t = rates.T
    weights = (fast_gate, fast_up, fast_down)

    def grads(head, received=None):
        return gradients(position, head, fast_k, fast_v, rates_t, *weights, received)

    if heads == 2 and count == 8:
        near, far = (lambda s: s[0] & 1), (lambda s: 1 - (s[0] & 1))
        received = exchange(grads(far)[0], 0)
        F = fast_gate.shape[1]
        mine = quarter(F)
        starts = [(F // 4, lambda s, at=i * F: at + mine(s)) for i in range(3)]
        old = turned(position, near, *weights, parts=tuple(starts))
        blocks = grads(near, received)
        pieces = synced_square(position, blocks, old)
        other = [exchange(p, 0) for p in pieces]
        news = []
        for head, new in ((near, pieces), (far, other)):
            news.append((head, hidden_part(position, head, fast_q, new), new))
    else:
        news = []
        bits = list(range(count.bit_length() - 1))
        for h in range(heads):
            head = lambda s, h=h: h
            old = turned(position, head, *weights)
            new = synced(grads(head)[0].astype(jnp.float32), old, bits, position[0])
            news.append((head, None, [new]))
    bq = min(256, half)
    tiles = half // bq
    late = [
        [(0, t * bq, half, 1), (1, 0, half + (t + 1) * bq, -1)] for t in range(tiles)
    ]
    early = [[(0, 0, (t + 1) * bq, -1)] for t in range(tiles)]
    guest = [[(0, t * bq, rows, 1)] for t in range(tiles)]
    here = (attn_k, 0, attn_v, 0, rows)
    returned, own_out, own_log = attention(position, [(guests, 0, guest, 2), (attn_q, 0, early, 1)], [here], bq, width)
    far_out = shifted(returned, 1)
    (high,) = attention(position, [(attn_q, 1, late, 0)], [(prev, 0, prev, 1, half), here], bq, width)
    low = merged(position, own_out, far_out, own_log, width)
    mixed = None
    for head, hidden, new in news:
        mixed = apply_head(position, head, fast_q, hidden, new, high, low, mixed)
    return mixed


def solution(mesh):
    placed = (P("seq", "head"),) * 7 + (P("head", None, None),) * 3
    return jax.shard_map(shards, mesh=mesh, in_specs=placed, out_specs=P("seq", "head"), check_vma=False)
```

```python
import functools
import math

import jax
import jax.numpy as jnp
from jax import lax
from jax.experimental import pallas as pl
from jax.experimental.pallas import tpu as pltpu
from jax.sharding import PartitionSpec as P


HD = 128
EPS = 1e-06
NN = (((1,), (0,)), ((), ()))
NT = (((1,), (1,)), ((), ()))
TN = (((0,), (0,)), ((), ()))


def room(mib):
    return pltpu.CompilerParams(vmem_limit_bytes=mib << 20)


def mm(a, b, dims=NN):
    return lax.dot_general(a, b, dims, preferred_element_type=jnp.float32)


def attn_kernel(position_ref, *refs, bq, jobs, sources, log_stride):
    queries = refs[: len(jobs)]
    keys = refs[len(jobs) : len(jobs) + sources]
    values = refs[len(jobs) + sources : len(jobs) + 2 * sources]
    rest = list(refs[len(jobs) + 2 * sources :])
    outs = []
    for _, sums in jobs:
        outs.append((rest.pop(0), rest.pop(0) if sums == 1 else None))
    bufs = (rest.pop(0), rest.pop(0))
    logs = [rest.pop(0) if sums else None for _, sums in jobs]
    group = pl.program_id(0)
    heads = queries[0].shape[1] // HD
    c = math.log2(math.e) / math.sqrt(HD)
    ri = lax.broadcasted_iota(jnp.int32, (bq, bq), 0)
    ci = lax.broadcasted_iota(jnp.int32, (bq, bq), 1)
    absent = position_ref[0] == 0
    units = [(h, j, t) for h in range(heads) for j in range(len(jobs)) for t in range(len(jobs[j][0]))]

    def scores(i):
        h, j, t = units[i]
        hs = slice(h * HD, (h + 1) * HD)
        buf = bufs[i % 2]
        q = queries[j][t * bq : (t + 1) * bq, hs]
        tops = []
        at = 0
        for source, lo, hi, edge in jobs[j][0][t]:
            s = mm(q, keys[source][lo:hi, hs], NT)
            n = hi - lo
            if edge == 1:
                kept = jnp.where(ci >= ri, s[:, :bq], -jnp.inf)
                s = jnp.concatenate([kept, s[:, bq:]], axis=1) if n > bq else kept
            elif edge == -1:
                kept = jnp.where(ci <= ri, s[:, n - bq :], -jnp.inf)
                s = jnp.concatenate([s[:, : n - bq], kept], axis=1) if n > bq else kept
            buf[:, at : at + n] = s
            tops.append(jnp.max(s, axis=1, keepdims=True))
            at += n
        if len(tops) == 1:
            return [tops[0] * c]
        m = jnp.maximum(tops[1], jnp.where(absent, -jnp.inf, tops[0])) * c
        return [jnp.where(absent, 1e30, m), m]

    def finish(i, ms):
        h, j, t = units[i]
        plan, sums = jobs[j]
        hs = slice(h * HD, (h + 1) * HD)
        buf = bufs[i % 2]
        out = total = None
        at = 0
        for (source, lo, hi, _), m in zip(plan[t], ms):
            p = jnp.exp2(buf[:, at : at + hi - lo] * c - m)
            part = jnp.sum(p, axis=1, keepdims=True)
            o = mm(p.astype(jnp.bfloat16), values[source][lo:hi, hs])
            total = part if total is None else total + part
            out = o if out is None else out + o
            at += hi - lo
        rows = slice(t * bq, (t + 1) * bq)
        out = (out / total).astype(jnp.bfloat16)
        head = group * heads + h
        if sums == 2:
            outs[j][0][rows, pl.ds(pl.multiple_of(head * HD, HD), HD)] = out
        else:
            outs[j][0][rows, hs] = out
        if sums:
            lane = lax.broadcasted_iota(jnp.int32, (bq, HD), 1)
            log = ms[-1] + jnp.log(total) * math.log2(math.e)
            logs[j][rows, :] = jnp.where(lane == head, log, logs[j][rows, :])

    if any(sums for _, sums in jobs):

        @pl.when(group == 0)
        def _():
            for log in logs:
                if log is not None:
                    log[...] = jnp.zeros(log.shape, log.dtype)

    ms = scores(0)
    for i in range(len(units)):
        nxt = scores(i + 1) if i + 1 < len(units) else None
        finish(i, ms)
        ms = nxt
    if any(sums for _, sums in jobs):

        @pl.when(group == pl.num_programs(0) - 1)
        def _():
            for (_, sums), (out, log_out), log in zip(jobs, outs, logs):
                if sums == 1:
                    log_out[...] = log[...]
                if sums == 2:
                    x = log[...]
                    a = x.astype(jnp.bfloat16).astype(jnp.float32)
                    b = (x - a).astype(jnp.bfloat16).astype(jnp.float32)
                    x = a + pltpu.roll(b, log_stride, 1) + pltpu.roll(x - a - b, 2 * log_stride, 1)
                    out[:, out.shape[1] - HD :] = x.astype(jnp.bfloat16)


def log_stride_of(cols):
    return 16 * pl.cdiv(cols // HD, 16)


def attention(position, jobs, sources, bq, width):
    cols = jobs[0][0].shape[1]
    w = width * HD
    ranges = [r for _, _, plan, _ in jobs for tile in plan for r in tile]
    span = max(sum(hi - lo for _, lo, hi, _ in tile) for _, _, plan, _ in jobs for tile in plan)
    pairs = bq * sum(hi - lo for _, lo, hi, _ in ranges) * cols // HD
    block = lambda n, at: pl.BlockSpec((n, w), lambda g, f: (at, g))
    whole = lambda *shape: pl.BlockSpec(shape, lambda g, f: (0, 0))
    outs, out_specs, logs = [], [], []
    for _, _, plan, sums in jobs:
        rows = len(plan) * bq
        if sums == 2:
            outs.append(jax.ShapeDtypeStruct((rows, cols + HD), jnp.bfloat16))
            out_specs.append(whole(rows, cols + HD))
        else:
            outs.append(jax.ShapeDtypeStruct((rows, cols), jnp.bfloat16))
            out_specs.append(block(rows, 0))
        if sums == 1:
            outs.append(jax.ShapeDtypeStruct((rows, HD), jnp.float32))
            out_specs.append(whole(rows, HD))
        if sums:
            logs.append(pltpu.VMEM((rows, HD), jnp.float32))
    specs = [block(len(plan) * bq, at) for _, at, plan, _ in jobs]
    specs += [block(n, at) for _, at, _, _, n in sources] + [block(n, at) for _, _, _, at, n in sources]
    kernel = functools.partial(
        attn_kernel,
        bq=bq,
        jobs=[(plan, sums) for _, _, plan, sums in jobs],
        sources=len(sources),
        log_stride=log_stride_of(cols),
    )
    return pl.pallas_call(
        kernel,
        grid_spec=pltpu.PrefetchScalarGridSpec(
            num_scalar_prefetch=1,
            grid=(cols // w,),
            in_specs=specs,
            out_specs=out_specs,
            scratch_shapes=[pltpu.VMEM((bq, span), jnp.float32)] * 2 + logs,
        ),
        out_shape=outs,
        cost_estimate=pl.CostEstimate(
            flops=4 * pairs * HD, bytes_accessed=8 * bq * cols * len(ranges), transcendentals=pairs
        ),
        compiler_params=room(14),
    )(position, *[job[0] for job in jobs], *[x[0] for x in sources], *[x[2] for x in sources])


def owned_rows(F):
    n, m, half = F // 4, F // 8, 3 * F // 2
    unit = 3 * F // 8
    segments = []
    for k in range(4):
        upper, lower = k * unit, half + (2 * (k % 2) + k // 2) * unit
        segments += [
            (k * n, (k + 1) * n, upper),
            (F + k * n, F + k * n + m, upper + n),
            (F + k * n + m, F + (k + 1) * n, lower),
            (2 * F + k * n, 2 * F + (k + 1) * n, lower + m),
        ]
    return segments


def at_x(s):
    return (s[0] >> 1) & 1


def at_y(s):
    return (s[0] >> 2) & 1


def grad_kernel(s_ref, x_ref, v_ref, r_ref, w1_ref, w3_ref, w2_ref, *refs, head, tm, tn, split):
    w13, w2, gu, hid, og = refs[-5:]
    F = w1_ref.shape[2]
    rows = x_ref.shape[0]
    w13[:, :F] = w1_ref[0].astype(jnp.bfloat16)
    w13[:, F:] = w3_ref[0].astype(jnp.bfloat16)
    w2[...] = w2_ref[0].astype(jnp.bfloat16)
    pick = lax.broadcasted_iota(jnp.int32, r_ref.shape, 0) == head(s_ref)
    rate = jnp.sum(jnp.where(pick, r_ref[...], 0.0), axis=0, keepdims=True)
    rate = jnp.transpose(jnp.broadcast_to(rate, (8, rows)))[:, :1]
    og[...] = (-rate * v_ref[...].astype(jnp.float32)).astype(jnp.bfloat16)
    n = rows // tm

    def products(i):
        r = slice(i * tm, (i + 1) * tm)
        return mm(x_ref[r, :], w13[...]), mm(og[r, :], w2[...], NT)

    def finish(i, pre, hg):
        r = slice(i * tm, (i + 1) * tm)
        pg, pu = pre[:, :F], pre[:, F:]
        sg = jax.nn.sigmoid(pg)
        act = pg * sg
        gu[r, :F] = (hg * pu * (sg * (1.0 + pg * (1.0 - sg)))).astype(jnp.bfloat16)
        gu[r, F:] = (hg * act).astype(jnp.bfloat16)
        hid[r, :] = (act * pu).astype(jnp.bfloat16)

    cur = products(0)
    for i in range(n):
        nxt = products(i + 1) if i + 1 < n else None
        finish(i, *cur)
        cur = nxt
    x = x_ref[...]
    hd = hid[...]
    x1, y1 = at_x(s_ref), at_y(s_ref)
    block_rows = 3 * F // 4
    segments = owned_rows(F) if split else []

    def put(lo, grad):
        if not split:
            refs[0][lo : lo + grad.shape[0], :] = grad.astype(refs[0].dtype)
            return
        grad = grad + refs[0][lo : lo + grad.shape[0], :].astype(jnp.float32)
        for a, b, to in segments:
            a, b, to = max(lo, a), min(lo + grad.shape[0], b), to + max(lo - a, 0)
            if a < b:
                block, row = divmod(to, block_rows)
                slot = jnp.where((x1 if block < 2 else y1) == block % 2, 0, 1)
                part = grad[a - lo : b - lo].astype(jnp.bfloat16)
                refs[1 + block // 2][slot, row : row + b - a, :] = part

    for j in range(2 * F // tn):
        put(j * tn, mm(gu[:, j * tn : (j + 1) * tn], x, TN))
    for j in range(F // HD):
        put(2 * F + j * HD, mm(og[:, j * HD : (j + 1) * HD], hd, TN))
    if split:
        for o in range(2):
            refs[3 + 2 * o][...] = refs[1 + o][0]
            refs[4 + 2 * o][...] = refs[1 + o][1]


def gradients(position, head, fk, fv, rates_t, w1, w3, w2, received=None):
    rows = fk.shape[0]
    F = w1.shape[1]
    tm = min(256, rows)
    tn = 256 if 2 * F % 256 == 0 else HD
    col = pl.BlockSpec((rows, F), lambda i, s: (0, head(s)))
    weight = pl.BlockSpec((1, F, F), lambda i, s: (head(s), 0, 0))
    whole = lambda *shape: pl.BlockSpec(shape, lambda i, s: (0,) * len(shape))
    bf = jnp.bfloat16
    args = [position, fk, fv, rates_t, w1, w3, w2]
    specs = [col, col, whole(*rates_t.shape), weight, weight, weight]
    scratch = [
        pltpu.VMEM((F, 2 * F), bf),
        pltpu.VMEM((F, F), bf),
        pltpu.VMEM((rows, 2 * F), bf),
        pltpu.VMEM((rows, F), bf),
        pltpu.VMEM((rows, F), bf),
    ]
    if received is None:
        shapes = [(3 * F, F)]
    else:
        shapes = [(3 * F // 4, F)] * 4
        args.append(received)
        specs.append(whole(3 * F, F))
        scratch = [pltpu.VMEM((2, 3 * F // 4, F), bf)] * 2 + scratch
    kernel = functools.partial(grad_kernel, head=head, tm=tm, tn=tn, split=received is not None)

    def body(*refs):
        if received is None:
            return kernel(*refs)
        ins, outs, halves, rest = refs[:8], refs[8:12], refs[12:14], refs[14:]
        return kernel(*ins, *halves, *outs, *rest)

    return pl.pallas_call(
        body,
        grid_spec=pltpu.PrefetchScalarGridSpec(
            num_scalar_prefetch=1,
            grid=(1,),
            in_specs=specs,
            out_specs=[whole(*shape) for shape in shapes],
            scratch_shapes=scratch,
        ),
        out_shape=[jax.ShapeDtypeStruct(shape, bf) for shape in shapes],
        cost_estimate=pl.CostEstimate(
            flops=12 * rows * F * F, bytes_accessed=rows * F * 4 + F * F * 18, transcendentals=rows * F
        ),
        name="grads",
        compiler_params=room(40),
    )(*args)


def turn_kernel(s_ref, w1, w3, w2, o_ref, *scratch, parts):
    F = w1.shape[2]
    all_ref = scratch[0] if scratch else o_ref
    all_ref[:F, :] = w1[0].T
    all_ref[F : 2 * F, :] = w3[0].T
    all_ref[2 * F :, :] = w2[0].T
    at = 0
    for n, start in parts:
        o_ref[at : at + n, :] = all_ref[pl.ds(pl.multiple_of(start(s_ref), 8), n), :]
        at += n


def turned(position, head, w1, w3, w2, parts=()):
    F = w1.shape[1]
    weight = pl.BlockSpec((1, F, F), lambda i, s: (head(s), 0, 0))
    shape = (sum(n for n, _ in parts), F) if parts else (3 * F, F)
    return pl.pallas_call(
        functools.partial(turn_kernel, parts=parts),
        grid_spec=pltpu.PrefetchScalarGridSpec(
            num_scalar_prefetch=1,
            grid=(1,),
            in_specs=[weight] * 3,
            out_specs=pl.BlockSpec(shape, lambda i, s: (0, 0)),
            scratch_shapes=[pltpu.VMEM((3 * F, F), jnp.float32)] if parts else [],
        ),
        out_shape=jax.ShapeDtypeStruct(shape, jnp.float32),
        cost_estimate=pl.CostEstimate(flops=3 * F * F, bytes_accessed=24 * F * F, transcendentals=0),
        name="turned",
        compiler_params=room(20),
    )(position, w1, w3, w2)


def renormed(old, grad):
    new = old - grad
    old_sq = jnp.sum(old * old, axis=-1, keepdims=True)
    new_sq = jnp.sum(new * new, axis=-1, keepdims=True)
    return (new * (jnp.sqrt(old_sq) / jnp.sqrt(new_sq + EPS))).astype(jnp.bfloat16)


def renorm_kernel(s_ref, old_ref, *refs):
    out = refs[-1]
    at = 0
    for i in range(2):
        a, b, c = (ref[...].astype(jnp.float32) for ref in refs[3 * i : 3 * i + 3])
        rows = slice(at, at + a.shape[0])
        out[rows, :] = renormed(old_ref[rows, :], a + b + c)
        at += a.shape[0]


def renorm_units(position, old, upper, lower):
    rows, F = old.shape
    specs = [pl.BlockSpec((rows, F), lambda i, s: (0, 0))]
    for group in (upper, lower):
        size = group[2][0].shape[0]
        specs += [pl.BlockSpec((size, F), lambda i, s, at=at: (at(s), 0)) for _, at in group]
    return pl.pallas_call(
        renorm_kernel,
        grid_spec=pltpu.PrefetchScalarGridSpec(
            num_scalar_prefetch=1,
            grid=(1,),
            in_specs=specs,
            out_specs=pl.BlockSpec((rows, F), lambda i, s: (0, 0)),
        ),
        out_shape=jax.ShapeDtypeStruct((rows, F), jnp.bfloat16),
        cost_estimate=pl.CostEstimate(flops=10 * rows * F, bytes_accessed=12 * rows * F, transcendentals=0),
        name="renorm",
        compiler_params=room(12),
    )(position, old, *[array for array, _ in upper + lower])


def merge_kernel(s_ref, own_ref, far_ref, own_log, far_log, o_ref, *, stride):
    lane = lax.broadcasted_iota(jnp.int32, own_log.shape, 1)
    heads = o_ref.shape[1] // HD
    for j in range(heads):
        cs = slice(j * HD, (j + 1) * HD)
        at = pl.program_id(0) * heads + j
        pick = lambda ref, of: jnp.sum(
            jnp.where(of, ref[...].astype(jnp.float32), 0.0), axis=1, keepdims=True
        )
        own = pick(own_log, lane == at)
        far = pick(far_log, (lane == at) | (lane == at + stride) | (lane == at + 2 * stride))
        far = jnp.where(s_ref[0] == 0, -jnp.inf, far)
        top = jnp.maximum(own, far)
        own, far = jnp.exp2(own - top), jnp.exp2(far - top)
        share = own / (own + far)
        a, b = own_ref[:, cs].astype(jnp.float32), far_ref[:, cs].astype(jnp.float32)
        o_ref[:, cs] = (a * share + b * (1.0 - share)).astype(o_ref.dtype)


def merged(position, own, far, own_log, width):
    rows, cols = own.shape
    w = width * HD
    col = pl.BlockSpec((rows, w), lambda g, s: (0, g))
    log = lambda at: pl.BlockSpec((rows, HD), lambda g, s: (0, at))
    return pl.pallas_call(
        functools.partial(merge_kernel, stride=log_stride_of(cols)),
        grid_spec=pltpu.PrefetchScalarGridSpec(
            num_scalar_prefetch=1,
            grid=(cols // w,),
            in_specs=[col, col, log(0), log(cols // HD)],
            out_specs=col,
        ),
        out_shape=jax.ShapeDtypeStruct((rows, cols), jnp.bfloat16),
        cost_estimate=pl.CostEstimate(
            flops=8 * rows * cols, bytes_accessed=6 * rows * cols, transcendentals=rows * cols // HD
        ),
        name="merge",
        compiler_params=room(8),
    )(position, own, far, own_log, far)


def gated(h, n):
    g = h[:, :n]
    return (g * jax.nn.sigmoid(g) * h[:, n:]).astype(jnp.bfloat16)


def staggered(n, first, second):
    cur = first(0)
    for i in range(n):
        nxt = first(i + 1) if i + 1 < n else None
        second(i, cur)
        cur = nxt


def put_quarter(s_ref, ref, rows, values, flip_x, flip_y):
    n = ref.shape[1] // 4
    chip = 2 * (at_x(s_ref) ^ flip_x) + (at_y(s_ref) ^ flip_y)
    for k in range(4):

        @pl.when(chip == k)
        def _():
            ref[rows, k * n : (k + 1) * n] = values


def hidden_kernel(s_ref, q_ref, own_ref, over_x, over_y, o_ref, w_ref, v_ref, *, tm):
    F = q_ref.shape[1]
    n = F // 4

    @pl.when(pl.program_id(0) == 0)
    def _():
        for i, ref in enumerate((own_ref, over_x, over_y)):
            w_ref[i * n : (i + 1) * n, :] = ref[:n, :]
            w_ref[(3 + i) * n : (4 + i) * n, :] = ref[n : 2 * n, :]

    def first(i):
        return mm(q_ref[i * tm : (i + 1) * tm, :], w_ref[...], NT)

    def second(i, h):
        v_ref[i * tm : (i + 1) * tm, : 3 * n] = gated(h, 3 * n)

    staggered(q_ref.shape[0] // tm, first, second)
    every = slice(0, q_ref.shape[0])
    for i, flips in enumerate(((0, 0), (1, 0), (0, 1))):
        put_quarter(s_ref, o_ref, every, v_ref[:, i * n : (i + 1) * n], *flips)


def hidden_part(position, head, fq, pieces):
    rows = fq.shape[0]
    F = pieces[0].shape[1]
    half = rows // 2
    whole = pl.BlockSpec(pieces[0].shape, lambda i, s: (0, 0))
    bf = jnp.bfloat16
    return pl.pallas_call(
        functools.partial(hidden_kernel, tm=min(256, half)),
        grid_spec=pltpu.PrefetchScalarGridSpec(
            num_scalar_prefetch=1,
            grid=(2,),
            in_specs=[pl.BlockSpec((half, F), lambda i, s: (i, head(s)))] + [whole] * 3,
            out_specs=pl.BlockSpec((half, F), lambda i, s: (i, 0)),
            scratch_shapes=[pltpu.VMEM((3 * F // 2, F), bf), pltpu.VMEM((half, F), bf)],
        ),
        out_shape=jax.ShapeDtypeStruct((rows, F), bf),
        cost_estimate=pl.CostEstimate(
            flops=3 * rows * F * F, bytes_accessed=rows * F * 4 + F * F * 3, transcendentals=rows * F
        ),
        name="hidden",
        compiler_params=room(14),
    )(position, fq, *pieces[:3])


def apply_kernel(s_ref, q_ref, high_ref, low_ref, *rest, tm, split):
    n_ref, w_ref, h_ref, a_ref = rest[-4:]
    o_ref = rest[-5]
    F = q_ref.shape[1]
    n, m = F // 4, F // 8
    step = pl.program_id(0)

    @pl.when(step == 0)
    def _():
        if split:
            own, over_x, over_y, upper, lower = rest[1:6]
            for ref, row, flips in (
                (own, 2 * n, (0, 0)),
                (over_x, 2 * n, (1, 0)),
                (over_y, 2 * n, (0, 1)),
                (lower, m, (1, 1)),
            ):
                to = pl.multiple_of(quarter(F, *flips)(s_ref), 16)
                n_ref[pl.ds(to, n), :] = ref[row : row + n, :]
            w_ref[: n + m, :] = upper[...]
            w_ref[n + m :, :] = lower[:m, :]
        else:
            w_ref[...] = rest[0][: 2 * F, :]
            n_ref[...] = rest[0][2 * F :, :]
        a_ref[...] = low_ref[...]

    @pl.when(step == 1)
    def _():
        a_ref[...] = high_ref[...]

    def first(i):
        return mm(q_ref[i * tm : (i + 1) * tm, :], w_ref[...], NT)

    def second(i, h):
        r = slice(i * tm, (i + 1) * tm)
        if split:
            h_ref[r, :] = rest[0][r, :]
            put_quarter(s_ref, h_ref, r, gated(h, n), 1, 1)
            hid = h_ref[r, :]
        else:
            hid = gated(h, F)
        o_ref[r, :] = (a_ref[r, :].astype(jnp.float32) + mm(hid, n_ref[...], NT)).astype(o_ref.dtype)

    staggered(q_ref.shape[0] // tm, first, second)


def apply_head(position, head, fq, hidden, pieces, high, low, into=None):
    rows, cols = fq.shape
    F = pieces[0].shape[1]
    half = rows // 2
    split = hidden is not None
    col = pl.BlockSpec((half, F), lambda i, s: (i, head(s)))
    part = pl.BlockSpec((half, F), lambda i, s: (0, head(s)))
    whole = lambda a: pl.BlockSpec(a.shape, lambda i, s: (0, 0))
    args = [position, fq, high, low]
    specs = [col, part, part]
    if split:
        args.append(hidden)
        specs.append(pl.BlockSpec((half, F), lambda i, s: (i, 0)))
    args += pieces
    specs += [whole(p) for p in pieces]
    aliases = {}
    if into is not None:
        aliases = {len(args): 0}
        args.append(into)
        specs.append(pl.BlockSpec(memory_space=pl.ANY))
    bf = jnp.bfloat16
    return pl.pallas_call(
        functools.partial(apply_kernel, tm=min(256, half), split=split),
        grid_spec=pltpu.PrefetchScalarGridSpec(
            num_scalar_prefetch=1,
            grid=(2,),
            in_specs=specs,
            out_specs=col,
            scratch_shapes=[
                pltpu.VMEM((F, F), bf),
                pltpu.VMEM((F // 2 if split else 2 * F, F), bf),
                pltpu.VMEM((half, F), bf),
                pltpu.VMEM((half, F), bf),
            ],
        ),
        out_shape=jax.ShapeDtypeStruct((rows, cols), bf),
        input_output_aliases=aliases,
        cost_estimate=pl.CostEstimate(
            flops=3 * rows * F * F, bytes_accessed=rows * F * 8 + F * F * 6, transcendentals=rows * F
        ),
        name="apply",
        compiler_params=room(14),
    )(*args)


def exchange(block, bit):
    size = lax.axis_size("seq")
    return lax.ppermute(block, "seq", [(i, i ^ (1 << bit)) for i in range(size)])


def shifted(block, by):
    size = lax.axis_size("seq")
    return lax.ppermute(block, "seq", [(i, i + by) for i in range(size) if 0 <= i + by < size])


def synced(total, old, bits, position):
    offset = 0
    for bit in bits:
        half = total.shape[0] // 2
        mine = (position >> bit) & 1
        away = lax.dynamic_slice_in_dim(total, (1 - mine) * half, half, 0).astype(jnp.bfloat16)
        kept = lax.dynamic_slice_in_dim(total, mine * half, half, 0)
        total = kept + exchange(away, bit).astype(jnp.float32)
        offset = offset + mine * half
    part = renormed(lax.dynamic_slice_in_dim(old, offset, total.shape[0], 0), total)
    for bit in reversed(bits):
        mine = (position >> bit) & 1
        other = exchange(part, bit)
        part = jnp.concatenate(
            [jnp.where(mine == 0, part, other), jnp.where(mine == 0, other, part)], axis=0
        )
    return part


def synced_square(position, blocks, old):
    x, y = (position[0] >> 1) & 1, (position[0] >> 2) & 1
    keep_x, send_x, keep_y, send_y = blocks
    top0, bottom0 = exchange(send_x, 1), exchange(send_y, 2)

    def fold(a, b, at):
        n = a.shape[0] // 2
        a, b = (lax.dynamic_slice_in_dim(v, at * n, n, 0).astype(jnp.float32) for v in (a, b))
        return (a + b).astype(jnp.bfloat16)

    top1 = exchange(fold(keep_x, top0, 1 - y), 2)
    bottom1 = exchange(fold(keep_y, bottom0, 1 - x), 1)
    zero = lambda s: 0
    part = renorm_units(
        position,
        old,
        [(keep_x, at_y), (top0, at_y), (top1, zero)],
        [(keep_y, at_x), (bottom0, at_x), (bottom1, zero)],
    )
    n = top1.shape[0]
    over_x, over_y = exchange(part, 1), exchange(part, 2)
    top2, bottom2 = exchange(over_y[:n], 1), exchange(over_x[n:], 2)
    return [part, over_x, over_y, top2, bottom2]


def quarter(F, flip_x=0, flip_y=0):
    return lambda s: (2 * (at_x(s) ^ flip_x) + (at_y(s) ^ flip_y)) * (F // 4)


def shards(attn_q, attn_k, attn_v, fast_q, fast_k, fast_v, rates, fast_gate, fast_up, fast_down):
    position = lax.axis_index("seq").astype(jnp.int32).reshape(1)
    count = lax.axis_size("seq")
    heads = fast_gate.shape[0]
    rows = attn_q.shape[0]
    half = rows // 2
    width = 2 if attn_q.shape[1] // HD % 2 == 0 else 1
    prev = shifted(jnp.concatenate([attn_k[half:], attn_v[half:]], axis=0), 1)
    guests = shifted(attn_q[:half], -1)
    rates_t = rates.T
    weights = (fast_gate, fast_up, fast_down)

    def grads(head, received=None):
        return gradients(position, head, fast_k, fast_v, rates_t, *weights, received)

    if heads == 2 and count == 8:
        near, far = (lambda s: s[0] & 1), (lambda s: 1 - (s[0] & 1))
        received = exchange(grads(far)[0], 0)
        F = fast_gate.shape[1]
        mine = quarter(F)
        starts = [(F // 4, lambda s, at=i * F: at + mine(s)) for i in range(3)]
        old = turned(position, near, *weights, parts=tuple(starts))
        blocks = grads(near, received)
        pieces = synced_square(position, blocks, old)
        other = [exchange(p, 0) for p in pieces]
        news = []
        for head, new in ((near, pieces), (far, other)):
            news.append((head, hidden_part(position, head, fast_q, new), new))
    else:
        news = []
        bits = list(range(count.bit_length() - 1))
        for h in range(heads):
            head = lambda s, h=h: h
            old = turned(position, head, *weights)
            new = synced(grads(head)[0].astype(jnp.float32), old, bits, position[0])
            news.append((head, None, [new]))
    bq = min(256, half)
    tiles = half // bq
    late = [
        [(0, t * bq, half, 1), (1, 0, half + (t + 1) * bq, -1)] for t in range(tiles)
    ]
    early = [[(0, 0, (t + 1) * bq, -1)] for t in range(tiles)]
    guest = [[(0, t * bq, rows, 1)] for t in range(tiles)]
    here = (attn_k, 0, attn_v, 0, rows)
    returned, own_out, own_log = attention(position, [(guests, 0, guest, 2), (attn_q, 0, early, 1)], [here], bq, width)
    far_out = shifted(returned, 1)
    (high,) = attention(position, [(attn_q, 1, late, 0)], [(prev, 0, prev, 1, half), here], bq, width)
    low = merged(position, own_out, far_out, own_log, width)
    mixed = None
    for head, hidden, new in news:
        mixed = apply_head(position, head, fast_q, hidden, new, high, low, mixed)
    return mixed


def solution(mesh):
    placed = (P("seq", "head"),) * 7 + (P("head", None, None),) * 3
    return jax.shard_map(shards, mesh=mesh, in_specs=placed, out_specs=P("seq", "head"), check_vma=False)
```

```python
import functools
import math

import jax
import jax.numpy as jnp
from jax import lax
from jax.experimental import pallas as pl
from jax.experimental.pallas import tpu as pltpu
from jax.sharding import PartitionSpec as P


HD = 128
EPS = 1e-06
NN = (((1,), (0,)), ((), ()))
NT = (((1,), (1,)), ((), ()))
TN = (((0,), (0,)), ((), ()))


def room(mib):
    return pltpu.CompilerParams(vmem_limit_bytes=mib << 20)


def mm(a, b, dims=NN):
    return lax.dot_general(a, b, dims, preferred_element_type=jnp.float32)


def attn_kernel(position_ref, *refs, bq, jobs, sources, log_stride):
    queries = refs[: len(jobs)]
    keys = refs[len(jobs) : len(jobs) + sources]
    values = refs[len(jobs) + sources : len(jobs) + 2 * sources]
    rest = list(refs[len(jobs) + 2 * sources :])
    outs = []
    for _, sums in jobs:
        outs.append((rest.pop(0), rest.pop(0) if sums == 1 else None))
    bufs = (rest.pop(0), rest.pop(0))
    logs = [rest.pop(0) if sums else None for _, sums in jobs]
    group = pl.program_id(0)
    heads = queries[0].shape[1] // HD
    c = math.log2(math.e) / math.sqrt(HD)
    ri = lax.broadcasted_iota(jnp.int32, (bq, bq), 0)
    ci = lax.broadcasted_iota(jnp.int32, (bq, bq), 1)
    absent = position_ref[0] == 0
    units = [(h, j, t) for h in range(heads) for j in range(len(jobs)) for t in range(len(jobs[j][0]))]

    def scores(i):
        h, j, t = units[i]
        hs = slice(h * HD, (h + 1) * HD)
        buf = bufs[i % 2]
        q = queries[j][t * bq : (t + 1) * bq, hs]
        tops = []
        at = 0
        for source, lo, hi, edge in jobs[j][0][t]:
            s = mm(q, keys[source][lo:hi, hs], NT)
            n = hi - lo
            if edge == 1:
                kept = jnp.where(ci >= ri, s[:, :bq], -jnp.inf)
                s = jnp.concatenate([kept, s[:, bq:]], axis=1) if n > bq else kept
            elif edge == -1:
                kept = jnp.where(ci <= ri, s[:, n - bq :], -jnp.inf)
                s = jnp.concatenate([s[:, : n - bq], kept], axis=1) if n > bq else kept
            buf[:, at : at + n] = s
            tops.append(jnp.max(s, axis=1, keepdims=True))
            at += n
        if len(tops) == 1:
            return [tops[0] * c]
        m = jnp.maximum(tops[1], jnp.where(absent, -jnp.inf, tops[0])) * c
        return [jnp.where(absent, 1e30, m), m]

    def finish(i, ms):
        h, j, t = units[i]
        plan, sums = jobs[j]
        hs = slice(h * HD, (h + 1) * HD)
        buf = bufs[i % 2]
        out = total = None
        at = 0
        for (source, lo, hi, _), m in zip(plan[t], ms):
            p = jnp.exp2(buf[:, at : at + hi - lo] * c - m)
            part = jnp.sum(p, axis=1, keepdims=True)
            o = mm(p.astype(jnp.bfloat16), values[source][lo:hi, hs])
            total = part if total is None else total + part
            out = o if out is None else out + o
            at += hi - lo
        rows = slice(t * bq, (t + 1) * bq)
        out = (out / total).astype(jnp.bfloat16)
        head = group * heads + h
        if sums == 2:
            outs[j][0][rows, pl.ds(pl.multiple_of(head * HD, HD), HD)] = out
        else:
            outs[j][0][rows, hs] = out
        if sums:
            lane = lax.broadcasted_iota(jnp.int32, (bq, HD), 1)
            log = ms[-1] + jnp.log(total) * math.log2(math.e)
            logs[j][rows, :] = jnp.where(lane == head, log, logs[j][rows, :])

    if any(sums for _, sums in jobs):

        @pl.when(group == 0)
        def _():
            for log in logs:
                if log is not None:
                    log[...] = jnp.zeros(log.shape, log.dtype)

    ms = scores(0)
    for i in range(len(units)):
        nxt = scores(i + 1) if i + 1 < len(units) else None
        finish(i, ms)
        ms = nxt
    if any(sums for _, sums in jobs):

        @pl.when(group == pl.num_programs(0) - 1)
        def _():
            for (_, sums), (out, log_out), log in zip(jobs, outs, logs):
                if sums == 1:
                    log_out[...] = log[...]
                if sums == 2:
                    x = log[...]
                    a = x.astype(jnp.bfloat16).astype(jnp.float32)
                    b = (x - a).astype(jnp.bfloat16).astype(jnp.float32)
                    x = a + pltpu.roll(b, log_stride, 1) + pltpu.roll(x - a - b, 2 * log_stride, 1)
                    out[:, out.shape[1] - HD :] = x.astype(jnp.bfloat16)


def log_stride_of(cols):
    return 16 * pl.cdiv(cols // HD, 16)


def attention(position, jobs, sources, bq, width):
    cols = jobs[0][0].shape[1]
    w = width * HD
    ranges = [r for _, _, plan, _ in jobs for tile in plan for r in tile]
    span = max(sum(hi - lo for _, lo, hi, _ in tile) for _, _, plan, _ in jobs for tile in plan)
    pairs = bq * sum(hi - lo for _, lo, hi, _ in ranges) * cols // HD
    block = lambda n, at: pl.BlockSpec((n, w), lambda g, f: (at, g))
    whole = lambda *shape: pl.BlockSpec(shape, lambda g, f: (0, 0))
    outs, out_specs, logs = [], [], []
    for _, _, plan, sums in jobs:
        rows = len(plan) * bq
        if sums == 2:
            outs.append(jax.ShapeDtypeStruct((rows, cols + HD), jnp.bfloat16))
            out_specs.append(whole(rows, cols + HD))
        else:
            outs.append(jax.ShapeDtypeStruct((rows, cols), jnp.bfloat16))
            out_specs.append(block(rows, 0))
        if sums == 1:
            outs.append(jax.ShapeDtypeStruct((rows, HD), jnp.float32))
            out_specs.append(whole(rows, HD))
        if sums:
            logs.append(pltpu.VMEM((rows, HD), jnp.float32))
    specs = [block(len(plan) * bq, at) for _, at, plan, _ in jobs]
    specs += [block(n, at) for _, at, _, _, n in sources] + [block(n, at) for _, _, _, at, n in sources]
    kernel = functools.partial(
        attn_kernel,
        bq=bq,
        jobs=[(plan, sums) for _, _, plan, sums in jobs],
        sources=len(sources),
        log_stride=log_stride_of(cols),
    )
    return pl.pallas_call(
        kernel,
        grid_spec=pltpu.PrefetchScalarGridSpec(
            num_scalar_prefetch=1,
            grid=(cols // w,),
            in_specs=specs,
            out_specs=out_specs,
            scratch_shapes=[pltpu.VMEM((bq, span), jnp.float32)] * 2 + logs,
        ),
        out_shape=outs,
        cost_estimate=pl.CostEstimate(
            flops=4 * pairs * HD, bytes_accessed=8 * bq * cols * len(ranges), transcendentals=pairs
        ),
        compiler_params=room(14),
    )(position, *[job[0] for job in jobs], *[x[0] for x in sources], *[x[2] for x in sources])


def owned_rows(F):
    n, m, half = F // 4, F // 8, 3 * F // 2
    unit = 3 * F // 8
    segments = []
    for k in range(4):
        upper, lower = k * unit, half + (2 * (k % 2) + k // 2) * unit
        segments += [
            (k * n, (k + 1) * n, upper),
            (F + k * n, F + k * n + m, upper + n),
            (F + k * n + m, F + (k + 1) * n, lower),
            (2 * F + k * n, 2 * F + (k + 1) * n, lower + m),
        ]
    return segments


def at_x(s):
    return (s[0] >> 1) & 1


def at_y(s):
    return (s[0] >> 2) & 1


def grad_kernel(s_ref, x_ref, v_ref, r_ref, w1_ref, w3_ref, w2_ref, *refs, head, tm, tn, split):
    w13, w2, gu, hid, og = refs[-5:]
    F = w1_ref.shape[2]
    rows = x_ref.shape[0]
    w13[:, :F] = w1_ref[0].astype(jnp.bfloat16)
    w13[:, F:] = w3_ref[0].astype(jnp.bfloat16)
    w2[...] = w2_ref[0].astype(jnp.bfloat16)
    pick = lax.broadcasted_iota(jnp.int32, r_ref.shape, 0) == head(s_ref)
    rate = jnp.sum(jnp.where(pick, r_ref[...], 0.0), axis=0, keepdims=True)
    rate = jnp.transpose(jnp.broadcast_to(rate, (8, rows)))[:, :1]
    og[...] = (-rate * v_ref[...].astype(jnp.float32)).astype(jnp.bfloat16)
    n = rows // tm

    def products(i):
        r = slice(i * tm, (i + 1) * tm)
        return mm(x_ref[r, :], w13[...]), mm(og[r, :], w2[...], NT)

    def finish(i, pre, hg):
        r = slice(i * tm, (i + 1) * tm)
        pg, pu = pre[:, :F], pre[:, F:]
        sg = jax.nn.sigmoid(pg)
        act = pg * sg
        gu[r, :F] = (hg * pu * (sg * (1.0 + pg * (1.0 - sg)))).astype(jnp.bfloat16)
        gu[r, F:] = (hg * act).astype(jnp.bfloat16)
        hid[r, :] = (act * pu).astype(jnp.bfloat16)

    cur = products(0)
    for i in range(n):
        nxt = products(i + 1) if i + 1 < n else None
        finish(i, *cur)
        cur = nxt
    x = x_ref[...]
    hd = hid[...]
    x1, y1 = at_x(s_ref), at_y(s_ref)
    block_rows = 3 * F // 4
    segments = owned_rows(F) if split else []

    def put(lo, grad):
        if not split:
            refs[0][lo : lo + grad.shape[0], :] = grad.astype(refs[0].dtype)
            return
        grad = grad + refs[0][lo : lo + grad.shape[0], :].astype(jnp.float32)
        for a, b, to in segments:
            a, b, to = max(lo, a), min(lo + grad.shape[0], b), to + max(lo - a, 0)
            if a < b:
                block, row = divmod(to, block_rows)
                slot = jnp.where((x1 if block < 2 else y1) == block % 2, 0, 1)
                part = grad[a - lo : b - lo].astype(jnp.bfloat16)
                refs[1 + block // 2][slot, row : row + b - a, :] = part

    for j in range(2 * F // tn):
        put(j * tn, mm(gu[:, j * tn : (j + 1) * tn], x, TN))
    for j in range(F // HD):
        put(2 * F + j * HD, mm(og[:, j * HD : (j + 1) * HD], hd, TN))
    if split:
        for o in range(2):
            refs[3 + 2 * o][...] = refs[1 + o][0]
            refs[4 + 2 * o][...] = refs[1 + o][1]


def gradients(position, head, fk, fv, rates_t, w1, w3, w2, received=None):
    rows = fk.shape[0]
    F = w1.shape[1]
    tm = min(256, rows)
    tn = 256 if 2 * F % 256 == 0 else HD
    once = dict(pipeline_mode=pl.Buffered(1))
    col = pl.BlockSpec((rows, F), lambda i, s: (0, head(s)), **once)
    weight = pl.BlockSpec((1, F, F), lambda i, s: (head(s), 0, 0), **once)
    whole = lambda *shape: pl.BlockSpec(shape, lambda i, s: (0,) * len(shape), **once)
    bf = jnp.bfloat16
    args = [position, fk, fv, rates_t, w1, w3, w2]
    specs = [col, col, whole(*rates_t.shape), weight, weight, weight]
    scratch = [
        pltpu.VMEM((F, 2 * F), bf),
        pltpu.VMEM((F, F), bf),
        pltpu.VMEM((rows, 2 * F), bf),
        pltpu.VMEM((rows, F), bf),
        pltpu.VMEM((rows, F), bf),
    ]
    if received is None:
        shapes = [(3 * F, F)]
    else:
        shapes = [(3 * F // 4, F)] * 4
        args.append(received)
        specs.append(whole(3 * F, F))
        scratch = [pltpu.VMEM((2, 3 * F // 4, F), bf)] * 2 + scratch
    kernel = functools.partial(grad_kernel, head=head, tm=tm, tn=tn, split=received is not None)

    def body(*refs):
        if received is None:
            return kernel(*refs)
        ins, outs, halves, rest = refs[:8], refs[8:12], refs[12:14], refs[14:]
        return kernel(*ins, *halves, *outs, *rest)

    return pl.pallas_call(
        body,
        grid_spec=pltpu.PrefetchScalarGridSpec(
            num_scalar_prefetch=1,
            grid=(1,),
            in_specs=specs,
            out_specs=[whole(*shape) for shape in shapes],
            scratch_shapes=scratch,
        ),
        out_shape=[jax.ShapeDtypeStruct(shape, bf) for shape in shapes],
        cost_estimate=pl.CostEstimate(
            flops=12 * rows * F * F, bytes_accessed=rows * F * 4 + F * F * 18, transcendentals=rows * F
        ),
        name="grads",
        compiler_params=room(40 if received is None else 36),
    )(*args)


def turn_kernel(s_ref, w1, w3, w2, o_ref, *scratch, parts):
    F = w1.shape[2]
    all_ref = scratch[0] if scratch else o_ref
    all_ref[:F, :] = w1[0].T
    all_ref[F : 2 * F, :] = w3[0].T
    all_ref[2 * F :, :] = w2[0].T
    at = 0
    for n, start in parts:
        o_ref[at : at + n, :] = all_ref[pl.ds(pl.multiple_of(start(s_ref), 8), n), :]
        at += n


def turned(position, head, w1, w3, w2, parts=()):
    F = w1.shape[1]
    weight = pl.BlockSpec((1, F, F), lambda i, s: (head(s), 0, 0))
    shape = (sum(n for n, _ in parts), F) if parts else (3 * F, F)
    return pl.pallas_call(
        functools.partial(turn_kernel, parts=parts),
        grid_spec=pltpu.PrefetchScalarGridSpec(
            num_scalar_prefetch=1,
            grid=(1,),
            in_specs=[weight] * 3,
            out_specs=pl.BlockSpec(shape, lambda i, s: (0, 0)),
            scratch_shapes=[pltpu.VMEM((3 * F, F), jnp.float32)] if parts else [],
        ),
        out_shape=jax.ShapeDtypeStruct(shape, jnp.float32),
        cost_estimate=pl.CostEstimate(flops=3 * F * F, bytes_accessed=24 * F * F, transcendentals=0),
        name="turned",
        compiler_params=room(20),
    )(position, w1, w3, w2)


def renormed(old, grad):
    new = old - grad
    old_sq = jnp.sum(old * old, axis=-1, keepdims=True)
    new_sq = jnp.sum(new * new, axis=-1, keepdims=True)
    return (new * (jnp.sqrt(old_sq) / jnp.sqrt(new_sq + EPS))).astype(jnp.bfloat16)


def renorm_kernel(s_ref, old_ref, *refs):
    out = refs[-1]
    at = 0
    for i in range(2):
        a, b, c = (ref[...].astype(jnp.float32) for ref in refs[3 * i : 3 * i + 3])
        rows = slice(at, at + a.shape[0])
        out[rows, :] = renormed(old_ref[rows, :], a + b + c)
        at += a.shape[0]


def renorm_units(position, old, upper, lower):
    rows, F = old.shape
    specs = [pl.BlockSpec((rows, F), lambda i, s: (0, 0))]
    for group in (upper, lower):
        size = group[2][0].shape[0]
        specs += [pl.BlockSpec((size, F), lambda i, s, at=at: (at(s), 0)) for _, at in group]
    return pl.pallas_call(
        renorm_kernel,
        grid_spec=pltpu.PrefetchScalarGridSpec(
            num_scalar_prefetch=1,
            grid=(1,),
            in_specs=specs,
            out_specs=pl.BlockSpec((rows, F), lambda i, s: (0, 0)),
        ),
        out_shape=jax.ShapeDtypeStruct((rows, F), jnp.bfloat16),
        cost_estimate=pl.CostEstimate(flops=10 * rows * F, bytes_accessed=12 * rows * F, transcendentals=0),
        name="renorm",
        compiler_params=room(12),
    )(position, old, *[array for array, _ in upper + lower])


def merge_kernel(s_ref, own_ref, far_ref, own_log, far_log, o_ref, *, stride):
    lane = lax.broadcasted_iota(jnp.int32, own_log.shape, 1)
    heads = o_ref.shape[1] // HD
    for j in range(heads):
        cs = slice(j * HD, (j + 1) * HD)
        at = pl.program_id(0) * heads + j
        pick = lambda ref, of: jnp.sum(
            jnp.where(of, ref[...].astype(jnp.float32), 0.0), axis=1, keepdims=True
        )
        own = pick(own_log, lane == at)
        far = pick(far_log, (lane == at) | (lane == at + stride) | (lane == at + 2 * stride))
        far = jnp.where(s_ref[0] == 0, -jnp.inf, far)
        top = jnp.maximum(own, far)
        own, far = jnp.exp2(own - top), jnp.exp2(far - top)
        share = own / (own + far)
        a, b = own_ref[:, cs].astype(jnp.float32), far_ref[:, cs].astype(jnp.float32)
        o_ref[:, cs] = (a * share + b * (1.0 - share)).astype(o_ref.dtype)


def merged(position, own, far, own_log, width):
    rows, cols = own.shape
    w = width * HD
    col = pl.BlockSpec((rows, w), lambda g, s: (0, g))
    log = lambda at: pl.BlockSpec((rows, HD), lambda g, s: (0, at))
    return pl.pallas_call(
        functools.partial(merge_kernel, stride=log_stride_of(cols)),
        grid_spec=pltpu.PrefetchScalarGridSpec(
            num_scalar_prefetch=1,
            grid=(cols // w,),
            in_specs=[col, col, log(0), log(cols // HD)],
            out_specs=col,
        ),
        out_shape=jax.ShapeDtypeStruct((rows, cols), jnp.bfloat16),
        cost_estimate=pl.CostEstimate(
            flops=8 * rows * cols, bytes_accessed=6 * rows * cols, transcendentals=rows * cols // HD
        ),
        name="merge",
        compiler_params=room(8),
    )(position, own, far, own_log, far)


def gated(h, n):
    g = h[:, :n]
    return (g * jax.nn.sigmoid(g) * h[:, n:]).astype(jnp.bfloat16)


def staggered(n, first, second):
    cur = first(0)
    for i in range(n):
        nxt = first(i + 1) if i + 1 < n else None
        second(i, cur)
        cur = nxt


def put_quarter(s_ref, ref, rows, values, flip_x, flip_y):
    n = ref.shape[1] // 4
    chip = 2 * (at_x(s_ref) ^ flip_x) + (at_y(s_ref) ^ flip_y)
    for k in range(4):

        @pl.when(chip == k)
        def _():
            ref[rows, k * n : (k + 1) * n] = values


def hidden_kernel(s_ref, q_ref, own_ref, over_x, over_y, o_ref, w_ref, v_ref, *, tm):
    F = q_ref.shape[1]
    n = F // 4

    @pl.when(pl.program_id(0) == 0)
    def _():
        for i, ref in enumerate((own_ref, over_x, over_y)):
            w_ref[i * n : (i + 1) * n, :] = ref[:n, :]
            w_ref[(3 + i) * n : (4 + i) * n, :] = ref[n : 2 * n, :]

    def first(i):
        return mm(q_ref[i * tm : (i + 1) * tm, :], w_ref[...], NT)

    def second(i, h):
        v_ref[i * tm : (i + 1) * tm, : 3 * n] = gated(h, 3 * n)

    staggered(q_ref.shape[0] // tm, first, second)
    every = slice(0, q_ref.shape[0])
    for i, flips in enumerate(((0, 0), (1, 0), (0, 1))):
        put_quarter(s_ref, o_ref, every, v_ref[:, i * n : (i + 1) * n], *flips)


def hidden_part(position, head, fq, pieces):
    rows = fq.shape[0]
    F = pieces[0].shape[1]
    half = rows // 2
    whole = pl.BlockSpec(pieces[0].shape, lambda i, s: (0, 0))
    bf = jnp.bfloat16
    return pl.pallas_call(
        functools.partial(hidden_kernel, tm=min(256, half)),
        grid_spec=pltpu.PrefetchScalarGridSpec(
            num_scalar_prefetch=1,
            grid=(2,),
            in_specs=[pl.BlockSpec((half, F), lambda i, s: (i, head(s)))] + [whole] * 3,
            out_specs=pl.BlockSpec((half, F), lambda i, s: (i, 0)),
            scratch_shapes=[pltpu.VMEM((3 * F // 2, F), bf), pltpu.VMEM((half, F), bf)],
        ),
        out_shape=jax.ShapeDtypeStruct((rows, F), bf),
        cost_estimate=pl.CostEstimate(
            flops=3 * rows * F * F, bytes_accessed=rows * F * 4 + F * F * 3, transcendentals=rows * F
        ),
        name="hidden",
        compiler_params=room(14),
    )(position, fq, *pieces[:3])


def apply_kernel(s_ref, q_ref, high_ref, low_ref, *rest, tm, split):
    n_ref, w_ref, h_ref, a_ref = rest[-4:]
    o_ref = rest[-5]
    F = q_ref.shape[1]
    n, m = F // 4, F // 8
    step = pl.program_id(0)

    @pl.when(step == 0)
    def _():
        if split:
            own, over_x, over_y, upper, lower = rest[1:6]
            for ref, row, flips in (
                (own, 2 * n, (0, 0)),
                (over_x, 2 * n, (1, 0)),
                (over_y, 2 * n, (0, 1)),
                (lower, m, (1, 1)),
            ):
                to = pl.multiple_of(quarter(F, *flips)(s_ref), 16)
                n_ref[pl.ds(to, n), :] = ref[row : row + n, :]
            w_ref[: n + m, :] = upper[...]
            w_ref[n + m :, :] = lower[:m, :]
        else:
            w_ref[...] = rest[0][: 2 * F, :]
            n_ref[...] = rest[0][2 * F :, :]
        a_ref[...] = low_ref[...]

    @pl.when(step == 1)
    def _():
        a_ref[...] = high_ref[...]

    def first(i):
        return mm(q_ref[i * tm : (i + 1) * tm, :], w_ref[...], NT)

    def second(i, h):
        r = slice(i * tm, (i + 1) * tm)
        if split:
            h_ref[r, :] = rest[0][r, :]
            put_quarter(s_ref, h_ref, r, gated(h, n), 1, 1)
            hid = h_ref[r, :]
        else:
            hid = gated(h, F)
        o_ref[r, :] = (a_ref[r, :].astype(jnp.float32) + mm(hid, n_ref[...], NT)).astype(o_ref.dtype)

    staggered(q_ref.shape[0] // tm, first, second)


def apply_head(position, head, fq, hidden, pieces, high, low, into=None):
    rows, cols = fq.shape
    F = pieces[0].shape[1]
    half = rows // 2
    split = hidden is not None
    col = pl.BlockSpec((half, F), lambda i, s: (i, head(s)))
    part = pl.BlockSpec((half, F), lambda i, s: (0, head(s)))
    whole = lambda a: pl.BlockSpec(a.shape, lambda i, s: (0, 0))
    args = [position, fq, high, low]
    specs = [col, part, part]
    if split:
        args.append(hidden)
        specs.append(pl.BlockSpec((half, F), lambda i, s: (i, 0)))
    args += pieces
    specs += [whole(p) for p in pieces]
    aliases = {}
    if into is not None:
        aliases = {len(args): 0}
        args.append(into)
        specs.append(pl.BlockSpec(memory_space=pl.ANY))
    bf = jnp.bfloat16
    return pl.pallas_call(
        functools.partial(apply_kernel, tm=min(256, half), split=split),
        grid_spec=pltpu.PrefetchScalarGridSpec(
            num_scalar_prefetch=1,
            grid=(2,),
            in_specs=specs,
            out_specs=col,
            scratch_shapes=[
                pltpu.VMEM((F, F), bf),
                pltpu.VMEM((F // 2 if split else 2 * F, F), bf),
                pltpu.VMEM((half, F), bf),
                pltpu.VMEM((half, F), bf),
            ],
        ),
        out_shape=jax.ShapeDtypeStruct((rows, cols), bf),
        input_output_aliases=aliases,
        cost_estimate=pl.CostEstimate(
            flops=3 * rows * F * F, bytes_accessed=rows * F * 8 + F * F * 6, transcendentals=rows * F
        ),
        name="apply",
        compiler_params=room(14),
    )(*args)


def exchange(block, bit):
    size = lax.axis_size("seq")
    return lax.ppermute(block, "seq", [(i, i ^ (1 << bit)) for i in range(size)])


def shifted(block, by):
    size = lax.axis_size("seq")
    return lax.ppermute(block, "seq", [(i, i + by) for i in range(size) if 0 <= i + by < size])


def synced(total, old, bits, position):
    offset = 0
    for bit in bits:
        half = total.shape[0] // 2
        mine = (position >> bit) & 1
        away = lax.dynamic_slice_in_dim(total, (1 - mine) * half, half, 0).astype(jnp.bfloat16)
        kept = lax.dynamic_slice_in_dim(total, mine * half, half, 0)
        total = kept + exchange(away, bit).astype(jnp.float32)
        offset = offset + mine * half
    part = renormed(lax.dynamic_slice_in_dim(old, offset, total.shape[0], 0), total)
    for bit in reversed(bits):
        mine = (position >> bit) & 1
        other = exchange(part, bit)
        part = jnp.concatenate(
            [jnp.where(mine == 0, part, other), jnp.where(mine == 0, other, part)], axis=0
        )
    return part


def synced_square(position, blocks, old):
    x, y = (position[0] >> 1) & 1, (position[0] >> 2) & 1
    keep_x, send_x, keep_y, send_y = blocks
    top0, bottom0 = exchange(send_x, 1), exchange(send_y, 2)

    def fold(a, b, at):
        n = a.shape[0] // 2
        a, b = (lax.dynamic_slice_in_dim(v, at * n, n, 0).astype(jnp.float32) for v in (a, b))
        return (a + b).astype(jnp.bfloat16)

    top1 = exchange(fold(keep_x, top0, 1 - y), 2)
    bottom1 = exchange(fold(keep_y, bottom0, 1 - x), 1)
    zero = lambda s: 0
    part = renorm_units(
        position,
        old,
        [(keep_x, at_y), (top0, at_y), (top1, zero)],
        [(keep_y, at_x), (bottom0, at_x), (bottom1, zero)],
    )
    n = top1.shape[0]
    over_x, over_y = exchange(part, 1), exchange(part, 2)
    top2, bottom2 = exchange(over_y[:n], 1), exchange(over_x[n:], 2)
    return [part, over_x, over_y, top2, bottom2]


def quarter(F, flip_x=0, flip_y=0):
    return lambda s: (2 * (at_x(s) ^ flip_x) + (at_y(s) ^ flip_y)) * (F // 4)


def shards(attn_q, attn_k, attn_v, fast_q, fast_k, fast_v, rates, fast_gate, fast_up, fast_down):
    position = lax.axis_index("seq").astype(jnp.int32).reshape(1)
    count = lax.axis_size("seq")
    heads = fast_gate.shape[0]
    rows = attn_q.shape[0]
    half = rows // 2
    width = 2 if attn_q.shape[1] // HD % 2 == 0 else 1
    prev = shifted(jnp.concatenate([attn_k[half:], attn_v[half:]], axis=0), 1)
    guests = shifted(attn_q[:half], -1)
    rates_t = rates.T
    stay = lambda a: pltpu.with_memory_space_constraint(a, pltpu.HBM)
    attn_q, attn_k, attn_v = stay(attn_q), stay(attn_k), stay(attn_v)
    fast_k, fast_v = stay(fast_k), stay(fast_v)
    weights = (stay(fast_gate), stay(fast_up), stay(fast_down))

    def grads(head, received=None):
        return gradients(position, head, fast_k, fast_v, rates_t, *weights, received)

    if heads == 2 and count == 8:
        near, far = (lambda s: s[0] & 1), (lambda s: 1 - (s[0] & 1))
        received = exchange(grads(far)[0], 0)
        F = fast_gate.shape[1]
        mine = quarter(F)
        starts = [(F // 4, lambda s, at=i * F: at + mine(s)) for i in range(3)]
        old = turned(position, near, *weights, parts=tuple(starts))
        blocks = grads(near, received)
        pieces = synced_square(position, blocks, old)
        other = [exchange(p, 0) for p in pieces]
        news = []
        for head, new in ((near, pieces), (far, other)):
            news.append((head, hidden_part(position, head, fast_q, new), new))
    else:
        news = []
        bits = list(range(count.bit_length() - 1))
        for h in range(heads):
            head = lambda s, h=h: h
            old = turned(position, head, *weights)
            new = synced(grads(head)[0].astype(jnp.float32), old, bits, position[0])
            news.append((head, None, [new]))
    bq = min(256, half)
    tiles = half // bq
    late = [
        [(0, t * bq, half, 1), (1, 0, half + (t + 1) * bq, -1)] for t in range(tiles)
    ]
    early = [[(0, 0, (t + 1) * bq, -1)] for t in range(tiles)]
    guest = [[(0, t * bq, rows, 1)] for t in range(tiles)]
    here = (attn_k, 0, attn_v, 0, rows)
    returned, own_out, own_log = attention(position, [(guests, 0, guest, 2), (attn_q, 0, early, 1)], [here], bq, width)
    far_out = shifted(returned, 1)
    (high,) = attention(position, [(attn_q, 1, late, 0)], [(prev, 0, prev, 1, half), here], bq, width)
    low = merged(position, own_out, far_out, own_log, width)
    mixed = None
    for head, hidden, new in news:
        mixed = apply_head(position, head, fast_q, hidden, new, high, low, mixed)
    return mixed


def solution(mesh):
    placed = (P("seq", "head"),) * 7 + (P("head", None, None),) * 3
    return jax.shard_map(shards, mesh=mesh, in_specs=placed, out_specs=P("seq", "head"), check_vma=False)
```

```python
import functools
import math

import jax
import jax.numpy as jnp
from jax import lax
from jax.experimental import pallas as pl
from jax.experimental.pallas import tpu as pltpu
from jax.sharding import PartitionSpec as P


HD = 128
EPS = 1e-06
NN = (((1,), (0,)), ((), ()))
NT = (((1,), (1,)), ((), ()))
TN = (((0,), (0,)), ((), ()))


def room(mib):
    return pltpu.CompilerParams(vmem_limit_bytes=mib << 20)


def mm(a, b, dims=NN):
    return lax.dot_general(a, b, dims, preferred_element_type=jnp.float32)


def attn_kernel(position_ref, *refs, bq, jobs, sources, log_stride):
    queries = refs[: len(jobs)]
    keys = refs[len(jobs) : len(jobs) + sources]
    values = refs[len(jobs) + sources : len(jobs) + 2 * sources]
    rest = list(refs[len(jobs) + 2 * sources :])
    outs = []
    for _, sums in jobs:
        outs.append((rest.pop(0), rest.pop(0) if sums == 1 else None))
    bufs = (rest.pop(0), rest.pop(0))
    logs = [rest.pop(0) if sums else None for _, sums in jobs]
    group = pl.program_id(0)
    heads = queries[0].shape[1] // HD
    c = math.log2(math.e) / math.sqrt(HD)
    ri = lax.broadcasted_iota(jnp.int32, (bq, bq), 0)
    ci = lax.broadcasted_iota(jnp.int32, (bq, bq), 1)
    absent = position_ref[0] == 0
    units = [(h, j, t) for h in range(heads) for j in range(len(jobs)) for t in range(len(jobs[j][0]))]

    def scores(i):
        h, j, t = units[i]
        hs = slice(h * HD, (h + 1) * HD)
        buf = bufs[i % 2]
        q = queries[j][t * bq : (t + 1) * bq, hs]
        tops = []
        at = 0
        for source, lo, hi, edge in jobs[j][0][t]:
            s = mm(q, keys[source][lo:hi, hs], NT)
            n = hi - lo
            if edge == 1:
                kept = jnp.where(ci >= ri, s[:, :bq], -jnp.inf)
                s = jnp.concatenate([kept, s[:, bq:]], axis=1) if n > bq else kept
            elif edge == -1:
                kept = jnp.where(ci <= ri, s[:, n - bq :], -jnp.inf)
                s = jnp.concatenate([s[:, : n - bq], kept], axis=1) if n > bq else kept
            buf[:, at : at + n] = s
            tops.append(jnp.max(s, axis=1, keepdims=True))
            at += n
        if len(tops) == 1:
            return [tops[0] * c]
        m = jnp.maximum(tops[1], jnp.where(absent, -jnp.inf, tops[0])) * c
        return [jnp.where(absent, 1e30, m), m]

    def finish(i, ms):
        h, j, t = units[i]
        plan, sums = jobs[j]
        hs = slice(h * HD, (h + 1) * HD)
        buf = bufs[i % 2]
        out = total = None
        at = 0
        for (source, lo, hi, _), m in zip(plan[t], ms):
            p = jnp.exp2(buf[:, at : at + hi - lo] * c - m)
            part = jnp.sum(p, axis=1, keepdims=True)
            o = mm(p.astype(jnp.bfloat16), values[source][lo:hi, hs])
            total = part if total is None else total + part
            out = o if out is None else out + o
            at += hi - lo
        rows = slice(t * bq, (t + 1) * bq)
        out = (out / total).astype(jnp.bfloat16)
        head = group * heads + h
        if sums == 2:
            outs[j][0][rows, pl.ds(pl.multiple_of(head * HD, HD), HD)] = out
        else:
            outs[j][0][rows, hs] = out
        if sums:
            lane = lax.broadcasted_iota(jnp.int32, (bq, HD), 1)
            log = ms[-1] + jnp.log(total) * math.log2(math.e)
            logs[j][rows, :] = jnp.where(lane == head, log, logs[j][rows, :])

    if any(sums for _, sums in jobs):

        @pl.when(group == 0)
        def _():
            for log in logs:
                if log is not None:
                    log[...] = jnp.zeros(log.shape, log.dtype)

    ms = scores(0)
    for i in range(len(units)):
        nxt = scores(i + 1) if i + 1 < len(units) else None
        finish(i, ms)
        ms = nxt
    if any(sums for _, sums in jobs):

        @pl.when(group == pl.num_programs(0) - 1)
        def _():
            for (_, sums), (out, log_out), log in zip(jobs, outs, logs):
                if sums == 1:
                    log_out[...] = log[...]
                if sums == 2:
                    x = log[...]
                    a = x.astype(jnp.bfloat16).astype(jnp.float32)
                    b = (x - a).astype(jnp.bfloat16).astype(jnp.float32)
                    x = a + pltpu.roll(b, log_stride, 1) + pltpu.roll(x - a - b, 2 * log_stride, 1)
                    out[:, out.shape[1] - HD :] = x.astype(jnp.bfloat16)


def log_stride_of(cols):
    return 16 * pl.cdiv(cols // HD, 16)


def attention(position, jobs, sources, bq, width):
    cols = jobs[0][0].shape[1]
    w = width * HD
    ranges = [r for _, _, plan, _ in jobs for tile in plan for r in tile]
    span = max(sum(hi - lo for _, lo, hi, _ in tile) for _, _, plan, _ in jobs for tile in plan)
    pairs = bq * sum(hi - lo for _, lo, hi, _ in ranges) * cols // HD
    block = lambda n, at: pl.BlockSpec((n, w), lambda g, f: (at, g))
    whole = lambda *shape: pl.BlockSpec(shape, lambda g, f: (0, 0))
    outs, out_specs, logs = [], [], []
    for _, _, plan, sums in jobs:
        rows = len(plan) * bq
        if sums == 2:
            outs.append(jax.ShapeDtypeStruct((rows, cols + HD), jnp.bfloat16))
            out_specs.append(whole(rows, cols + HD))
        else:
            outs.append(jax.ShapeDtypeStruct((rows, cols), jnp.bfloat16))
            out_specs.append(block(rows, 0))
        if sums == 1:
            outs.append(jax.ShapeDtypeStruct((rows, HD), jnp.float32))
            out_specs.append(whole(rows, HD))
        if sums:
            logs.append(pltpu.VMEM((rows, HD), jnp.float32))
    specs = [block(len(plan) * bq, at) for _, at, plan, _ in jobs]
    specs += [block(n, at) for _, at, _, _, n in sources] + [block(n, at) for _, _, _, at, n in sources]
    kernel = functools.partial(
        attn_kernel,
        bq=bq,
        jobs=[(plan, sums) for _, _, plan, sums in jobs],
        sources=len(sources),
        log_stride=log_stride_of(cols),
    )
    return pl.pallas_call(
        kernel,
        grid_spec=pltpu.PrefetchScalarGridSpec(
            num_scalar_prefetch=1,
            grid=(cols // w,),
            in_specs=specs,
            out_specs=out_specs,
            scratch_shapes=[pltpu.VMEM((bq, span), jnp.float32)] * 2 + logs,
        ),
        out_shape=outs,
        cost_estimate=pl.CostEstimate(
            flops=4 * pairs * HD, bytes_accessed=8 * bq * cols * len(ranges), transcendentals=pairs
        ),
        compiler_params=room(14),
    )(position, *[job[0] for job in jobs], *[x[0] for x in sources], *[x[2] for x in sources])


def owned_rows(F):
    n, m, half = F // 4, F // 8, 3 * F // 2
    unit = 3 * F // 8
    segments = []
    for k in range(4):
        upper, lower = k * unit, half + (2 * (k % 2) + k // 2) * unit
        segments += [
            (k * n, (k + 1) * n, upper),
            (F + k * n, F + k * n + m, upper + n),
            (F + k * n + m, F + (k + 1) * n, lower),
            (2 * F + k * n, 2 * F + (k + 1) * n, lower + m),
        ]
    return segments


def at_x(s):
    return (s[0] >> 1) & 1


def at_y(s):
    return (s[0] >> 2) & 1


def grad_kernel(s_ref, x_ref, v_ref, r_ref, w1_ref, w3_ref, w2_ref, *refs, head, tm, tn, split):
    w13, w2, gu, hid, og = refs[-5:]
    F = w1_ref.shape[2]
    rows = x_ref.shape[0]
    w13[:, :F] = w1_ref[0].astype(jnp.bfloat16)
    w13[:, F:] = w3_ref[0].astype(jnp.bfloat16)
    w2[...] = w2_ref[0].astype(jnp.bfloat16)
    pick = lax.broadcasted_iota(jnp.int32, r_ref.shape, 0) == head(s_ref)
    rate = jnp.sum(jnp.where(pick, r_ref[...], 0.0), axis=0, keepdims=True)
    rate = jnp.transpose(jnp.broadcast_to(rate, (8, rows)))[:, :1]
    og[...] = (-rate * v_ref[...].astype(jnp.float32)).astype(jnp.bfloat16)
    n = rows // tm

    def products(i):
        r = slice(i * tm, (i + 1) * tm)
        return mm(x_ref[r, :], w13[...]), mm(og[r, :], w2[...], NT)

    def finish(i, pre, hg):
        r = slice(i * tm, (i + 1) * tm)
        pg, pu = pre[:, :F], pre[:, F:]
        sg = jax.nn.sigmoid(pg)
        act = pg * sg
        gu[r, :F] = (hg * pu * (sg * (1.0 + pg * (1.0 - sg)))).astype(jnp.bfloat16)
        gu[r, F:] = (hg * act).astype(jnp.bfloat16)
        hid[r, :] = (act * pu).astype(jnp.bfloat16)

    cur = products(0)
    for i in range(n):
        nxt = products(i + 1) if i + 1 < n else None
        finish(i, *cur)
        cur = nxt
    x = x_ref[...]
    hd = hid[...]
    x1, y1 = at_x(s_ref), at_y(s_ref)
    block_rows = 3 * F // 4
    segments = owned_rows(F) if split else []

    def put(lo, grad):
        if not split:
            refs[0][lo : lo + grad.shape[0], :] = grad.astype(refs[0].dtype)
            return
        grad = grad + refs[0][lo : lo + grad.shape[0], :].astype(jnp.float32)
        for a, b, to in segments:
            a, b, to = max(lo, a), min(lo + grad.shape[0], b), to + max(lo - a, 0)
            if a < b:
                block, row = divmod(to, block_rows)
                slot = jnp.where((x1 if block < 2 else y1) == block % 2, 0, 1)
                part = grad[a - lo : b - lo].astype(jnp.bfloat16)
                refs[1 + block // 2][slot, row : row + b - a, :] = part

    for j in range(2 * F // tn):
        put(j * tn, mm(gu[:, j * tn : (j + 1) * tn], x, TN))
    for j in range(F // HD):
        put(2 * F + j * HD, mm(og[:, j * HD : (j + 1) * HD], hd, TN))
    if split:
        for o in range(2):
            refs[3 + 2 * o][...] = refs[1 + o][0]
            refs[4 + 2 * o][...] = refs[1 + o][1]


def gradients(position, head, fk, fv, rates_t, w1, w3, w2, received=None):
    rows = fk.shape[0]
    F = w1.shape[1]
    tm = min(256, rows)
    tn = 256 if 2 * F % 256 == 0 else HD
    once = dict(pipeline_mode=pl.Buffered(1))
    col = pl.BlockSpec((rows, F), lambda i, s: (0, head(s)), **once)
    weight = pl.BlockSpec((1, F, F), lambda i, s: (head(s), 0, 0), **once)
    whole = lambda *shape: pl.BlockSpec(shape, lambda i, s: (0,) * len(shape), **once)
    bf = jnp.bfloat16
    args = [position, fk, fv, rates_t, w1, w3, w2]
    specs = [col, col, whole(*rates_t.shape), weight, weight, weight]
    scratch = [
        pltpu.VMEM((F, 2 * F), bf),
        pltpu.VMEM((F, F), bf),
        pltpu.VMEM((rows, 2 * F), bf),
        pltpu.VMEM((rows, F), bf),
        pltpu.VMEM((rows, F), bf),
    ]
    if received is None:
        shapes = [(3 * F, F)]
    else:
        shapes = [(3 * F // 4, F)] * 4
        args.append(received)
        specs.append(whole(3 * F, F))
        scratch = [pltpu.VMEM((2, 3 * F // 4, F), bf)] * 2 + scratch
    kernel = functools.partial(grad_kernel, head=head, tm=tm, tn=tn, split=received is not None)

    def body(*refs):
        if received is None:
            return kernel(*refs)
        ins, outs, halves, rest = refs[:8], refs[8:12], refs[12:14], refs[14:]
        return kernel(*ins, *halves, *outs, *rest)

    return pl.pallas_call(
        body,
        grid_spec=pltpu.PrefetchScalarGridSpec(
            num_scalar_prefetch=1,
            grid=(1,),
            in_specs=specs,
            out_specs=[whole(*shape) for shape in shapes],
            scratch_shapes=scratch,
        ),
        out_shape=[jax.ShapeDtypeStruct(shape, bf) for shape in shapes],
        cost_estimate=pl.CostEstimate(
            flops=12 * rows * F * F, bytes_accessed=rows * F * 4 + F * F * 18, transcendentals=rows * F
        ),
        name="grads",
        compiler_params=room(40 if received is None else 36),
    )(*args)


def turn_kernel(s_ref, w1, w3, w2, o_ref, *scratch, parts):
    F = w1.shape[2]
    all_ref = scratch[0] if scratch else o_ref
    all_ref[:F, :] = w1[0].T
    all_ref[F : 2 * F, :] = w3[0].T
    all_ref[2 * F :, :] = w2[0].T
    at = 0
    for n, start in parts:
        o_ref[at : at + n, :] = all_ref[pl.ds(pl.multiple_of(start(s_ref), 8), n), :]
        at += n


def turned(position, head, w1, w3, w2, parts=()):
    F = w1.shape[1]
    weight = pl.BlockSpec((1, F, F), lambda i, s: (head(s), 0, 0))
    shape = (sum(n for n, _ in parts), F) if parts else (3 * F, F)
    return pl.pallas_call(
        functools.partial(turn_kernel, parts=parts),
        grid_spec=pltpu.PrefetchScalarGridSpec(
            num_scalar_prefetch=1,
            grid=(1,),
            in_specs=[weight] * 3,
            out_specs=pl.BlockSpec(shape, lambda i, s: (0, 0)),
            scratch_shapes=[pltpu.VMEM((3 * F, F), jnp.float32)] if parts else [],
        ),
        out_shape=jax.ShapeDtypeStruct(shape, jnp.float32),
        cost_estimate=pl.CostEstimate(flops=3 * F * F, bytes_accessed=24 * F * F, transcendentals=0),
        name="turned",
        compiler_params=room(20),
    )(position, w1, w3, w2)


def renormed(old, grad):
    new = old - grad
    old_sq = jnp.sum(old * old, axis=-1, keepdims=True)
    new_sq = jnp.sum(new * new, axis=-1, keepdims=True)
    return (new * (jnp.sqrt(old_sq) / jnp.sqrt(new_sq + EPS))).astype(jnp.bfloat16)


def renorm_kernel(s_ref, old_ref, *refs):
    out = refs[-1]
    at = 0
    for i in range(2):
        a, b, c = (ref[...].astype(jnp.float32) for ref in refs[3 * i : 3 * i + 3])
        rows = slice(at, at + a.shape[0])
        out[rows, :] = renormed(old_ref[rows, :], a + b + c)
        at += a.shape[0]


def renorm_units(position, old, upper, lower):
    rows, F = old.shape
    specs = [pl.BlockSpec((rows, F), lambda i, s: (0, 0))]
    for group in (upper, lower):
        size = group[2][0].shape[0]
        specs += [pl.BlockSpec((size, F), lambda i, s, at=at: (at(s), 0)) for _, at in group]
    return pl.pallas_call(
        renorm_kernel,
        grid_spec=pltpu.PrefetchScalarGridSpec(
            num_scalar_prefetch=1,
            grid=(1,),
            in_specs=specs,
            out_specs=pl.BlockSpec((rows, F), lambda i, s: (0, 0)),
        ),
        out_shape=jax.ShapeDtypeStruct((rows, F), jnp.bfloat16),
        cost_estimate=pl.CostEstimate(flops=10 * rows * F, bytes_accessed=12 * rows * F, transcendentals=0),
        name="renorm",
        compiler_params=room(12),
    )(position, old, *[array for array, _ in upper + lower])


def merge_kernel(s_ref, own_ref, far_ref, own_log, far_log, o_ref, *, stride):
    lane = lax.broadcasted_iota(jnp.int32, own_log.shape, 1)
    heads = o_ref.shape[1] // HD
    for j in range(heads):
        cs = slice(j * HD, (j + 1) * HD)
        at = pl.program_id(0) * heads + j
        pick = lambda ref, of: jnp.sum(
            jnp.where(of, ref[...].astype(jnp.float32), 0.0), axis=1, keepdims=True
        )
        own = pick(own_log, lane == at)
        far = pick(far_log, (lane == at) | (lane == at + stride) | (lane == at + 2 * stride))
        far = jnp.where(s_ref[0] == 0, -jnp.inf, far)
        top = jnp.maximum(own, far)
        own, far = jnp.exp2(own - top), jnp.exp2(far - top)
        share = own / (own + far)
        a, b = own_ref[:, cs].astype(jnp.float32), far_ref[:, cs].astype(jnp.float32)
        o_ref[:, cs] = (a * share + b * (1.0 - share)).astype(o_ref.dtype)


def merged(position, own, far, own_log, width):
    rows, cols = own.shape
    w = width * HD
    col = pl.BlockSpec((rows, w), lambda g, s: (0, g))
    log = lambda at: pl.BlockSpec((rows, HD), lambda g, s: (0, at))
    return pl.pallas_call(
        functools.partial(merge_kernel, stride=log_stride_of(cols)),
        grid_spec=pltpu.PrefetchScalarGridSpec(
            num_scalar_prefetch=1,
            grid=(cols // w,),
            in_specs=[col, col, log(0), log(cols // HD)],
            out_specs=col,
        ),
        out_shape=jax.ShapeDtypeStruct((rows, cols), jnp.bfloat16),
        cost_estimate=pl.CostEstimate(
            flops=8 * rows * cols, bytes_accessed=6 * rows * cols, transcendentals=rows * cols // HD
        ),
        name="merge",
        compiler_params=room(8),
    )(position, own, far, own_log, far)


def gated(h, n):
    g = h[:, :n]
    return (g * jax.nn.sigmoid(g) * h[:, n:]).astype(jnp.bfloat16)


def staggered(n, first, second):
    cur = first(0)
    for i in range(n):
        nxt = first(i + 1) if i + 1 < n else None
        second(i, cur)
        cur = nxt


def for_each_chip(s_ref, body):
    chip = 2 * at_x(s_ref) + at_y(s_ref)
    for k in range(4):
        pl.when(chip == k)(functools.partial(body, k))


NEIGHBOURS = (0, 2, 1, 3)


def hidden_kernel(s_ref, q_ref, own_ref, over_x, over_y, o_ref, w_ref, *, tm, head):
    F = own_ref.shape[1]
    n = F // 4
    for i, ref in enumerate((own_ref, over_x, over_y)):
        w_ref[i * n : (i + 1) * n, :] = ref[:n, :]
        w_ref[(3 + i) * n : (4 + i) * n, :] = ref[n : 2 * n, :]
    cols = pl.ds(pl.multiple_of(head(s_ref) * F, HD), F)

    def first(i):
        return mm(q_ref[i * tm : (i + 1) * tm, cols], w_ref[...], NT)

    def second(i, h):
        o_ref[i * tm : (i + 1) * tm, : 3 * n] = gated(h, 3 * n)

    staggered(q_ref.shape[0] // tm, first, second)


VMEM = pl.BlockSpec(memory_space=pltpu.VMEM)
SMEM = pl.BlockSpec(memory_space=pltpu.SMEM)
ANY = pl.BlockSpec(memory_space=pl.ANY)


def hidden_part(position, head, fq, pieces):
    rows = fq.shape[0]
    F = pieces[0].shape[1]
    bf = jnp.bfloat16
    return pl.pallas_call(
        functools.partial(hidden_kernel, tm=min(256, rows), head=head),
        in_specs=[SMEM] + [VMEM] * 4,
        out_specs=VMEM,
        scratch_shapes=[pltpu.VMEM((3 * F // 2, F), bf)],
        out_shape=jax.ShapeDtypeStruct((rows, F), bf),
        cost_estimate=pl.CostEstimate(
            flops=3 * rows * F * F, bytes_accessed=rows * F * 4 + F * F * 3, transcendentals=rows * F
        ),
        name="hidden",
        compiler_params=room(24),
    )(position, fq, *pieces[:3])


def apply_kernel(s_ref, q_ref, high_ref, low_ref, *rest, tm, head, split):
    o_ref, n_ref, w_ref, h_ref, r_ref, sems = rest[-6:]
    rows = q_ref.shape[0]
    half = rows // 2
    F = n_ref.shape[1]
    n, m = F // 4, F // 8
    cols = pl.ds(pl.multiple_of(head(s_ref) * F, HD), F)
    if split:
        own, over_x, over_y, upper, lower = rest[1:6]
        w_ref[: n + m, :] = upper[...]
        w_ref[n + m :, :] = lower[:m, :]
    else:
        w_ref[...] = rest[0][: 2 * F, :]
        n_ref[...] = rest[0][2 * F :, :]

    def copy_out(i):
        r = pl.ds(i * tm, tm)
        return pltpu.make_async_copy(r_ref.at[r, :], o_ref.at[r, cols], sems.at[i])

    def place(k):
        rows_of = ((own, 2 * n), (over_x, 2 * n), (over_y, 2 * n), (lower, m))
        for flip, (ref, row) in zip(NEIGHBOURS, rows_of):
            for j, from_flip in enumerate(NEIGHBOURS):
                to, at = (k ^ flip) * n, (k ^ from_flip) * n
                n_ref[to : to + n, j * n : (j + 1) * n] = ref[row : row + n, at : at + n]

    if split:
        for_each_chip(s_ref, place)

    def first(i):
        return mm(q_ref[i * tm : (i + 1) * tm, cols], w_ref[...], NT)

    def second(i, h):
        r = slice(i * tm, (i + 1) * tm)
        if split:
            h_ref[r, : 3 * n] = rest[0][r, : 3 * n]
            h_ref[r, 3 * n :] = gated(h, n)
            hid = h_ref[r, :]
        else:
            hid = gated(h, F)
        source, at = (low_ref, i * tm) if i * tm < half else (high_ref, i * tm - half)
        a = source[at : at + tm, cols].astype(jnp.float32)
        r_ref[r, :] = (a + mm(hid, n_ref[...], NT)).astype(r_ref.dtype)
        copy_out(i).start()

    staggered(rows // tm, first, second)
    for i in range(rows // tm):
        copy_out(i).wait()


def apply_head(position, head, fq, hidden, pieces, high, low, into=None):
    rows, cols = fq.shape
    F = pieces[0].shape[1]
    split = hidden is not None
    tm = min(256, rows // 2)
    args = [position, fq, high, low] + ([hidden] if split else []) + list(pieces)
    specs = [SMEM] + [VMEM] * (len(args) - 1)
    aliases = {}
    if into is not None:
        aliases = {len(args): 0}
        args.append(into)
        specs.append(ANY)
    bf = jnp.bfloat16
    return pl.pallas_call(
        functools.partial(apply_kernel, tm=tm, head=head, split=split),
        in_specs=specs,
        out_specs=ANY,
        scratch_shapes=[
            pltpu.VMEM((F, F), bf),
            pltpu.VMEM((F // 2 if split else 2 * F, F), bf),
            pltpu.VMEM((rows, F), bf),
            pltpu.VMEM((rows, F), bf),
            pltpu.SemaphoreType.DMA((rows // tm,)),
        ],
        out_shape=jax.ShapeDtypeStruct((rows, cols), bf),
        input_output_aliases=aliases,
        cost_estimate=pl.CostEstimate(
            flops=3 * rows * F * F, bytes_accessed=rows * F * 8 + F * F * 6, transcendentals=rows * F
        ),
        name="apply",
        compiler_params=room(24),
    )(*args)


def exchange(block, bit):
    size = lax.axis_size("seq")
    return lax.ppermute(block, "seq", [(i, i ^ (1 << bit)) for i in range(size)])


def shifted(block, by):
    size = lax.axis_size("seq")
    return lax.ppermute(block, "seq", [(i, i + by) for i in range(size) if 0 <= i + by < size])


def synced(total, old, bits, position):
    offset = 0
    for bit in bits:
        half = total.shape[0] // 2
        mine = (position >> bit) & 1
        away = lax.dynamic_slice_in_dim(total, (1 - mine) * half, half, 0).astype(jnp.bfloat16)
        kept = lax.dynamic_slice_in_dim(total, mine * half, half, 0)
        total = kept + exchange(away, bit).astype(jnp.float32)
        offset = offset + mine * half
    part = renormed(lax.dynamic_slice_in_dim(old, offset, total.shape[0], 0), total)
    for bit in reversed(bits):
        mine = (position >> bit) & 1
        other = exchange(part, bit)
        part = jnp.concatenate(
            [jnp.where(mine == 0, part, other), jnp.where(mine == 0, other, part)], axis=0
        )
    return part


def synced_square(position, blocks, old):
    x, y = (position[0] >> 1) & 1, (position[0] >> 2) & 1
    keep_x, send_x, keep_y, send_y = blocks
    top0, bottom0 = exchange(send_x, 1), exchange(send_y, 2)

    def fold(a, b, at):
        n = a.shape[0] // 2
        a, b = (lax.dynamic_slice_in_dim(v, at * n, n, 0).astype(jnp.float32) for v in (a, b))
        return (a + b).astype(jnp.bfloat16)

    top1 = exchange(fold(keep_x, top0, 1 - y), 2)
    bottom1 = exchange(fold(keep_y, bottom0, 1 - x), 1)
    zero = lambda s: 0
    part = renorm_units(
        position,
        old,
        [(keep_x, at_y), (top0, at_y), (top1, zero)],
        [(keep_y, at_x), (bottom0, at_x), (bottom1, zero)],
    )
    n = top1.shape[0]
    over_x, over_y = exchange(part, 1), exchange(part, 2)
    top2, bottom2 = exchange(over_y[:n], 1), exchange(over_x[n:], 2)
    return [part, over_x, over_y, top2, bottom2]


def quarter(F, flip_x=0, flip_y=0):
    return lambda s: (2 * (at_x(s) ^ flip_x) + (at_y(s) ^ flip_y)) * (F // 4)


def shards(attn_q, attn_k, attn_v, fast_q, fast_k, fast_v, rates, fast_gate, fast_up, fast_down):
    position = lax.axis_index("seq").astype(jnp.int32).reshape(1)
    count = lax.axis_size("seq")
    heads = fast_gate.shape[0]
    rows = attn_q.shape[0]
    half = rows // 2
    width = 2 if attn_q.shape[1] // HD % 2 == 0 else 1
    prev = shifted(jnp.concatenate([attn_k[half:], attn_v[half:]], axis=0), 1)
    guests = shifted(attn_q[:half], -1)
    rates_t = rates.T
    stay = lambda a: pltpu.with_memory_space_constraint(a, pltpu.HBM)
    attn_q, attn_k, attn_v = stay(attn_q), stay(attn_k), stay(attn_v)
    fast_k, fast_v = stay(fast_k), stay(fast_v)
    weights = (stay(fast_gate), stay(fast_up), stay(fast_down))

    def grads(head, received=None):
        return gradients(position, head, fast_k, fast_v, rates_t, *weights, received)

    if heads == 2 and count == 8:
        near, far = (lambda s: s[0] & 1), (lambda s: 1 - (s[0] & 1))
        received = exchange(grads(far)[0], 0)
        F = fast_gate.shape[1]
        mine = quarter(F)
        starts = [(F // 4, lambda s, at=i * F: at + mine(s)) for i in range(3)]
        old = turned(position, near, *weights, parts=tuple(starts))
        blocks = grads(near, received)
        pieces = synced_square(position, blocks, old)
        other = [exchange(p, 0) for p in pieces]
        news = []
        for head, new in ((near, pieces), (far, other)):
            news.append((head, hidden_part(position, head, fast_q, new), new))
    else:
        news = []
        bits = list(range(count.bit_length() - 1))
        for h in range(heads):
            head = lambda s, h=h: h
            old = turned(position, head, *weights)
            new = synced(grads(head)[0].astype(jnp.float32), old, bits, position[0])
            news.append((head, None, [new]))
    bq = min(256, half)
    tiles = half // bq
    late = [
        [(0, t * bq, half, 1), (1, 0, half + (t + 1) * bq, -1)] for t in range(tiles)
    ]
    early = [[(0, 0, (t + 1) * bq, -1)] for t in range(tiles)]
    guest = [[(0, t * bq, rows, 1)] for t in range(tiles)]
    here = (attn_k, 0, attn_v, 0, rows)
    returned, own_out, own_log = attention(position, [(guests, 0, guest, 2), (attn_q, 0, early, 1)], [here], bq, width)
    far_out = shifted(returned, 1)
    (high,) = attention(position, [(attn_q, 1, late, 0)], [(prev, 0, prev, 1, half), here], bq, width)
    low = merged(position, own_out, far_out, own_log, width)
    mixed = None
    for head, hidden, new in news:
        mixed = apply_head(position, head, fast_q, hidden, new, high, low, mixed)
    return mixed


def solution(mesh):
    placed = (P("seq", "head"),) * 7 + (P("head", None, None),) * 3
    return jax.shard_map(shards, mesh=mesh, in_specs=placed, out_specs=P("seq", "head"), check_vma=False)
```

```python
import functools
import math

import jax
import jax.numpy as jnp
from jax import lax
from jax.experimental import pallas as pl
from jax.experimental.pallas import tpu as pltpu
from jax.sharding import PartitionSpec as P


HD = 128
EPS = 1e-06
NN = (((1,), (0,)), ((), ()))
NT = (((1,), (1,)), ((), ()))
TN = (((0,), (0,)), ((), ()))


def room(mib):
    return pltpu.CompilerParams(vmem_limit_bytes=mib << 20)


def mm(a, b, dims=NN):
    return lax.dot_general(a, b, dims, preferred_element_type=jnp.float32)


def attn_kernel(position_ref, *refs, only, **sizes):
    if only is None:
        return attend(position_ref, *refs, **sizes)
    pl.when(position_ref[0] == only)(functools.partial(attend, position_ref, *refs, **sizes))


def attend(position_ref, *refs, bq, jobs, sources, log_stride):
    queries = refs[: len(jobs)]
    keys = refs[len(jobs) : len(jobs) + sources]
    values = refs[len(jobs) + sources : len(jobs) + 2 * sources]
    rest = list(refs[len(jobs) + 2 * sources :])
    outs = []
    for _, sums in jobs:
        outs.append((rest.pop(0), rest.pop(0) if sums == 1 else None))
    bufs = (rest.pop(0), rest.pop(0))
    logs = [rest.pop(0) if sums else None for _, sums in jobs]
    group = pl.program_id(0)
    heads = queries[0].shape[1] // HD
    c = math.log2(math.e) / math.sqrt(HD)
    ri = lax.broadcasted_iota(jnp.int32, (bq, bq), 0)
    ci = lax.broadcasted_iota(jnp.int32, (bq, bq), 1)
    absent = position_ref[0] == 0
    units = [(h, j, t) for h in range(heads) for j in range(len(jobs)) for t in range(len(jobs[j][0]))]

    def scores(i):
        h, j, t = units[i]
        hs = slice(h * HD, (h + 1) * HD)
        buf = bufs[i % 2]
        q = queries[j][t * bq : (t + 1) * bq, hs]
        tops = []
        at = 0
        for source, lo, hi, edge in jobs[j][0][t]:
            s = mm(q, keys[source][lo:hi, hs], NT)
            n = hi - lo
            if edge == 1:
                kept = jnp.where(ci >= ri, s[:, :bq], -jnp.inf)
                s = jnp.concatenate([kept, s[:, bq:]], axis=1) if n > bq else kept
            elif edge == -1:
                kept = jnp.where(ci <= ri, s[:, n - bq :], -jnp.inf)
                s = jnp.concatenate([s[:, : n - bq], kept], axis=1) if n > bq else kept
            buf[:, at : at + n] = s
            tops.append(jnp.max(s, axis=1, keepdims=True))
            at += n
        if len(tops) == 1:
            return [tops[0] * c]
        m = jnp.maximum(tops[1], jnp.where(absent, -jnp.inf, tops[0])) * c
        return [jnp.where(absent, 1e30, m), m]

    def finish(i, ms):
        h, j, t = units[i]
        plan, sums = jobs[j]
        hs = slice(h * HD, (h + 1) * HD)
        buf = bufs[i % 2]
        out = total = None
        at = 0
        for (source, lo, hi, _), m in zip(plan[t], ms):
            p = jnp.exp2(buf[:, at : at + hi - lo] * c - m)
            part = jnp.sum(p, axis=1, keepdims=True)
            o = mm(p.astype(jnp.bfloat16), values[source][lo:hi, hs])
            total = part if total is None else total + part
            out = o if out is None else out + o
            at += hi - lo
        rows = slice(t * bq, (t + 1) * bq)
        out = (out / total).astype(jnp.bfloat16)
        head = group * heads + h
        if sums == 2:
            outs[j][0][rows, pl.ds(pl.multiple_of(head * HD, HD), HD)] = out
        else:
            outs[j][0][rows, hs] = out
        if sums:
            lane = lax.broadcasted_iota(jnp.int32, (bq, HD), 1)
            log = ms[-1] + jnp.log(total) * math.log2(math.e)
            logs[j][rows, :] = jnp.where(lane == head, log, logs[j][rows, :])

    if any(sums for _, sums in jobs):

        @pl.when(group == 0)
        def _():
            for log in logs:
                if log is not None:
                    log[...] = jnp.zeros(log.shape, log.dtype)

    ms = scores(0)
    for i in range(len(units)):
        nxt = scores(i + 1) if i + 1 < len(units) else None
        finish(i, ms)
        ms = nxt
    if any(sums for _, sums in jobs):

        @pl.when(group == pl.num_programs(0) - 1)
        def _():
            for (_, sums), (out, log_out), log in zip(jobs, outs, logs):
                if sums == 1:
                    log_out[...] = log[...]
                if sums == 2:
                    x = log[...]
                    a = x.astype(jnp.bfloat16).astype(jnp.float32)
                    b = (x - a).astype(jnp.bfloat16).astype(jnp.float32)
                    x = a + pltpu.roll(b, log_stride, 1) + pltpu.roll(x - a - b, 2 * log_stride, 1)
                    out[:, out.shape[1] - HD :] = x.astype(jnp.bfloat16)


def log_stride_of(cols):
    return 16 * pl.cdiv(cols // HD, 16)


def attention(position, jobs, sources, bq, width, only=None):
    cols = jobs[0][0].shape[1]
    w = width * HD
    ranges = [r for _, _, plan, _ in jobs for tile in plan for r in tile]
    span = max(sum(hi - lo for _, lo, hi, _ in tile) for _, _, plan, _ in jobs for tile in plan)
    pairs = bq * sum(hi - lo for _, lo, hi, _ in ranges) * cols // HD
    block = lambda n, at: pl.BlockSpec((n, w), lambda g, f: (at, g))
    whole = lambda *shape: pl.BlockSpec(shape, lambda g, f: (0, 0))
    outs, out_specs, logs = [], [], []
    for _, _, plan, sums in jobs:
        rows = len(plan) * bq
        if sums == 2:
            outs.append(jax.ShapeDtypeStruct((rows, cols + HD), jnp.bfloat16))
            out_specs.append(whole(rows, cols + HD))
        else:
            outs.append(jax.ShapeDtypeStruct((rows, cols), jnp.bfloat16))
            out_specs.append(block(rows, 0))
        if sums == 1:
            outs.append(jax.ShapeDtypeStruct((rows, HD), jnp.float32))
            out_specs.append(whole(rows, HD))
        if sums:
            logs.append(pltpu.VMEM((rows, HD), jnp.float32))
    specs = [block(len(plan) * bq, at) for _, at, plan, _ in jobs]
    specs += [block(n, at) for _, at, _, _, n in sources] + [block(n, at) for _, _, _, at, n in sources]
    kernel = functools.partial(
        attn_kernel,
        only=only,
        bq=bq,
        jobs=[(plan, sums) for _, _, plan, sums in jobs],
        sources=len(sources),
        log_stride=log_stride_of(cols),
    )
    return pl.pallas_call(
        kernel,
        grid_spec=pltpu.PrefetchScalarGridSpec(
            num_scalar_prefetch=1,
            grid=(cols // w,),
            in_specs=specs,
            out_specs=out_specs,
            scratch_shapes=[pltpu.VMEM((bq, span), jnp.float32)] * 2 + logs,
        ),
        out_shape=outs,
        cost_estimate=pl.CostEstimate(
            flops=4 * pairs * HD, bytes_accessed=8 * bq * cols * len(ranges), transcendentals=pairs
        ),
        compiler_params=room(14),
    )(position, *[job[0] for job in jobs], *[x[0] for x in sources], *[x[2] for x in sources])


def owned_rows(F):
    n, m, half = F // 4, F // 8, 3 * F // 2
    unit = 3 * F // 8
    segments = []
    for k in range(4):
        upper, lower = k * unit, half + (2 * (k % 2) + k // 2) * unit
        segments += [
            (k * n, (k + 1) * n, upper),
            (F + k * n, F + k * n + m, upper + n),
            (F + k * n + m, F + (k + 1) * n, lower),
            (2 * F + k * n, 2 * F + (k + 1) * n, lower + m),
        ]
    return segments


def at_x(s):
    return (s[0] >> 1) & 1


def at_y(s):
    return (s[0] >> 2) & 1


def grad_kernel(s_ref, x_ref, v_ref, r_ref, w1_ref, w3_ref, w2_ref, *refs, head, tm, tn, split):
    w13, w2, gu, hid, og = refs[-5:]
    F = w1_ref.shape[2]
    rows = x_ref.shape[0]
    w13[:, :F] = w1_ref[0].astype(jnp.bfloat16)
    w13[:, F:] = w3_ref[0].astype(jnp.bfloat16)
    w2[...] = w2_ref[0].astype(jnp.bfloat16)
    pick = lax.broadcasted_iota(jnp.int32, r_ref.shape, 0) == head(s_ref)
    rate = jnp.sum(jnp.where(pick, r_ref[...], 0.0), axis=0, keepdims=True)
    rate = jnp.transpose(jnp.broadcast_to(rate, (8, rows)))[:, :1]
    og[...] = (-rate * v_ref[...].astype(jnp.float32)).astype(jnp.bfloat16)
    n = rows // tm

    def products(i):
        r = slice(i * tm, (i + 1) * tm)
        return mm(x_ref[r, :], w13[...]), mm(og[r, :], w2[...], NT)

    def finish(i, pre, hg):
        r = slice(i * tm, (i + 1) * tm)
        pg, pu = pre[:, :F], pre[:, F:]
        sg = jax.nn.sigmoid(pg)
        act = pg * sg
        gu[r, :F] = (hg * pu * (sg * (1.0 + pg * (1.0 - sg)))).astype(jnp.bfloat16)
        gu[r, F:] = (hg * act).astype(jnp.bfloat16)
        hid[r, :] = (act * pu).astype(jnp.bfloat16)

    cur = products(0)
    for i in range(n):
        nxt = products(i + 1) if i + 1 < n else None
        finish(i, *cur)
        cur = nxt
    x = x_ref[...]
    hd = hid[...]
    x1, y1 = at_x(s_ref), at_y(s_ref)
    block_rows = 3 * F // 4
    segments = owned_rows(F) if split else []

    def put(lo, grad):
        if not split:
            refs[0][lo : lo + grad.shape[0], :] = grad.astype(refs[0].dtype)
            return
        grad = grad + refs[0][lo : lo + grad.shape[0], :].astype(jnp.float32)
        for a, b, to in segments:
            a, b, to = max(lo, a), min(lo + grad.shape[0], b), to + max(lo - a, 0)
            if a < b:
                block, row = divmod(to, block_rows)
                slot = jnp.where((x1 if block < 2 else y1) == block % 2, 0, 1)
                part = grad[a - lo : b - lo].astype(jnp.bfloat16)
                refs[1 + block // 2][slot, row : row + b - a, :] = part

    for j in range(2 * F // tn):
        put(j * tn, mm(gu[:, j * tn : (j + 1) * tn], x, TN))
    for j in range(F // HD):
        put(2 * F + j * HD, mm(og[:, j * HD : (j + 1) * HD], hd, TN))
    if split:
        for o in range(2):
            refs[3 + 2 * o][...] = refs[1 + o][0]
            refs[4 + 2 * o][...] = refs[1 + o][1]


def gradients(position, head, fk, fv, rates_t, w1, w3, w2, received=None):
    rows = fk.shape[0]
    F = w1.shape[1]
    tm = min(256, rows)
    tn = 256 if 2 * F % 256 == 0 else HD
    once = dict(pipeline_mode=pl.Buffered(1))
    col = pl.BlockSpec((rows, F), lambda i, s: (0, head(s)), **once)
    weight = pl.BlockSpec((1, F, F), lambda i, s: (head(s), 0, 0), **once)
    whole = lambda *shape: pl.BlockSpec(shape, lambda i, s: (0,) * len(shape), **once)
    bf = jnp.bfloat16
    args = [position, fk, fv, rates_t, w1, w3, w2]
    specs = [col, col, whole(*rates_t.shape), weight, weight, weight]
    scratch = [
        pltpu.VMEM((F, 2 * F), bf),
        pltpu.VMEM((F, F), bf),
        pltpu.VMEM((rows, 2 * F), bf),
        pltpu.VMEM((rows, F), bf),
        pltpu.VMEM((rows, F), bf),
    ]
    if received is None:
        shapes = [(3 * F, F)]
    else:
        shapes = [(3 * F // 4, F)] * 4
        args.append(received)
        specs.append(whole(3 * F, F))
        scratch = [pltpu.VMEM((2, 3 * F // 4, F), bf)] * 2 + scratch
    kernel = functools.partial(grad_kernel, head=head, tm=tm, tn=tn, split=received is not None)

    def body(*refs):
        if received is None:
            return kernel(*refs)
        ins, outs, halves, rest = refs[:8], refs[8:12], refs[12:14], refs[14:]
        return kernel(*ins, *halves, *outs, *rest)

    return pl.pallas_call(
        body,
        grid_spec=pltpu.PrefetchScalarGridSpec(
            num_scalar_prefetch=1,
            grid=(1,),
            in_specs=specs,
            out_specs=[whole(*shape) for shape in shapes],
            scratch_shapes=scratch,
        ),
        out_shape=[jax.ShapeDtypeStruct(shape, bf) for shape in shapes],
        cost_estimate=pl.CostEstimate(
            flops=12 * rows * F * F, bytes_accessed=rows * F * 4 + F * F * 18, transcendentals=rows * F
        ),
        name="grads",
        compiler_params=room(40 if received is None else 36),
    )(*args)


def turn_kernel(s_ref, w1, w3, w2, o_ref, *scratch, parts):
    F = w1.shape[2]
    all_ref = scratch[0] if scratch else o_ref
    all_ref[:F, :] = w1[0].T
    all_ref[F : 2 * F, :] = w3[0].T
    all_ref[2 * F :, :] = w2[0].T
    at = 0
    for n, start in parts:
        o_ref[at : at + n, :] = all_ref[pl.ds(pl.multiple_of(start(s_ref), 8), n), :]
        at += n


def turned(position, head, w1, w3, w2, parts=()):
    F = w1.shape[1]
    weight = pl.BlockSpec((1, F, F), lambda i, s: (head(s), 0, 0))
    shape = (sum(n for n, _ in parts), F) if parts else (3 * F, F)
    return pl.pallas_call(
        functools.partial(turn_kernel, parts=parts),
        grid_spec=pltpu.PrefetchScalarGridSpec(
            num_scalar_prefetch=1,
            grid=(1,),
            in_specs=[weight] * 3,
            out_specs=pl.BlockSpec(shape, lambda i, s: (0, 0)),
            scratch_shapes=[pltpu.VMEM((3 * F, F), jnp.float32)] if parts else [],
        ),
        out_shape=jax.ShapeDtypeStruct(shape, jnp.float32),
        cost_estimate=pl.CostEstimate(flops=3 * F * F, bytes_accessed=24 * F * F, transcendentals=0),
        name="turned",
        compiler_params=room(20),
    )(position, w1, w3, w2)


def renormed(old, grad):
    new = old - grad
    old_sq = jnp.sum(old * old, axis=-1, keepdims=True)
    new_sq = jnp.sum(new * new, axis=-1, keepdims=True)
    return (new * (jnp.sqrt(old_sq) / jnp.sqrt(new_sq + EPS))).astype(jnp.bfloat16)


def renorm_kernel(s_ref, old_ref, *refs):
    out = refs[-1]
    at = 0
    for i in range(2):
        a, b, c = (ref[...].astype(jnp.float32) for ref in refs[3 * i : 3 * i + 3])
        rows = slice(at, at + a.shape[0])
        out[rows, :] = renormed(old_ref[rows, :], a + b + c)
        at += a.shape[0]


def renorm_units(position, old, upper, lower):
    rows, F = old.shape
    specs = [pl.BlockSpec((rows, F), lambda i, s: (0, 0))]
    for group in (upper, lower):
        size = group[2][0].shape[0]
        specs += [pl.BlockSpec((size, F), lambda i, s, at=at: (at(s), 0)) for _, at in group]
    return pl.pallas_call(
        renorm_kernel,
        grid_spec=pltpu.PrefetchScalarGridSpec(
            num_scalar_prefetch=1,
            grid=(1,),
            in_specs=specs,
            out_specs=pl.BlockSpec((rows, F), lambda i, s: (0, 0)),
        ),
        out_shape=jax.ShapeDtypeStruct((rows, F), jnp.bfloat16),
        cost_estimate=pl.CostEstimate(flops=10 * rows * F, bytes_accessed=12 * rows * F, transcendentals=0),
        name="renorm",
        compiler_params=room(12),
    )(position, old, *[array for array, _ in upper + lower])


def merge_kernel(s_ref, own_ref, far_ref, own_log, far_log, *rest, stride, local):
    o_ref = rest[-1]
    lane = lax.broadcasted_iota(jnp.int32, own_log.shape, 1)
    heads = o_ref.shape[1] // HD
    here = s_ref[0] == local
    for j in range(heads):
        cs = slice(j * HD, (j + 1) * HD)
        at = pl.program_id(0) * heads + j
        pick = lambda ref, of: jnp.sum(
            jnp.where(of, ref[...].astype(jnp.float32), 0.0), axis=1, keepdims=True
        )
        own = pick(own_log, lane == at)
        far = pick(far_log, (lane == at) | (lane == at + stride) | (lane == at + 2 * stride))
        b = far_ref[:, cs]
        if local is not None:
            far = jnp.where(here, pick(rest[1], lane == at), far)
            b = jnp.where(here, rest[0][:, cs], b)
        far = jnp.where(s_ref[0] == 0, -jnp.inf, far)
        top = jnp.maximum(own, far)
        own, far = jnp.exp2(own - top), jnp.exp2(far - top)
        share = own / (own + far)
        a = own_ref[:, cs].astype(jnp.float32)
        o_ref[:, cs] = (a * share + b.astype(jnp.float32) * (1.0 - share)).astype(o_ref.dtype)


def merged(position, own, far, own_log, width, local=None, local_parts=()):
    rows, cols = own.shape
    w = width * HD
    col = pl.BlockSpec((rows, w), lambda g, s: (0, g))
    log = lambda at: pl.BlockSpec((rows, HD), lambda g, s: (0, at))
    specs = [col, col, log(0), log(cols // HD)]
    if local is not None:
        specs += [col, log(0)]
    return pl.pallas_call(
        functools.partial(merge_kernel, stride=log_stride_of(cols), local=local),
        grid_spec=pltpu.PrefetchScalarGridSpec(
            num_scalar_prefetch=1,
            grid=(cols // w,),
            in_specs=specs,
            out_specs=col,
        ),
        out_shape=jax.ShapeDtypeStruct((rows, cols), jnp.bfloat16),
        cost_estimate=pl.CostEstimate(
            flops=8 * rows * cols, bytes_accessed=6 * rows * cols, transcendentals=rows * cols // HD
        ),
        name="merge",
        compiler_params=room(10),
    )(position, own, far, own_log, far, *local_parts)


def gated(h, n):
    g = h[:, :n]
    return (g * jax.nn.sigmoid(g) * h[:, n:]).astype(jnp.bfloat16)


def staggered(n, first, second):
    cur = first(0)
    for i in range(n):
        nxt = first(i + 1) if i + 1 < n else None
        second(i, cur)
        cur = nxt


def for_each_chip(s_ref, body):
    chip = 2 * at_x(s_ref) + at_y(s_ref)
    for k in range(4):
        pl.when(chip == k)(functools.partial(body, k))


NEIGHBOURS = (0, 2, 1, 3)


def hidden_kernel(s_ref, q_ref, own_ref, over_x, over_y, o_ref, w_ref, *, tm, head):
    F = own_ref.shape[1]
    n = F // 4
    for i, ref in enumerate((own_ref, over_x, over_y)):
        w_ref[i * n : (i + 1) * n, :] = ref[:n, :]
        w_ref[(3 + i) * n : (4 + i) * n, :] = ref[n : 2 * n, :]
    cols = pl.ds(pl.multiple_of(head(s_ref) * F, HD), F)

    def first(i):
        return mm(q_ref[i * tm : (i + 1) * tm, cols], w_ref[...], NT)

    def second(i, h):
        o_ref[i * tm : (i + 1) * tm, : 3 * n] = gated(h, 3 * n)

    staggered(q_ref.shape[0] // tm, first, second)


VMEM = pl.BlockSpec(memory_space=pltpu.VMEM)
SMEM = pl.BlockSpec(memory_space=pltpu.SMEM)
ANY = pl.BlockSpec(memory_space=pl.ANY)


def hidden_part(position, head, fq, pieces):
    rows = fq.shape[0]
    F = pieces[0].shape[1]
    bf = jnp.bfloat16
    return pl.pallas_call(
        functools.partial(hidden_kernel, tm=min(256, rows), head=head),
        in_specs=[SMEM] + [VMEM] * 4,
        out_specs=VMEM,
        scratch_shapes=[pltpu.VMEM((3 * F // 2, F), bf)],
        out_shape=jax.ShapeDtypeStruct((rows, F), bf),
        cost_estimate=pl.CostEstimate(
            flops=3 * rows * F * F, bytes_accessed=rows * F * 4 + F * F * 3, transcendentals=rows * F
        ),
        name="hidden",
        compiler_params=room(24),
    )(position, fq, *pieces[:3])


def apply_kernel(s_ref, q_ref, high_ref, low_ref, *rest, tm, head, split):
    o_ref, n_ref, w_ref, h_ref, r_ref, sems = rest[-6:]
    rows = q_ref.shape[0]
    half = rows // 2
    F = n_ref.shape[1]
    n, m = F // 4, F // 8
    cols = pl.ds(pl.multiple_of(head(s_ref) * F, HD), F)
    if split:
        own, over_x, over_y, upper, lower = rest[1:6]
        w_ref[: n + m, :] = upper[...]
        w_ref[n + m :, :] = lower[:m, :]
    else:
        w_ref[...] = rest[0][: 2 * F, :]
        n_ref[...] = rest[0][2 * F :, :]

    def copy_out(i):
        r = pl.ds(i * tm, tm)
        return pltpu.make_async_copy(r_ref.at[r, :], o_ref.at[r, cols], sems.at[i])

    def place(k):
        rows_of = ((own, 2 * n), (over_x, 2 * n), (over_y, 2 * n), (lower, m))
        for flip, (ref, row) in zip(NEIGHBOURS, rows_of):
            for j, from_flip in enumerate(NEIGHBOURS):
                to, at = (k ^ flip) * n, (k ^ from_flip) * n
                n_ref[to : to + n, j * n : (j + 1) * n] = ref[row : row + n, at : at + n]

    if split:
        for_each_chip(s_ref, place)

    def first(i):
        return mm(q_ref[i * tm : (i + 1) * tm, cols], w_ref[...], NT)

    def second(i, h):
        r = slice(i * tm, (i + 1) * tm)
        if split:
            h_ref[r, : 3 * n] = rest[0][r, : 3 * n]
            h_ref[r, 3 * n :] = gated(h, n)
            hid = h_ref[r, :]
        else:
            hid = gated(h, F)
        source, at = (low_ref, i * tm) if i * tm < half else (high_ref, i * tm - half)
        a = source[at : at + tm, cols].astype(jnp.float32)
        r_ref[r, :] = (a + mm(hid, n_ref[...], NT)).astype(r_ref.dtype)
        copy_out(i).start()

    staggered(rows // tm, first, second)
    for i in range(rows // tm):
        copy_out(i).wait()


def apply_head(position, head, fq, hidden, pieces, high, low, into=None):
    rows, cols = fq.shape
    F = pieces[0].shape[1]
    split = hidden is not None
    tm = min(256, rows // 2)
    args = [position, fq, high, low] + ([hidden] if split else []) + list(pieces)
    specs = [SMEM] + [VMEM] * (len(args) - 1)
    aliases = {}
    if into is not None:
        aliases = {len(args): 0}
        args.append(into)
        specs.append(ANY)
    bf = jnp.bfloat16
    return pl.pallas_call(
        functools.partial(apply_kernel, tm=tm, head=head, split=split),
        in_specs=specs,
        out_specs=ANY,
        scratch_shapes=[
            pltpu.VMEM((F, F), bf),
            pltpu.VMEM((F // 2 if split else 2 * F, F), bf),
            pltpu.VMEM((rows, F), bf),
            pltpu.VMEM((rows, F), bf),
            pltpu.SemaphoreType.DMA((rows // tm,)),
        ],
        out_shape=jax.ShapeDtypeStruct((rows, cols), bf),
        input_output_aliases=aliases,
        cost_estimate=pl.CostEstimate(
            flops=3 * rows * F * F, bytes_accessed=rows * F * 8 + F * F * 6, transcendentals=rows * F
        ),
        name="apply",
        compiler_params=room(24),
    )(*args)


def exchange(block, bit):
    size = lax.axis_size("seq")
    return lax.ppermute(block, "seq", [(i, i ^ (1 << bit)) for i in range(size)])


def shifted(block, by, skip=None):
    size = lax.axis_size("seq")
    route = [(i, i + by) for i in range(size) if 0 <= i + by < size and (i, i + by) != skip]
    return lax.ppermute(block, "seq", route)


def sent(block, source, target):
    size = lax.axis_size("seq")
    route = [(source, target)] + [(i, i) for i in range(size) if i not in (source, target)]
    return lax.ppermute(block, "seq", route)


def synced(total, old, bits, position):
    offset = 0
    for bit in bits:
        half = total.shape[0] // 2
        mine = (position >> bit) & 1
        away = lax.dynamic_slice_in_dim(total, (1 - mine) * half, half, 0).astype(jnp.bfloat16)
        kept = lax.dynamic_slice_in_dim(total, mine * half, half, 0)
        total = kept + exchange(away, bit).astype(jnp.float32)
        offset = offset + mine * half
    part = renormed(lax.dynamic_slice_in_dim(old, offset, total.shape[0], 0), total)
    for bit in reversed(bits):
        mine = (position >> bit) & 1
        other = exchange(part, bit)
        part = jnp.concatenate(
            [jnp.where(mine == 0, part, other), jnp.where(mine == 0, other, part)], axis=0
        )
    return part


def synced_square(position, blocks, old):
    x, y = (position[0] >> 1) & 1, (position[0] >> 2) & 1
    keep_x, send_x, keep_y, send_y = blocks
    top0, bottom0 = exchange(send_x, 1), exchange(send_y, 2)

    def fold(a, b, at):
        n = a.shape[0] // 2
        a, b = (lax.dynamic_slice_in_dim(v, at * n, n, 0).astype(jnp.float32) for v in (a, b))
        return (a + b).astype(jnp.bfloat16)

    top1 = exchange(fold(keep_x, top0, 1 - y), 2)
    bottom1 = exchange(fold(keep_y, bottom0, 1 - x), 1)
    zero = lambda s: 0
    part = renorm_units(
        position,
        old,
        [(keep_x, at_y), (top0, at_y), (top1, zero)],
        [(keep_y, at_x), (bottom0, at_x), (bottom1, zero)],
    )
    n = top1.shape[0]
    over_x, over_y = exchange(part, 1), exchange(part, 2)
    top2, bottom2 = exchange(over_y[:n], 1), exchange(over_x[n:], 2)
    return [part, over_x, over_y, top2, bottom2]


def quarter(F, flip_x=0, flip_y=0):
    return lambda s: (2 * (at_x(s) ^ flip_x) + (at_y(s) ^ flip_y)) * (F // 4)


def shards(attn_q, attn_k, attn_v, fast_q, fast_k, fast_v, rates, fast_gate, fast_up, fast_down):
    position = lax.axis_index("seq").astype(jnp.int32).reshape(1)
    count = lax.axis_size("seq")
    heads = fast_gate.shape[0]
    rows = attn_q.shape[0]
    half = rows // 2
    width = 2 if attn_q.shape[1] // HD % 2 == 0 else 1
    square = heads == 2 and count == 8
    pack = lambda lo, hi: jnp.concatenate([attn_k[lo:hi], attn_v[lo:hi]], axis=0)
    guests = shifted(attn_q[:half], -1, (4, 3) if square else None)
    prev = shifted(pack(half, rows), 1)
    all_k, all_v = attn_k, attn_v
    rates_t = rates.T
    stay = lambda a: pltpu.with_memory_space_constraint(a, pltpu.HBM)
    attn_q, attn_k, attn_v = stay(attn_q), stay(attn_k), stay(attn_v)
    fast_k, fast_v = stay(fast_k), stay(fast_v)
    weights = (stay(fast_gate), stay(fast_up), stay(fast_down))

    def grads(head, received=None):
        return gradients(position, head, fast_k, fast_v, rates_t, *weights, received)

    if square:
        near, far = (lambda s: s[0] & 1), (lambda s: 1 - (s[0] & 1))
        theirs = grads(far)[0]
        received = exchange(theirs, 0)
        F = fast_gate.shape[1]
        mine = quarter(F)
        starts = [(F // 4, lambda s, at=i * F: at + mine(s)) for i in range(3)]
        old = turned(position, near, *weights, parts=tuple(starts))
        blocks = grads(near, received)
        pieces = synced_square(position, blocks, old)
        other = [exchange(p, 0) for p in pieces]
        news = []
        for head, new in ((near, pieces), (far, other)):
            news.append((head, hidden_part(position, head, fast_q, new), new))
    else:
        news = []
        bits = list(range(count.bit_length() - 1))
        for h in range(heads):
            head = lambda s, h=h: h
            old = turned(position, head, *weights)
            new = synced(grads(head)[0].astype(jnp.float32), old, bits, position[0])
            news.append((head, None, [new]))
    bq = min(256, half)
    tiles = half // bq
    late = [
        [(0, t * bq, half, 1), (1, 0, half + (t + 1) * bq, -1)] for t in range(tiles)
    ]
    early = [[(0, 0, (t + 1) * bq, -1)] for t in range(tiles)]
    guest = [[(0, t * bq, rows, 1)] for t in range(tiles)]
    here = (attn_k, 0, attn_v, 0, rows)
    returned, own_out, own_log = attention(position, [(guests, 0, guest, 2), (attn_q, 0, early, 1)], [here], bq, width)
    far_out = shifted(returned, 1, (3, 4) if square else None)
    (high,) = attention(position, [(attn_q, 1, late, 0)], [(prev, 0, prev, 1, half), here], bq, width)
    local, local_parts = None, ()
    if square:
        local = 4
        all_k, all_v, _ = lax.optimization_barrier((all_k, all_v, theirs))
        first = jnp.concatenate([all_k[:half], all_v[:half]], axis=0)
        first = sent(first, 3, 7)
        first = sent(first, 7, local)
        both = [[(0, t * bq, half, 1), (1, 0, half, 0)] for t in range(tiles)]
        local_parts = attention(
            position, [(attn_q, 0, both, 1)], [(first, 0, first, 1, half), (prev, 0, prev, 1, half)], bq, width, local
        )
    low = merged(position, own_out, far_out, own_log, width, local, local_parts)
    mixed = None
    for head, hidden, new in news:
        mixed = apply_head(position, head, fast_q, hidden, new, high, low, mixed)
    return mixed


def solution(mesh):
    placed = (P("seq", "head"),) * 7 + (P("head", None, None),) * 3
    return jax.shard_map(shards, mesh=mesh, in_specs=placed, out_specs=P("seq", "head"), check_vma=False)
```

```python
import functools
import math

import jax
import jax.numpy as jnp
from jax import lax
from jax.experimental import pallas as pl
from jax.experimental.pallas import tpu as pltpu
from jax.sharding import PartitionSpec as P


HD = 128
EPS = 1e-06
NN = (((1,), (0,)), ((), ()))
NT = (((1,), (1,)), ((), ()))
TN = (((0,), (0,)), ((), ()))


def room(mib):
    return pltpu.CompilerParams(vmem_limit_bytes=mib << 20)


def mm(a, b, dims=NN):
    return lax.dot_general(a, b, dims, preferred_element_type=jnp.float32)


def attn_kernel(position_ref, *refs, only, **sizes):
    if only is None:
        return attend(position_ref, *refs, **sizes)
    pl.when(position_ref[0] == only)(functools.partial(attend, position_ref, *refs, **sizes))


def attend(position_ref, *refs, bq, jobs, sources, log_stride):
    queries = refs[: len(jobs)]
    keys = refs[len(jobs) : len(jobs) + sources]
    values = refs[len(jobs) + sources : len(jobs) + 2 * sources]
    rest = list(refs[len(jobs) + 2 * sources :])
    outs = []
    for _, sums in jobs:
        outs.append((rest.pop(0), rest.pop(0) if sums == 1 else None))
    bufs = (rest.pop(0), rest.pop(0))
    logs = [rest.pop(0) if sums else None for _, sums in jobs]
    group = pl.program_id(0)
    heads = queries[0].shape[1] // HD
    c = math.log2(math.e) / math.sqrt(HD)
    ri = lax.broadcasted_iota(jnp.int32, (bq, bq), 0)
    ci = lax.broadcasted_iota(jnp.int32, (bq, bq), 1)
    absent = position_ref[0] == 0
    units = [(h, j, t) for h in range(heads) for j in range(len(jobs)) for t in range(len(jobs[j][0]))]

    def scores(i):
        h, j, t = units[i]
        hs = slice(h * HD, (h + 1) * HD)
        buf = bufs[i % 2]
        q = queries[j][t * bq : (t + 1) * bq, hs]
        tops = []
        at = 0
        for source, lo, hi, edge in jobs[j][0][t]:
            s = mm(q, keys[source][lo:hi, hs], NT)
            n = hi - lo
            if edge == 1:
                kept = jnp.where(ci >= ri, s[:, :bq], -jnp.inf)
                s = jnp.concatenate([kept, s[:, bq:]], axis=1) if n > bq else kept
            elif edge == -1:
                kept = jnp.where(ci <= ri, s[:, n - bq :], -jnp.inf)
                s = jnp.concatenate([s[:, : n - bq], kept], axis=1) if n > bq else kept
            buf[:, at : at + n] = s
            tops.append(jnp.max(s, axis=1, keepdims=True))
            at += n
        if len(tops) == 1:
            return [tops[0] * c]
        m = jnp.maximum(tops[1], jnp.where(absent, -jnp.inf, tops[0])) * c
        return [jnp.where(absent, 1e30, m), m]

    def finish(i, ms):
        h, j, t = units[i]
        plan, sums = jobs[j]
        hs = slice(h * HD, (h + 1) * HD)
        buf = bufs[i % 2]
        out = total = None
        at = 0
        for (source, lo, hi, _), m in zip(plan[t], ms):
            p = jnp.exp2(buf[:, at : at + hi - lo] * c - m)
            part = jnp.sum(p, axis=1, keepdims=True)
            o = mm(p.astype(jnp.bfloat16), values[source][lo:hi, hs])
            total = part if total is None else total + part
            out = o if out is None else out + o
            at += hi - lo
        rows = slice(t * bq, (t + 1) * bq)
        out = (out / total).astype(jnp.bfloat16)
        head = group * heads + h
        if sums == 2:
            outs[j][0][rows, pl.ds(pl.multiple_of(head * HD, HD), HD)] = out
        else:
            outs[j][0][rows, hs] = out
        if sums:
            lane = lax.broadcasted_iota(jnp.int32, (bq, HD), 1)
            log = ms[-1] + jnp.log(total) * math.log2(math.e)
            logs[j][rows, :] = jnp.where(lane == head, log, logs[j][rows, :])

    if any(sums for _, sums in jobs):

        @pl.when(group == 0)
        def _():
            for log in logs:
                if log is not None:
                    log[...] = jnp.zeros(log.shape, log.dtype)

    ms = scores(0)
    for i in range(len(units)):
        nxt = scores(i + 1) if i + 1 < len(units) else None
        finish(i, ms)
        ms = nxt
    if any(sums for _, sums in jobs):

        @pl.when(group == pl.num_programs(0) - 1)
        def _():
            for (_, sums), (out, log_out), log in zip(jobs, outs, logs):
                if sums == 1:
                    log_out[...] = log[...]
                if sums == 2:
                    x = log[...]
                    a = x.astype(jnp.bfloat16).astype(jnp.float32)
                    b = (x - a).astype(jnp.bfloat16).astype(jnp.float32)
                    x = a + pltpu.roll(b, log_stride, 1) + pltpu.roll(x - a - b, 2 * log_stride, 1)
                    out[:, out.shape[1] - HD :] = x.astype(jnp.bfloat16)


def log_stride_of(cols):
    return 16 * pl.cdiv(cols // HD, 16)


def attention(position, jobs, sources, bq, width, only=None):
    cols = jobs[0][0].shape[1]
    w = width * HD
    ranges = [r for _, _, plan, _ in jobs for tile in plan for r in tile]
    span = max(sum(hi - lo for _, lo, hi, _ in tile) for _, _, plan, _ in jobs for tile in plan)
    pairs = bq * sum(hi - lo for _, lo, hi, _ in ranges) * cols // HD
    moving = (lambda g, f: g) if only is None else (lambda g, f: jnp.where(f[0] == only, g, 0))
    block = lambda n, at: pl.BlockSpec((n, w), lambda g, f: (at, moving(g, f)))
    whole = lambda *shape: pl.BlockSpec(shape, lambda g, f: (0, 0))
    outs, out_specs, logs = [], [], []
    for _, _, plan, sums in jobs:
        rows = len(plan) * bq
        if sums == 2:
            outs.append(jax.ShapeDtypeStruct((rows, cols + HD), jnp.bfloat16))
            out_specs.append(whole(rows, cols + HD))
        else:
            outs.append(jax.ShapeDtypeStruct((rows, cols), jnp.bfloat16))
            out_specs.append(block(rows, 0))
        if sums == 1:
            outs.append(jax.ShapeDtypeStruct((rows, HD), jnp.float32))
            out_specs.append(whole(rows, HD))
        if sums:
            logs.append(pltpu.VMEM((rows, HD), jnp.float32))
    specs = [block(len(plan) * bq, at) for _, at, plan, _ in jobs]
    specs += [block(n, at) for _, at, _, _, n in sources] + [block(n, at) for _, _, _, at, n in sources]
    kernel = functools.partial(
        attn_kernel,
        only=only,
        bq=bq,
        jobs=[(plan, sums) for _, _, plan, sums in jobs],
        sources=len(sources),
        log_stride=log_stride_of(cols),
    )
    return pl.pallas_call(
        kernel,
        grid_spec=pltpu.PrefetchScalarGridSpec(
            num_scalar_prefetch=1,
            grid=(cols // w,),
            in_specs=specs,
            out_specs=out_specs,
            scratch_shapes=[pltpu.VMEM((bq, span), jnp.float32)] * 2 + logs,
        ),
        out_shape=outs,
        cost_estimate=pl.CostEstimate(
            flops=4 * pairs * HD, bytes_accessed=8 * bq * cols * len(ranges), transcendentals=pairs
        ),
        compiler_params=room(14),
    )(position, *[job[0] for job in jobs], *[x[0] for x in sources], *[x[2] for x in sources])


def owned_rows(F):
    n, m, half = F // 4, F // 8, 3 * F // 2
    unit = 3 * F // 8
    segments = []
    for k in range(4):
        upper, lower = k * unit, half + (2 * (k % 2) + k // 2) * unit
        segments += [
            (k * n, (k + 1) * n, upper),
            (F + k * n, F + k * n + m, upper + n),
            (F + k * n + m, F + (k + 1) * n, lower),
            (2 * F + k * n, 2 * F + (k + 1) * n, lower + m),
        ]
    return segments


def at_x(s):
    return (s[0] >> 1) & 1


def at_y(s):
    return (s[0] >> 2) & 1


def grad_kernel(s_ref, x_ref, v_ref, r_ref, w1_ref, w3_ref, w2_ref, *refs, head, tm, tn, split):
    w13, w2, gu, hid, og = refs[-5:]
    F = w1_ref.shape[2]
    rows = x_ref.shape[0]
    w13[:, :F] = w1_ref[0].astype(jnp.bfloat16)
    w13[:, F:] = w3_ref[0].astype(jnp.bfloat16)
    w2[...] = w2_ref[0].astype(jnp.bfloat16)
    pick = lax.broadcasted_iota(jnp.int32, r_ref.shape, 0) == head(s_ref)
    rate = jnp.sum(jnp.where(pick, r_ref[...], 0.0), axis=0, keepdims=True)
    rate = jnp.transpose(jnp.broadcast_to(rate, (8, rows)))[:, :1]
    og[...] = (-rate * v_ref[...].astype(jnp.float32)).astype(jnp.bfloat16)
    n = rows // tm

    def products(i):
        r = slice(i * tm, (i + 1) * tm)
        return mm(x_ref[r, :], w13[...]), mm(og[r, :], w2[...], NT)

    def finish(i, pre, hg):
        r = slice(i * tm, (i + 1) * tm)
        pg, pu = pre[:, :F], pre[:, F:]
        sg = jax.nn.sigmoid(pg)
        act = pg * sg
        gu[r, :F] = (hg * pu * (sg * (1.0 + pg * (1.0 - sg)))).astype(jnp.bfloat16)
        gu[r, F:] = (hg * act).astype(jnp.bfloat16)
        hid[r, :] = (act * pu).astype(jnp.bfloat16)

    cur = products(0)
    for i in range(n):
        nxt = products(i + 1) if i + 1 < n else None
        finish(i, *cur)
        cur = nxt
    x = x_ref[...]
    hd = hid[...]
    x1, y1 = at_x(s_ref), at_y(s_ref)
    block_rows = 3 * F // 4
    segments = owned_rows(F) if split else []

    def put(lo, grad):
        if not split:
            refs[0][lo : lo + grad.shape[0], :] = grad.astype(refs[0].dtype)
            return
        grad = grad + refs[0][lo : lo + grad.shape[0], :].astype(jnp.float32)
        for a, b, to in segments:
            a, b, to = max(lo, a), min(lo + grad.shape[0], b), to + max(lo - a, 0)
            if a < b:
                block, row = divmod(to, block_rows)
                slot = jnp.where((x1 if block < 2 else y1) == block % 2, 0, 1)
                part = grad[a - lo : b - lo].astype(jnp.bfloat16)
                refs[1 + block // 2][slot, row : row + b - a, :] = part

    for j in range(2 * F // tn):
        put(j * tn, mm(gu[:, j * tn : (j + 1) * tn], x, TN))
    for j in range(F // HD):
        put(2 * F + j * HD, mm(og[:, j * HD : (j + 1) * HD], hd, TN))
    if split:
        for o in range(2):
            refs[3 + 2 * o][...] = refs[1 + o][0]
            refs[4 + 2 * o][...] = refs[1 + o][1]


def gradients(position, head, fk, fv, rates_t, w1, w3, w2, received=None):
    rows = fk.shape[0]
    F = w1.shape[1]
    tm = min(256, rows)
    tn = 256 if 2 * F % 256 == 0 else HD
    once = dict(pipeline_mode=pl.Buffered(1))
    col = pl.BlockSpec((rows, F), lambda i, s: (0, head(s)), **once)
    weight = pl.BlockSpec((1, F, F), lambda i, s: (head(s), 0, 0), **once)
    whole = lambda *shape: pl.BlockSpec(shape, lambda i, s: (0,) * len(shape), **once)
    bf = jnp.bfloat16
    args = [position, fk, fv, rates_t, w1, w3, w2]
    specs = [col, col, whole(*rates_t.shape), weight, weight, weight]
    scratch = [
        pltpu.VMEM((F, 2 * F), bf),
        pltpu.VMEM((F, F), bf),
        pltpu.VMEM((rows, 2 * F), bf),
        pltpu.VMEM((rows, F), bf),
        pltpu.VMEM((rows, F), bf),
    ]
    if received is None:
        shapes = [(3 * F, F)]
    else:
        shapes = [(3 * F // 4, F)] * 4
        args.append(received)
        specs.append(whole(3 * F, F))
        scratch = [pltpu.VMEM((2, 3 * F // 4, F), bf)] * 2 + scratch
    kernel = functools.partial(grad_kernel, head=head, tm=tm, tn=tn, split=received is not None)

    def body(*refs):
        if received is None:
            return kernel(*refs)
        ins, outs, halves, rest = refs[:8], refs[8:12], refs[12:14], refs[14:]
        return kernel(*ins, *halves, *outs, *rest)

    return pl.pallas_call(
        body,
        grid_spec=pltpu.PrefetchScalarGridSpec(
            num_scalar_prefetch=1,
            grid=(1,),
            in_specs=specs,
            out_specs=[whole(*shape) for shape in shapes],
            scratch_shapes=scratch,
        ),
        out_shape=[jax.ShapeDtypeStruct(shape, bf) for shape in shapes],
        cost_estimate=pl.CostEstimate(
            flops=12 * rows * F * F, bytes_accessed=rows * F * 4 + F * F * 18, transcendentals=rows * F
        ),
        name="grads",
        compiler_params=room(40 if received is None else 36),
    )(*args)


def turn_kernel(s_ref, w1, w3, w2, o_ref, *scratch, parts):
    F = w1.shape[2]
    all_ref = scratch[0] if scratch else o_ref
    all_ref[:F, :] = w1[0].T
    all_ref[F : 2 * F, :] = w3[0].T
    all_ref[2 * F :, :] = w2[0].T
    at = 0
    for n, start in parts:
        o_ref[at : at + n, :] = all_ref[pl.ds(pl.multiple_of(start(s_ref), 8), n), :]
        at += n


def turned(position, head, w1, w3, w2, parts=()):
    F = w1.shape[1]
    weight = pl.BlockSpec((1, F, F), lambda i, s: (head(s), 0, 0))
    shape = (sum(n for n, _ in parts), F) if parts else (3 * F, F)
    return pl.pallas_call(
        functools.partial(turn_kernel, parts=parts),
        grid_spec=pltpu.PrefetchScalarGridSpec(
            num_scalar_prefetch=1,
            grid=(1,),
            in_specs=[weight] * 3,
            out_specs=pl.BlockSpec(shape, lambda i, s: (0, 0)),
            scratch_shapes=[pltpu.VMEM((3 * F, F), jnp.float32)] if parts else [],
        ),
        out_shape=jax.ShapeDtypeStruct(shape, jnp.float32),
        cost_estimate=pl.CostEstimate(flops=3 * F * F, bytes_accessed=24 * F * F, transcendentals=0),
        name="turned",
        compiler_params=room(20),
    )(position, w1, w3, w2)


def renormed(old, grad):
    new = old - grad
    old_sq = jnp.sum(old * old, axis=-1, keepdims=True)
    new_sq = jnp.sum(new * new, axis=-1, keepdims=True)
    return (new * (jnp.sqrt(old_sq) / jnp.sqrt(new_sq + EPS))).astype(jnp.bfloat16)


def renorm_kernel(s_ref, old_ref, *refs):
    out = refs[-1]
    at = 0
    for i in range(2):
        a, b, c = (ref[...].astype(jnp.float32) for ref in refs[3 * i : 3 * i + 3])
        rows = slice(at, at + a.shape[0])
        out[rows, :] = renormed(old_ref[rows, :], a + b + c)
        at += a.shape[0]


def renorm_units(position, old, upper, lower):
    rows, F = old.shape
    specs = [pl.BlockSpec((rows, F), lambda i, s: (0, 0))]
    for group in (upper, lower):
        size = group[2][0].shape[0]
        specs += [pl.BlockSpec((size, F), lambda i, s, at=at: (at(s), 0)) for _, at in group]
    return pl.pallas_call(
        renorm_kernel,
        grid_spec=pltpu.PrefetchScalarGridSpec(
            num_scalar_prefetch=1,
            grid=(1,),
            in_specs=specs,
            out_specs=pl.BlockSpec((rows, F), lambda i, s: (0, 0)),
        ),
        out_shape=jax.ShapeDtypeStruct((rows, F), jnp.bfloat16),
        cost_estimate=pl.CostEstimate(flops=10 * rows * F, bytes_accessed=12 * rows * F, transcendentals=0),
        name="renorm",
        compiler_params=room(12),
    )(position, old, *[array for array, _ in upper + lower])


def merge_kernel(s_ref, own_ref, far_ref, own_log, far_log, *rest, stride, local):
    o_ref = rest[-1]
    lane = lax.broadcasted_iota(jnp.int32, own_log.shape, 1)
    heads = o_ref.shape[1] // HD
    here = s_ref[0] == local
    for j in range(heads):
        cs = slice(j * HD, (j + 1) * HD)
        at = pl.program_id(0) * heads + j
        pick = lambda ref, of: jnp.sum(
            jnp.where(of, ref[...].astype(jnp.float32), 0.0), axis=1, keepdims=True
        )
        own = pick(own_log, lane == at)
        far = pick(far_log, (lane == at) | (lane == at + stride) | (lane == at + 2 * stride))
        b = far_ref[:, cs]
        if local is not None:
            far = jnp.where(here, pick(rest[1], lane == at), far)
            b = jnp.where(here, rest[0][:, cs], b)
        far = jnp.where(s_ref[0] == 0, -jnp.inf, far)
        top = jnp.maximum(own, far)
        own, far = jnp.exp2(own - top), jnp.exp2(far - top)
        share = own / (own + far)
        a = own_ref[:, cs].astype(jnp.float32)
        o_ref[:, cs] = (a * share + b.astype(jnp.float32) * (1.0 - share)).astype(o_ref.dtype)


def merged(position, own, far, own_log, width, local=None, local_parts=()):
    rows, cols = own.shape
    w = width * HD
    col = pl.BlockSpec((rows, w), lambda g, s: (0, g))
    log = lambda at: pl.BlockSpec((rows, HD), lambda g, s: (0, at))
    specs = [col, col, log(0), log(cols // HD)]
    if local is not None:
        specs += [col, log(0)]
    return pl.pallas_call(
        functools.partial(merge_kernel, stride=log_stride_of(cols), local=local),
        grid_spec=pltpu.PrefetchScalarGridSpec(
            num_scalar_prefetch=1,
            grid=(cols // w,),
            in_specs=specs,
            out_specs=col,
        ),
        out_shape=jax.ShapeDtypeStruct((rows, cols), jnp.bfloat16),
        cost_estimate=pl.CostEstimate(
            flops=8 * rows * cols, bytes_accessed=6 * rows * cols, transcendentals=rows * cols // HD
        ),
        name="merge",
        compiler_params=room(10),
    )(position, own, far, own_log, far, *local_parts)


def gated(h, n):
    g = h[:, :n]
    return (g * jax.nn.sigmoid(g) * h[:, n:]).astype(jnp.bfloat16)


def staggered(n, first, second):
    cur = first(0)
    for i in range(n):
        nxt = first(i + 1) if i + 1 < n else None
        second(i, cur)
        cur = nxt


def for_each_chip(s_ref, body):
    chip = 2 * at_x(s_ref) + at_y(s_ref)
    for k in range(4):
        pl.when(chip == k)(functools.partial(body, k))


NEIGHBOURS = (0, 2, 1, 3)


def hidden_kernel(s_ref, q_ref, own_ref, over_x, over_y, o_ref, w_ref, *, tm, head):
    F = own_ref.shape[1]
    n = F // 4
    for i, ref in enumerate((own_ref, over_x, over_y)):
        w_ref[i * n : (i + 1) * n, :] = ref[:n, :]
        w_ref[(3 + i) * n : (4 + i) * n, :] = ref[n : 2 * n, :]
    cols = pl.ds(pl.multiple_of(head(s_ref) * F, HD), F)

    def first(i):
        return mm(q_ref[i * tm : (i + 1) * tm, cols], w_ref[...], NT)

    def second(i, h):
        o_ref[i * tm : (i + 1) * tm, : 3 * n] = gated(h, 3 * n)

    staggered(q_ref.shape[0] // tm, first, second)


VMEM = pl.BlockSpec(memory_space=pltpu.VMEM)
SMEM = pl.BlockSpec(memory_space=pltpu.SMEM)
ANY = pl.BlockSpec(memory_space=pl.ANY)


def hidden_part(position, head, fq, pieces):
    rows = fq.shape[0]
    F = pieces[0].shape[1]
    bf = jnp.bfloat16
    return pl.pallas_call(
        functools.partial(hidden_kernel, tm=min(256, rows), head=head),
        in_specs=[SMEM] + [VMEM] * 4,
        out_specs=VMEM,
        scratch_shapes=[pltpu.VMEM((3 * F // 2, F), bf)],
        out_shape=jax.ShapeDtypeStruct((rows, F), bf),
        cost_estimate=pl.CostEstimate(
            flops=3 * rows * F * F, bytes_accessed=rows * F * 4 + F * F * 3, transcendentals=rows * F
        ),
        name="hidden",
        compiler_params=room(24),
    )(position, fq, *pieces[:3])


def apply_kernel(s_ref, q_ref, high_ref, low_ref, *rest, tm, head, split):
    o_ref, n_ref, w_ref, h_ref, r_ref, sems = rest[-6:]
    rows = q_ref.shape[0]
    half = rows // 2
    F = n_ref.shape[1]
    n, m = F // 4, F // 8
    cols = pl.ds(pl.multiple_of(head(s_ref) * F, HD), F)
    if split:
        own, over_x, over_y, upper, lower = rest[1:6]
        w_ref[: n + m, :] = upper[...]
        w_ref[n + m :, :] = lower[:m, :]
    else:
        w_ref[...] = rest[0][: 2 * F, :]
        n_ref[...] = rest[0][2 * F :, :]

    def copy_out(i):
        r = pl.ds(i * tm, tm)
        return pltpu.make_async_copy(r_ref.at[r, :], o_ref.at[r, cols], sems.at[i])

    def place(k):
        rows_of = ((own, 2 * n), (over_x, 2 * n), (over_y, 2 * n), (lower, m))
        for flip, (ref, row) in zip(NEIGHBOURS, rows_of):
            for j, from_flip in enumerate(NEIGHBOURS):
                to, at = (k ^ flip) * n, (k ^ from_flip) * n
                n_ref[to : to + n, j * n : (j + 1) * n] = ref[row : row + n, at : at + n]

    if split:
        for_each_chip(s_ref, place)

    def first(i):
        return mm(q_ref[i * tm : (i + 1) * tm, cols], w_ref[...], NT)

    def second(i, h):
        r = slice(i * tm, (i + 1) * tm)
        if split:
            h_ref[r, : 3 * n] = rest[0][r, : 3 * n]
            h_ref[r, 3 * n :] = gated(h, n)
            hid = h_ref[r, :]
        else:
            hid = gated(h, F)
        source, at = (low_ref, i * tm) if i * tm < half else (high_ref, i * tm - half)
        a = source[at : at + tm, cols].astype(jnp.float32)
        r_ref[r, :] = (a + mm(hid, n_ref[...], NT)).astype(r_ref.dtype)
        copy_out(i).start()

    staggered(rows // tm, first, second)
    for i in range(rows // tm):
        copy_out(i).wait()


def apply_head(position, head, fq, hidden, pieces, high, low, into=None):
    rows, cols = fq.shape
    F = pieces[0].shape[1]
    split = hidden is not None
    tm = min(256, rows // 2)
    args = [position, fq, high, low] + ([hidden] if split else []) + list(pieces)
    specs = [SMEM] + [VMEM] * (len(args) - 1)
    aliases = {}
    if into is not None:
        aliases = {len(args): 0}
        args.append(into)
        specs.append(ANY)
    bf = jnp.bfloat16
    return pl.pallas_call(
        functools.partial(apply_kernel, tm=tm, head=head, split=split),
        in_specs=specs,
        out_specs=ANY,
        scratch_shapes=[
            pltpu.VMEM((F, F), bf),
            pltpu.VMEM((F // 2 if split else 2 * F, F), bf),
            pltpu.VMEM((rows, F), bf),
            pltpu.VMEM((rows, F), bf),
            pltpu.SemaphoreType.DMA((rows // tm,)),
        ],
        out_shape=jax.ShapeDtypeStruct((rows, cols), bf),
        input_output_aliases=aliases,
        cost_estimate=pl.CostEstimate(
            flops=3 * rows * F * F, bytes_accessed=rows * F * 8 + F * F * 6, transcendentals=rows * F
        ),
        name="apply",
        compiler_params=room(24),
    )(*args)


def exchange(block, bit):
    size = lax.axis_size("seq")
    return lax.ppermute(block, "seq", [(i, i ^ (1 << bit)) for i in range(size)])


def shifted(block, by, skip=None):
    size = lax.axis_size("seq")
    route = [(i, i + by) for i in range(size) if 0 <= i + by < size and (i, i + by) != skip]
    return lax.ppermute(block, "seq", route)


def sent(block, source, target):
    return lax.ppermute(block, "seq", [(source, target)])


def synced(total, old, bits, position):
    offset = 0
    for bit in bits:
        half = total.shape[0] // 2
        mine = (position >> bit) & 1
        away = lax.dynamic_slice_in_dim(total, (1 - mine) * half, half, 0).astype(jnp.bfloat16)
        kept = lax.dynamic_slice_in_dim(total, mine * half, half, 0)
        total = kept + exchange(away, bit).astype(jnp.float32)
        offset = offset + mine * half
    part = renormed(lax.dynamic_slice_in_dim(old, offset, total.shape[0], 0), total)
    for bit in reversed(bits):
        mine = (position >> bit) & 1
        other = exchange(part, bit)
        part = jnp.concatenate(
            [jnp.where(mine == 0, part, other), jnp.where(mine == 0, other, part)], axis=0
        )
    return part


def synced_square(position, blocks, old):
    x, y = (position[0] >> 1) & 1, (position[0] >> 2) & 1
    keep_x, send_x, keep_y, send_y = blocks
    top0, bottom0 = exchange(send_x, 1), exchange(send_y, 2)

    def fold(a, b, at):
        n = a.shape[0] // 2
        a, b = (lax.dynamic_slice_in_dim(v, at * n, n, 0).astype(jnp.float32) for v in (a, b))
        return (a + b).astype(jnp.bfloat16)

    top1 = exchange(fold(keep_x, top0, 1 - y), 2)
    bottom1 = exchange(fold(keep_y, bottom0, 1 - x), 1)
    zero = lambda s: 0
    part = renorm_units(
        position,
        old,
        [(keep_x, at_y), (top0, at_y), (top1, zero)],
        [(keep_y, at_x), (bottom0, at_x), (bottom1, zero)],
    )
    n = top1.shape[0]
    over_x, over_y = exchange(part, 1), exchange(part, 2)
    top2, bottom2 = exchange(over_y[:n], 1), exchange(over_x[n:], 2)
    return [part, over_x, over_y, top2, bottom2]


def quarter(F, flip_x=0, flip_y=0):
    return lambda s: (2 * (at_x(s) ^ flip_x) + (at_y(s) ^ flip_y)) * (F // 4)


def shards(attn_q, attn_k, attn_v, fast_q, fast_k, fast_v, rates, fast_gate, fast_up, fast_down):
    position = lax.axis_index("seq").astype(jnp.int32).reshape(1)
    count = lax.axis_size("seq")
    heads = fast_gate.shape[0]
    rows = attn_q.shape[0]
    half = rows // 2
    width = 2 if attn_q.shape[1] // HD % 2 == 0 else 1
    square = heads == 2 and count == 8
    pack = lambda lo, hi: jnp.concatenate([attn_k[lo:hi], attn_v[lo:hi]], axis=0)
    guests = shifted(attn_q[:half], -1, (4, 3) if square else None)
    prev = shifted(pack(half, rows), 1)
    all_k, all_v = attn_k, attn_v
    rates_t = rates.T
    stay = lambda a: pltpu.with_memory_space_constraint(a, pltpu.HBM)
    attn_q, attn_k, attn_v = stay(attn_q), stay(attn_k), stay(attn_v)
    fast_k, fast_v = stay(fast_k), stay(fast_v)
    weights = (stay(fast_gate), stay(fast_up), stay(fast_down))

    def grads(head, received=None):
        return gradients(position, head, fast_k, fast_v, rates_t, *weights, received)

    if square:
        near, far = (lambda s: s[0] & 1), (lambda s: 1 - (s[0] & 1))
        theirs = grads(far)[0]
        received = exchange(theirs, 0)
        F = fast_gate.shape[1]
        mine = quarter(F)
        starts = [(F // 4, lambda s, at=i * F: at + mine(s)) for i in range(3)]
        old = turned(position, near, *weights, parts=tuple(starts))
        blocks = grads(near, received)
        pieces = synced_square(position, blocks, old)
        other = [exchange(p, 0) for p in pieces]
        news = []
        for head, new in ((near, pieces), (far, other)):
            news.append((head, hidden_part(position, head, fast_q, new), new))
    else:
        news = []
        bits = list(range(count.bit_length() - 1))
        for h in range(heads):
            head = lambda s, h=h: h
            old = turned(position, head, *weights)
            new = synced(grads(head)[0].astype(jnp.float32), old, bits, position[0])
            news.append((head, None, [new]))
    bq = min(256, half)
    tiles = half // bq
    late = [
        [(0, t * bq, half, 1), (1, 0, half + (t + 1) * bq, -1)] for t in range(tiles)
    ]
    early = [[(0, 0, (t + 1) * bq, -1)] for t in range(tiles)]
    guest = [[(0, t * bq, rows, 1)] for t in range(tiles)]
    here = (attn_k, 0, attn_v, 0, rows)
    returned, own_out, own_log = attention(position, [(guests, 0, guest, 2), (attn_q, 0, early, 1)], [here], bq, width)
    far_out = shifted(returned, 1, (3, 4) if square else None)
    (high,) = attention(position, [(attn_q, 1, late, 0)], [(prev, 0, prev, 1, half), here], bq, width)
    local, local_parts = None, ()
    if square:
        local = 4
        all_k, all_v, _ = lax.optimization_barrier((all_k, all_v, theirs))
        first = jnp.concatenate([all_k[:half], all_v[:half]], axis=0)
        first = sent(first, 3, 7)
        first = sent(first, 7, local)
        both = [[(0, t * bq, half, 1), (1, 0, half, 0)] for t in range(tiles)]
        local_parts = attention(
            position, [(attn_q, 0, both, 1)], [(first, 0, first, 1, half), (prev, 0, prev, 1, half)], bq, width, local
        )
    low = merged(position, own_out, far_out, own_log, width, local, local_parts)
    mixed = None
    for head, hidden, new in news:
        mixed = apply_head(position, head, fast_q, hidden, new, high, low, mixed)
    return mixed


def solution(mesh):
    placed = (P("seq", "head"),) * 7 + (P("head", None, None),) * 3
    return jax.shard_map(shards, mesh=mesh, in_specs=placed, out_specs=P("seq", "head"), check_vma=False)
```

```python
import functools
import math

import jax
import jax.numpy as jnp
from jax import lax
from jax.experimental import pallas as pl
from jax.experimental.pallas import tpu as pltpu
from jax.sharding import PartitionSpec as P


HD = 128
EPS = 1e-06
NN = (((1,), (0,)), ((), ()))
NT = (((1,), (1,)), ((), ()))
TN = (((0,), (0,)), ((), ()))


def room(mib):
    return pltpu.CompilerParams(vmem_limit_bytes=mib << 20)


def mm(a, b, dims=NN):
    return lax.dot_general(a, b, dims, preferred_element_type=jnp.float32)


def attn_kernel(position_ref, *refs, bq, jobs, sources, log_stride):
    queries = refs[: len(jobs)]
    keys = refs[len(jobs) : len(jobs) + sources]
    values = refs[len(jobs) + sources : len(jobs) + 2 * sources]
    rest = list(refs[len(jobs) + 2 * sources :])
    outs = []
    for _, sums in jobs:
        outs.append((rest.pop(0), rest.pop(0) if sums == 1 else None))
    bufs = (rest.pop(0), rest.pop(0))
    logs = [rest.pop(0) if sums else None for _, sums in jobs]
    group = pl.program_id(0)
    heads = queries[0].shape[1] // HD
    c = math.log2(math.e) / math.sqrt(HD)
    ri = lax.broadcasted_iota(jnp.int32, (bq, bq), 0)
    ci = lax.broadcasted_iota(jnp.int32, (bq, bq), 1)
    absent = position_ref[0] == 0
    units = [(h, j, t) for h in range(heads) for j in range(len(jobs)) for t in range(len(jobs[j][0]))]

    def scores(i):
        h, j, t = units[i]
        hs = slice(h * HD, (h + 1) * HD)
        buf = bufs[i % 2]
        q = queries[j][t * bq : (t + 1) * bq, hs]
        tops = []
        at = 0
        for source, lo, hi, edge in jobs[j][0][t]:
            s = mm(q, keys[source][lo:hi, hs], NT)
            n = hi - lo
            if edge == 1:
                kept = jnp.where(ci >= ri, s[:, :bq], -jnp.inf)
                s = jnp.concatenate([kept, s[:, bq:]], axis=1) if n > bq else kept
            elif edge == -1:
                kept = jnp.where(ci <= ri, s[:, n - bq :], -jnp.inf)
                s = jnp.concatenate([s[:, : n - bq], kept], axis=1) if n > bq else kept
            buf[:, at : at + n] = s
            tops.append(jnp.max(s, axis=1, keepdims=True))
            at += n
        if len(tops) == 1:
            return [tops[0] * c]
        m = jnp.maximum(tops[1], jnp.where(absent, -jnp.inf, tops[0])) * c
        return [jnp.where(absent, 1e30, m), m]

    def finish(i, ms):
        h, j, t = units[i]
        plan, sums = jobs[j]
        hs = slice(h * HD, (h + 1) * HD)
        buf = bufs[i % 2]
        out = total = None
        at = 0
        for (source, lo, hi, _), m in zip(plan[t], ms):
            p = jnp.exp2(buf[:, at : at + hi - lo] * c - m)
            part = jnp.sum(p, axis=1, keepdims=True)
            o = mm(p.astype(jnp.bfloat16), values[source][lo:hi, hs])
            total = part if total is None else total + part
            out = o if out is None else out + o
            at += hi - lo
        rows = slice(t * bq, (t + 1) * bq)
        out = (out / total).astype(jnp.bfloat16)
        head = group * heads + h
        if sums == 2:
            outs[j][0][rows, pl.ds(pl.multiple_of(head * HD, HD), HD)] = out
        else:
            outs[j][0][rows, hs] = out
        if sums:
            lane = lax.broadcasted_iota(jnp.int32, (bq, HD), 1)
            log = ms[-1] + jnp.log(total) * math.log2(math.e)
            logs[j][rows, :] = jnp.where(lane == head, log, logs[j][rows, :])

    if any(sums for _, sums in jobs):

        @pl.when(group == 0)
        def _():
            for log in logs:
                if log is not None:
                    log[...] = jnp.zeros(log.shape, log.dtype)

    ms = scores(0)
    for i in range(len(units)):
        nxt = scores(i + 1) if i + 1 < len(units) else None
        finish(i, ms)
        ms = nxt
    if any(sums for _, sums in jobs):

        @pl.when(group == pl.num_programs(0) - 1)
        def _():
            for (_, sums), (out, log_out), log in zip(jobs, outs, logs):
                if sums == 1:
                    log_out[...] = log[...]
                if sums == 2:
                    x = log[...]
                    a = x.astype(jnp.bfloat16).astype(jnp.float32)
                    b = (x - a).astype(jnp.bfloat16).astype(jnp.float32)
                    x = a + pltpu.roll(b, log_stride, 1) + pltpu.roll(x - a - b, 2 * log_stride, 1)
                    out[:, out.shape[1] - HD :] = x.astype(jnp.bfloat16)


def log_stride_of(cols):
    return 16 * pl.cdiv(cols // HD, 16)


def attention(position, jobs, sources, bq, width):
    cols = jobs[0][0].shape[1]
    w = width * HD
    ranges = [r for _, _, plan, _ in jobs for tile in plan for r in tile]
    span = max(sum(hi - lo for _, lo, hi, _ in tile) for _, _, plan, _ in jobs for tile in plan)
    pairs = bq * sum(hi - lo for _, lo, hi, _ in ranges) * cols // HD
    block = lambda n, at: pl.BlockSpec((n, w), lambda g, f: (at, g))
    whole = lambda *shape: pl.BlockSpec(shape, lambda g, f: (0, 0))
    outs, out_specs, logs = [], [], []
    for _, _, plan, sums in jobs:
        rows = len(plan) * bq
        if sums == 2:
            outs.append(jax.ShapeDtypeStruct((rows, cols + HD), jnp.bfloat16))
            out_specs.append(whole(rows, cols + HD))
        else:
            outs.append(jax.ShapeDtypeStruct((rows, cols), jnp.bfloat16))
            out_specs.append(block(rows, 0))
        if sums == 1:
            outs.append(jax.ShapeDtypeStruct((rows, HD), jnp.float32))
            out_specs.append(whole(rows, HD))
        if sums:
            logs.append(pltpu.VMEM((rows, HD), jnp.float32))
    specs = [block(len(plan) * bq, at) for _, at, plan, _ in jobs]
    specs += [block(n, at) for _, at, _, _, n in sources] + [block(n, at) for _, _, _, at, n in sources]
    kernel = functools.partial(
        attn_kernel,
        bq=bq,
        jobs=[(plan, sums) for _, _, plan, sums in jobs],
        sources=len(sources),
        log_stride=log_stride_of(cols),
    )
    return pl.pallas_call(
        kernel,
        grid_spec=pltpu.PrefetchScalarGridSpec(
            num_scalar_prefetch=1,
            grid=(cols // w,),
            in_specs=specs,
            out_specs=out_specs,
            scratch_shapes=[pltpu.VMEM((bq, span), jnp.float32)] * 2 + logs,
        ),
        out_shape=outs,
        cost_estimate=pl.CostEstimate(
            flops=4 * pairs * HD, bytes_accessed=8 * bq * cols * len(ranges), transcendentals=pairs
        ),
        compiler_params=room(14),
    )(position, *[job[0] for job in jobs], *[x[0] for x in sources], *[x[2] for x in sources])


def owned_rows(F):
    n, m, half = F // 4, F // 8, 3 * F // 2
    unit = 3 * F // 8
    segments = []
    for k in range(4):
        upper, lower = k * unit, half + (2 * (k % 2) + k // 2) * unit
        segments += [
            (k * n, (k + 1) * n, upper),
            (F + k * n, F + k * n + m, upper + n),
            (F + k * n + m, F + (k + 1) * n, lower),
            (2 * F + k * n, 2 * F + (k + 1) * n, lower + m),
        ]
    return segments


def at_x(s):
    return (s[0] >> 1) & 1


def at_y(s):
    return (s[0] >> 2) & 1


def grad_kernel(s_ref, x_ref, v_ref, r_ref, w1_ref, w3_ref, w2_ref, *refs, head, tm, tn, split):
    w13, w2, gu, hid, og = refs[-5:]
    F = w1_ref.shape[2]
    rows = x_ref.shape[0]
    w13[:, :F] = w1_ref[0].astype(jnp.bfloat16)
    w13[:, F:] = w3_ref[0].astype(jnp.bfloat16)
    w2[...] = w2_ref[0].astype(jnp.bfloat16)
    pick = lax.broadcasted_iota(jnp.int32, r_ref.shape, 0) == head(s_ref)
    rate = jnp.sum(jnp.where(pick, r_ref[...], 0.0), axis=0, keepdims=True)
    rate = jnp.transpose(jnp.broadcast_to(rate, (8, rows)))[:, :1]
    og[...] = (-rate * v_ref[...].astype(jnp.float32)).astype(jnp.bfloat16)
    n = rows // tm

    def products(i):
        r = slice(i * tm, (i + 1) * tm)
        return mm(x_ref[r, :], w13[...]), mm(og[r, :], w2[...], NT)

    def finish(i, pre, hg):
        r = slice(i * tm, (i + 1) * tm)
        pg, pu = pre[:, :F], pre[:, F:]
        sg = jax.nn.sigmoid(pg)
        act = pg * sg
        gu[r, :F] = (hg * pu * (sg * (1.0 + pg * (1.0 - sg)))).astype(jnp.bfloat16)
        gu[r, F:] = (hg * act).astype(jnp.bfloat16)
        hid[r, :] = (act * pu).astype(jnp.bfloat16)

    cur = products(0)
    for i in range(n):
        nxt = products(i + 1) if i + 1 < n else None
        finish(i, *cur)
        cur = nxt
    x = x_ref[...]
    hd = hid[...]
    x1, y1 = at_x(s_ref), at_y(s_ref)
    block_rows = 3 * F // 4
    segments = owned_rows(F) if split else []

    def put(lo, grad):
        if not split:
            refs[0][lo : lo + grad.shape[0], :] = grad.astype(refs[0].dtype)
            return
        grad = grad + refs[0][lo : lo + grad.shape[0], :].astype(jnp.float32)
        for a, b, to in segments:
            a, b, to = max(lo, a), min(lo + grad.shape[0], b), to + max(lo - a, 0)
            if a < b:
                block, row = divmod(to, block_rows)
                slot = jnp.where((x1 if block < 2 else y1) == block % 2, 0, 1)
                part = grad[a - lo : b - lo].astype(jnp.bfloat16)
                refs[1 + block // 2][slot, row : row + b - a, :] = part

    for j in range(2 * F // tn):
        put(j * tn, mm(gu[:, j * tn : (j + 1) * tn], x, TN))
    for j in range(F // HD):
        put(2 * F + j * HD, mm(og[:, j * HD : (j + 1) * HD], hd, TN))
    if split:
        for o in range(2):
            refs[3 + 2 * o][...] = refs[1 + o][0]
            refs[4 + 2 * o][...] = refs[1 + o][1]


def gradients(position, head, fk, fv, rates_t, w1, w3, w2, received=None):
    rows = fk.shape[0]
    F = w1.shape[1]
    tm = min(256, rows)
    tn = 256 if 2 * F % 256 == 0 else HD
    once = dict(pipeline_mode=pl.Buffered(1))
    col = pl.BlockSpec((rows, F), lambda i, s: (0, head(s)), **once)
    weight = pl.BlockSpec((1, F, F), lambda i, s: (head(s), 0, 0), **once)
    whole = lambda *shape: pl.BlockSpec(shape, lambda i, s: (0,) * len(shape), **once)
    bf = jnp.bfloat16
    args = [position, fk, fv, rates_t, w1, w3, w2]
    specs = [col, col, whole(*rates_t.shape), weight, weight, weight]
    scratch = [
        pltpu.VMEM((F, 2 * F), bf),
        pltpu.VMEM((F, F), bf),
        pltpu.VMEM((rows, 2 * F), bf),
        pltpu.VMEM((rows, F), bf),
        pltpu.VMEM((rows, F), bf),
    ]
    if received is None:
        shapes = [(3 * F, F)]
    else:
        shapes = [(3 * F // 4, F)] * 4
        args.append(received)
        specs.append(whole(3 * F, F))
        scratch = [pltpu.VMEM((2, 3 * F // 4, F), bf)] * 2 + scratch
    kernel = functools.partial(grad_kernel, head=head, tm=tm, tn=tn, split=received is not None)

    def body(*refs):
        if received is None:
            return kernel(*refs)
        ins, outs, halves, rest = refs[:8], refs[8:12], refs[12:14], refs[14:]
        return kernel(*ins, *halves, *outs, *rest)

    return pl.pallas_call(
        body,
        grid_spec=pltpu.PrefetchScalarGridSpec(
            num_scalar_prefetch=1,
            grid=(1,),
            in_specs=specs,
            out_specs=[whole(*shape) for shape in shapes],
            scratch_shapes=scratch,
        ),
        out_shape=[jax.ShapeDtypeStruct(shape, bf) for shape in shapes],
        cost_estimate=pl.CostEstimate(
            flops=12 * rows * F * F, bytes_accessed=rows * F * 4 + F * F * 18, transcendentals=rows * F
        ),
        name="grads",
        compiler_params=room(40 if received is None else 36),
    )(*args)


def turn_kernel(s_ref, w1, w3, w2, o_ref, *scratch, parts):
    F = w1.shape[2]
    all_ref = scratch[0] if scratch else o_ref
    all_ref[:F, :] = w1[0].T
    all_ref[F : 2 * F, :] = w3[0].T
    all_ref[2 * F :, :] = w2[0].T
    at = 0
    for n, start in parts:
        o_ref[at : at + n, :] = all_ref[pl.ds(pl.multiple_of(start(s_ref), 8), n), :]
        at += n


def turned(position, head, w1, w3, w2, parts=()):
    F = w1.shape[1]
    weight = pl.BlockSpec((1, F, F), lambda i, s: (head(s), 0, 0))
    shape = (sum(n for n, _ in parts), F) if parts else (3 * F, F)
    return pl.pallas_call(
        functools.partial(turn_kernel, parts=parts),
        grid_spec=pltpu.PrefetchScalarGridSpec(
            num_scalar_prefetch=1,
            grid=(1,),
            in_specs=[weight] * 3,
            out_specs=pl.BlockSpec(shape, lambda i, s: (0, 0)),
            scratch_shapes=[pltpu.VMEM((3 * F, F), jnp.float32)] if parts else [],
        ),
        out_shape=jax.ShapeDtypeStruct(shape, jnp.float32),
        cost_estimate=pl.CostEstimate(flops=3 * F * F, bytes_accessed=24 * F * F, transcendentals=0),
        name="turned",
        compiler_params=room(20),
    )(position, w1, w3, w2)


def renormed(old, grad):
    new = old - grad
    old_sq = jnp.sum(old * old, axis=-1, keepdims=True)
    new_sq = jnp.sum(new * new, axis=-1, keepdims=True)
    return (new * (jnp.sqrt(old_sq) / jnp.sqrt(new_sq + EPS))).astype(jnp.bfloat16)


def renorm_kernel(s_ref, old_ref, *refs):
    out = refs[-1]
    at = 0
    for i in range(2):
        a, b, c = (ref[...].astype(jnp.float32) for ref in refs[3 * i : 3 * i + 3])
        rows = slice(at, at + a.shape[0])
        out[rows, :] = renormed(old_ref[rows, :], a + b + c)
        at += a.shape[0]


def renorm_units(position, old, upper, lower):
    rows, F = old.shape
    specs = [pl.BlockSpec((rows, F), lambda i, s: (0, 0))]
    for group in (upper, lower):
        size = group[2][0].shape[0]
        specs += [pl.BlockSpec((size, F), lambda i, s, at=at: (at(s), 0)) for _, at in group]
    return pl.pallas_call(
        renorm_kernel,
        grid_spec=pltpu.PrefetchScalarGridSpec(
            num_scalar_prefetch=1,
            grid=(1,),
            in_specs=specs,
            out_specs=pl.BlockSpec((rows, F), lambda i, s: (0, 0)),
        ),
        out_shape=jax.ShapeDtypeStruct((rows, F), jnp.bfloat16),
        cost_estimate=pl.CostEstimate(flops=10 * rows * F, bytes_accessed=12 * rows * F, transcendentals=0),
        name="renorm",
        compiler_params=room(12),
    )(position, old, *[array for array, _ in upper + lower])


def merge_kernel(s_ref, own_ref, far_ref, own_log, far_log, o_ref, *, stride):
    lane = lax.broadcasted_iota(jnp.int32, own_log.shape, 1)
    heads = o_ref.shape[1] // HD
    for j in range(heads):
        cs = slice(j * HD, (j + 1) * HD)
        at = pl.program_id(0) * heads + j
        pick = lambda ref, of: jnp.sum(
            jnp.where(of, ref[...].astype(jnp.float32), 0.0), axis=1, keepdims=True
        )
        own = pick(own_log, lane == at)
        far = pick(far_log, (lane == at) | (lane == at + stride) | (lane == at + 2 * stride))
        far = jnp.where(s_ref[0] == 0, -jnp.inf, far)
        top = jnp.maximum(own, far)
        own, far = jnp.exp2(own - top), jnp.exp2(far - top)
        share = own / (own + far)
        a, b = own_ref[:, cs].astype(jnp.float32), far_ref[:, cs].astype(jnp.float32)
        o_ref[:, cs] = (a * share + b * (1.0 - share)).astype(o_ref.dtype)


def merged(position, own, far, own_log, width, tile):
    rows, cols = far.shape[0], own.shape[1]
    w = width * HD
    mine = pl.BlockSpec((rows, w), lambda g, s: (tile, g))
    col = pl.BlockSpec((rows, w), lambda g, s: (0, g))
    own_logs = pl.BlockSpec((rows, HD), lambda g, s: (tile, 0))
    far_logs = pl.BlockSpec((rows, HD), lambda g, s: (0, cols // HD))
    return pl.pallas_call(
        functools.partial(merge_kernel, stride=log_stride_of(cols)),
        grid_spec=pltpu.PrefetchScalarGridSpec(
            num_scalar_prefetch=1,
            grid=(cols // w,),
            in_specs=[mine, col, own_logs, far_logs],
            out_specs=col,
        ),
        out_shape=jax.ShapeDtypeStruct((rows, cols), jnp.bfloat16),
        cost_estimate=pl.CostEstimate(
            flops=8 * rows * cols, bytes_accessed=6 * rows * cols, transcendentals=rows * cols // HD
        ),
        name="merge",
        compiler_params=room(8),
    )(position, own, far, own_log, far)


def gated(h, n):
    g = h[:, :n]
    return (g * jax.nn.sigmoid(g) * h[:, n:]).astype(jnp.bfloat16)


def staggered(n, first, second):
    cur = first(0)
    for i in range(n):
        nxt = first(i + 1) if i + 1 < n else None
        second(i, cur)
        cur = nxt


def for_each_chip(s_ref, body):
    chip = 2 * at_x(s_ref) + at_y(s_ref)
    for k in range(4):
        pl.when(chip == k)(functools.partial(body, k))


NEIGHBOURS = (0, 2, 1, 3)


def hidden_kernel(s_ref, q_ref, own_ref, over_x, over_y, o_ref, w_ref, *, tm, head):
    F = own_ref.shape[1]
    n = F // 4
    for i, ref in enumerate((own_ref, over_x, over_y)):
        w_ref[i * n : (i + 1) * n, :] = ref[:n, :]
        w_ref[(3 + i) * n : (4 + i) * n, :] = ref[n : 2 * n, :]
    cols = pl.ds(pl.multiple_of(head(s_ref) * F, HD), F)

    def first(i):
        return mm(q_ref[i * tm : (i + 1) * tm, cols], w_ref[...], NT)

    def second(i, h):
        o_ref[i * tm : (i + 1) * tm, : 3 * n] = gated(h, 3 * n)

    staggered(q_ref.shape[0] // tm, first, second)


VMEM = pl.BlockSpec(memory_space=pltpu.VMEM)
SMEM = pl.BlockSpec(memory_space=pltpu.SMEM)
ANY = pl.BlockSpec(memory_space=pl.ANY)


def hidden_part(position, head, fq, pieces):
    rows = fq.shape[0]
    F = pieces[0].shape[1]
    bf = jnp.bfloat16
    return pl.pallas_call(
        functools.partial(hidden_kernel, tm=min(256, rows), head=head),
        in_specs=[SMEM] + [VMEM] * 4,
        out_specs=VMEM,
        scratch_shapes=[pltpu.VMEM((3 * F // 2, F), bf)],
        out_shape=jax.ShapeDtypeStruct((rows, F), bf),
        cost_estimate=pl.CostEstimate(
            flops=3 * rows * F * F, bytes_accessed=rows * F * 4 + F * F * 3, transcendentals=rows * F
        ),
        name="hidden",
        compiler_params=room(24),
    )(position, fq, *pieces[:3])


def apply_kernel(s_ref, q_ref, *rest, tm, head, split, tiles, sources):
    attended, rest = rest[:sources], rest[sources:]
    o_ref, n_ref, w_ref, h_ref, r_ref, sems = rest[-6:]
    F = n_ref.shape[1]
    n, m = F // 4, F // 8
    cols = pl.ds(pl.multiple_of(head(s_ref) * F, HD), F)
    if split:
        own, over_x, over_y, upper, lower = rest[1:6]
        w_ref[: n + m, :] = upper[...]
        w_ref[n + m :, :] = lower[:m, :]
    else:
        w_ref[...] = rest[0][: 2 * F, :]
        n_ref[...] = rest[0][2 * F :, :]

    def copy_out(i):
        to = pl.ds(tiles[i][0] * tm, tm)
        return pltpu.make_async_copy(r_ref.at[pl.ds(i * tm, tm), :], o_ref.at[to, cols], sems.at[i])

    def place(k):
        rows_of = ((own, 2 * n), (over_x, 2 * n), (over_y, 2 * n), (lower, m))
        for flip, (ref, row) in zip(NEIGHBOURS, rows_of):
            for j, from_flip in enumerate(NEIGHBOURS):
                to, at = (k ^ flip) * n, (k ^ from_flip) * n
                n_ref[to : to + n, j * n : (j + 1) * n] = ref[row : row + n, at : at + n]

    if split:
        for_each_chip(s_ref, place)

    def first(i):
        at = tiles[i][0] * tm
        return mm(q_ref[at : at + tm, cols], w_ref[...], NT)

    def second(i, h):
        tile, source, at = tiles[i]
        r = slice(i * tm, (i + 1) * tm)
        if split:
            h_ref[r, : 3 * n] = rest[0][tile * tm : (tile + 1) * tm, : 3 * n]
            h_ref[r, 3 * n :] = gated(h, n)
            hid = h_ref[r, :]
        else:
            hid = gated(h, F)
        a = attended[source][at : at + tm, cols].astype(jnp.float32)
        r_ref[r, :] = (a + mm(hid, n_ref[...], NT)).astype(r_ref.dtype)
        copy_out(i).start()

    staggered(len(tiles), first, second)
    for i in range(len(tiles)):
        copy_out(i).wait()


def apply_head(position, head, fq, hidden, pieces, attended, tiles, tm, into=None):
    rows, cols = fq.shape
    F = pieces[0].shape[1]
    split = hidden is not None
    args = [position, fq, *attended] + ([hidden] if split else []) + list(pieces)
    specs = [SMEM] + [VMEM] * (len(args) - 1)
    aliases = {}
    if into is not None:
        aliases = {len(args): 0}
        args.append(into)
        specs.append(ANY)
    bf = jnp.bfloat16
    mine = len(tiles) * tm
    return pl.pallas_call(
        functools.partial(
            apply_kernel, tm=tm, head=head, split=split, tiles=tiles, sources=len(attended)
        ),
        in_specs=specs,
        out_specs=ANY,
        scratch_shapes=[
            pltpu.VMEM((F, F), bf),
            pltpu.VMEM((F // 2 if split else 2 * F, F), bf),
            pltpu.VMEM((mine, F), bf),
            pltpu.VMEM((mine, F), bf),
            pltpu.SemaphoreType.DMA((len(tiles),)),
        ],
        out_shape=jax.ShapeDtypeStruct((rows, cols), bf),
        input_output_aliases=aliases,
        cost_estimate=pl.CostEstimate(
            flops=3 * mine * F * F, bytes_accessed=mine * F * 8 + F * F * 6, transcendentals=mine * F
        ),
        name="apply",
        compiler_params=room(24),
    )(*args)


def exchange(block, bit):
    size = lax.axis_size("seq")
    return lax.ppermute(block, "seq", [(i, i ^ (1 << bit)) for i in range(size)])


def shifted(block, by):
    size = lax.axis_size("seq")
    return lax.ppermute(block, "seq", [(i, i + by) for i in range(size) if 0 <= i + by < size])


def synced(total, old, bits, position):
    offset = 0
    for bit in bits:
        half = total.shape[0] // 2
        mine = (position >> bit) & 1
        away = lax.dynamic_slice_in_dim(total, (1 - mine) * half, half, 0).astype(jnp.bfloat16)
        kept = lax.dynamic_slice_in_dim(total, mine * half, half, 0)
        total = kept + exchange(away, bit).astype(jnp.float32)
        offset = offset + mine * half
    part = renormed(lax.dynamic_slice_in_dim(old, offset, total.shape[0], 0), total)
    for bit in reversed(bits):
        mine = (position >> bit) & 1
        other = exchange(part, bit)
        part = jnp.concatenate(
            [jnp.where(mine == 0, part, other), jnp.where(mine == 0, other, part)], axis=0
        )
    return part


def synced_square(position, blocks, old):
    x, y = (position[0] >> 1) & 1, (position[0] >> 2) & 1
    keep_x, send_x, keep_y, send_y = blocks
    top0, bottom0 = exchange(send_x, 1), exchange(send_y, 2)

    def fold(a, b, at):
        n = a.shape[0] // 2
        a, b = (lax.dynamic_slice_in_dim(v, at * n, n, 0).astype(jnp.float32) for v in (a, b))
        return (a + b).astype(jnp.bfloat16)

    top1 = exchange(fold(keep_x, top0, 1 - y), 2)
    bottom1 = exchange(fold(keep_y, bottom0, 1 - x), 1)
    zero = lambda s: 0
    part = renorm_units(
        position,
        old,
        [(keep_x, at_y), (top0, at_y), (top1, zero)],
        [(keep_y, at_x), (bottom0, at_x), (bottom1, zero)],
    )
    n = top1.shape[0]
    over_x, over_y = exchange(part, 1), exchange(part, 2)
    top2, bottom2 = exchange(over_y[:n], 1), exchange(over_x[n:], 2)
    return [part, over_x, over_y, top2, bottom2]


def quarter(F, flip_x=0, flip_y=0):
    return lambda s: (2 * (at_x(s) ^ flip_x) + (at_y(s) ^ flip_y)) * (F // 4)


def shards(attn_q, attn_k, attn_v, fast_q, fast_k, fast_v, rates, fast_gate, fast_up, fast_down):
    position = lax.axis_index("seq").astype(jnp.int32).reshape(1)
    count = lax.axis_size("seq")
    heads = fast_gate.shape[0]
    rows = attn_q.shape[0]
    half = rows // 2
    width = 2 if attn_q.shape[1] // HD % 2 == 0 else 1
    prev = shifted(jnp.concatenate([attn_k[half:], attn_v[half:]], axis=0), 1)
    guests = shifted(attn_q[:half], -1)
    rates_t = rates.T
    stay = lambda a: pltpu.with_memory_space_constraint(a, pltpu.HBM)
    attn_q, attn_k, attn_v = stay(attn_q), stay(attn_k), stay(attn_v)
    fast_k, fast_v = stay(fast_k), stay(fast_v)
    weights = (stay(fast_gate), stay(fast_up), stay(fast_down))

    def grads(head, received=None):
        return gradients(position, head, fast_k, fast_v, rates_t, *weights, received)

    if heads == 2 and count == 8:
        near, far = (lambda s: s[0] & 1), (lambda s: 1 - (s[0] & 1))
        received = exchange(grads(far)[0], 0)
        F = fast_gate.shape[1]
        mine = quarter(F)
        starts = [(F // 4, lambda s, at=i * F: at + mine(s)) for i in range(3)]
        old = turned(position, near, *weights, parts=tuple(starts))
        blocks = grads(near, received)
        pieces = synced_square(position, blocks, old)
        other = [exchange(p, 0) for p in pieces]
        news = []
        for head, new in ((near, pieces), (far, other)):
            news.append((head, hidden_part(position, head, fast_q, new), new))
    else:
        news = []
        bits = list(range(count.bit_length() - 1))
        for h in range(heads):
            head = lambda s, h=h: h
            old = turned(position, head, *weights)
            new = synced(grads(head)[0].astype(jnp.float32), old, bits, position[0])
            news.append((head, None, [new]))
    bq = min(256, half)
    tiles = half // bq
    late = [
        [(0, t * bq, half, 1), (1, 0, half + (t + 1) * bq, -1)] for t in range(tiles)
    ]
    early = [[(0, 0, (t + 1) * bq, -1)] for t in range(tiles)]
    guest = [[(0, t * bq, rows, 1)] for t in range(tiles)]
    here = (attn_k, 0, attn_v, 0, rows)
    jobs = [(guests, t, guest[t : t + 1], 2) for t in range(tiles)] + [(attn_q, 0, early, 1)]
    *returned, own_out, own_log = attention(position, jobs, [here], bq, width)
    far_outs = [shifted(part, 1) for part in returned]
    (high,) = attention(position, [(attn_q, 1, late, 0)], [(prev, 0, prev, 1, half), here], bq, width)
    lows = []
    for t, part in enumerate(far_outs):
        lows.append(merged(position, own_out, part, own_log, width, t))
    soon = [(t, t, 0) for t in range(tiles - 1)] + [(tiles + t, tiles - 1, t * bq) for t in range(tiles)]
    mixed = None
    for attended, rows_of in (([*lows[:-1], high], soon), (lows[-1:], [(tiles - 1, 0, 0)])):
        for head, hidden, new in news:
            mixed = apply_head(position, head, fast_q, hidden, new, attended, rows_of, bq, mixed)
    return mixed


def solution(mesh):
    placed = (P("seq", "head"),) * 7 + (P("head", None, None),) * 3
    return jax.shard_map(shards, mesh=mesh, in_specs=placed, out_specs=P("seq", "head"), check_vma=False)
```

```python
import functools
import math

import jax
import jax.numpy as jnp
from jax import lax
from jax.experimental import pallas as pl
from jax.experimental.pallas import tpu as pltpu
from jax.sharding import PartitionSpec as P


HD = 128
EPS = 1e-06
NN = (((1,), (0,)), ((), ()))
NT = (((1,), (1,)), ((), ()))
TN = (((0,), (0,)), ((), ()))


def room(mib):
    return pltpu.CompilerParams(vmem_limit_bytes=mib << 20)


def mm(a, b, dims=NN):
    return lax.dot_general(a, b, dims, preferred_element_type=jnp.float32)


def attn_kernel(position_ref, *refs, bq, jobs, sources, log_stride):
    queries = refs[: len(jobs)]
    keys = refs[len(jobs) : len(jobs) + sources]
    values = refs[len(jobs) + sources : len(jobs) + 2 * sources]
    rest = list(refs[len(jobs) + 2 * sources :])
    outs = []
    for _, sums in jobs:
        outs.append((rest.pop(0), rest.pop(0) if sums == 1 else None))
    bufs = (rest.pop(0), rest.pop(0))
    logs = [rest.pop(0) if sums else None for _, sums in jobs]
    group = pl.program_id(0)
    heads = queries[0].shape[1] // HD
    c = math.log2(math.e) / math.sqrt(HD)
    ri = lax.broadcasted_iota(jnp.int32, (bq, bq), 0)
    ci = lax.broadcasted_iota(jnp.int32, (bq, bq), 1)
    absent = position_ref[0] == 0
    units = [(h, j, t) for h in range(heads) for j in range(len(jobs)) for t in range(len(jobs[j][0]))]

    def scores(i):
        h, j, t = units[i]
        hs = slice(h * HD, (h + 1) * HD)
        buf = bufs[i % 2]
        q = queries[j][t * bq : (t + 1) * bq, hs]
        tops = []
        at = 0
        for source, lo, hi, edge in jobs[j][0][t]:
            s = mm(q, keys[source][lo:hi, hs], NT)
            n = hi - lo
            if edge == 1:
                kept = jnp.where(ci >= ri, s[:, :bq], -jnp.inf)
                s = jnp.concatenate([kept, s[:, bq:]], axis=1) if n > bq else kept
            elif edge == -1:
                kept = jnp.where(ci <= ri, s[:, n - bq :], -jnp.inf)
                s = jnp.concatenate([s[:, : n - bq], kept], axis=1) if n > bq else kept
            buf[:, at : at + n] = s
            tops.append(jnp.max(s, axis=1, keepdims=True))
            at += n
        if len(tops) == 1:
            return [tops[0] * c]
        m = jnp.maximum(tops[1], jnp.where(absent, -jnp.inf, tops[0])) * c
        return [jnp.where(absent, 1e30, m), m]

    def finish(i, ms):
        h, j, t = units[i]
        plan, sums = jobs[j]
        hs = slice(h * HD, (h + 1) * HD)
        buf = bufs[i % 2]
        out = total = None
        at = 0
        for (source, lo, hi, _), m in zip(plan[t], ms):
            p = jnp.exp2(buf[:, at : at + hi - lo] * c - m)
            part = jnp.sum(p, axis=1, keepdims=True)
            o = mm(p.astype(jnp.bfloat16), values[source][lo:hi, hs])
            total = part if total is None else total + part
            out = o if out is None else out + o
            at += hi - lo
        rows = slice(t * bq, (t + 1) * bq)
        out = (out / total).astype(jnp.bfloat16)
        head = group * heads + h
        if sums == 2:
            outs[j][0][rows, pl.ds(pl.multiple_of(head * HD, HD), HD)] = out
        else:
            outs[j][0][rows, hs] = out
        if sums:
            lane = lax.broadcasted_iota(jnp.int32, (bq, HD), 1)
            log = ms[-1] + jnp.log(total) * math.log2(math.e)
            logs[j][rows, :] = jnp.where(lane == head, log, logs[j][rows, :])

    if any(sums for _, sums in jobs):

        @pl.when(group == 0)
        def _():
            for log in logs:
                if log is not None:
                    log[...] = jnp.zeros(log.shape, log.dtype)

    ms = scores(0)
    for i in range(len(units)):
        nxt = scores(i + 1) if i + 1 < len(units) else None
        finish(i, ms)
        ms = nxt
    if any(sums for _, sums in jobs):

        @pl.when(group == pl.num_programs(0) - 1)
        def _():
            for (_, sums), (out, log_out), log in zip(jobs, outs, logs):
                if sums == 1:
                    log_out[...] = log[...]
                if sums == 2:
                    x = log[...]
                    a = x.astype(jnp.bfloat16).astype(jnp.float32)
                    b = (x - a).astype(jnp.bfloat16).astype(jnp.float32)
                    x = a + pltpu.roll(b, log_stride, 1) + pltpu.roll(x - a - b, 2 * log_stride, 1)
                    out[:, out.shape[1] - HD :] = x.astype(jnp.bfloat16)


def log_stride_of(cols):
    return 16 * pl.cdiv(cols // HD, 16)


def attention(position, jobs, sources, bq, width):
    cols = jobs[0][0].shape[1]
    w = width * HD
    ranges = [r for _, _, plan, _ in jobs for tile in plan for r in tile]
    span = max(sum(hi - lo for _, lo, hi, _ in tile) for _, _, plan, _ in jobs for tile in plan)
    pairs = bq * sum(hi - lo for _, lo, hi, _ in ranges) * cols // HD
    block = lambda n, at: pl.BlockSpec((n, w), lambda g, f: (at, g))
    whole = lambda *shape: pl.BlockSpec(shape, lambda g, f: (0, 0))
    outs, out_specs, logs = [], [], []
    for _, _, plan, sums in jobs:
        rows = len(plan) * bq
        if sums == 2:
            outs.append(jax.ShapeDtypeStruct((rows, cols + HD), jnp.bfloat16))
            out_specs.append(whole(rows, cols + HD))
        else:
            outs.append(jax.ShapeDtypeStruct((rows, cols), jnp.bfloat16))
            out_specs.append(block(rows, 0))
        if sums == 1:
            outs.append(jax.ShapeDtypeStruct((rows, HD), jnp.float32))
            out_specs.append(whole(rows, HD))
        if sums:
            logs.append(pltpu.VMEM((rows, HD), jnp.float32))
    specs = [block(len(plan) * bq, at) for _, at, plan, _ in jobs]
    specs += [block(n, at) for _, at, _, _, n in sources] + [block(n, at) for _, _, _, at, n in sources]
    kernel = functools.partial(
        attn_kernel,
        bq=bq,
        jobs=[(plan, sums) for _, _, plan, sums in jobs],
        sources=len(sources),
        log_stride=log_stride_of(cols),
    )
    return pl.pallas_call(
        kernel,
        grid_spec=pltpu.PrefetchScalarGridSpec(
            num_scalar_prefetch=1,
            grid=(cols // w,),
            in_specs=specs,
            out_specs=out_specs,
            scratch_shapes=[pltpu.VMEM((bq, span), jnp.float32)] * 2 + logs,
        ),
        out_shape=outs,
        cost_estimate=pl.CostEstimate(
            flops=4 * pairs * HD, bytes_accessed=8 * bq * cols * len(ranges), transcendentals=pairs
        ),
        compiler_params=room(14),
    )(position, *[job[0] for job in jobs], *[x[0] for x in sources], *[x[2] for x in sources])


def owned_rows(F):
    n, m, half = F // 4, F // 8, 3 * F // 2
    unit = 3 * F // 8
    segments = []
    for k in range(4):
        upper, lower = k * unit, half + (2 * (k % 2) + k // 2) * unit
        segments += [
            (k * n, (k + 1) * n, upper),
            (F + k * n, F + k * n + m, upper + n),
            (F + k * n + m, F + (k + 1) * n, lower),
            (2 * F + k * n, 2 * F + (k + 1) * n, lower + m),
        ]
    return segments


def at_x(s):
    return (s[0] >> 1) & 1


def at_y(s):
    return (s[0] >> 2) & 1


def grad_kernel(s_ref, x_ref, v_ref, r_ref, w1_ref, w3_ref, w2_ref, *refs, head, tm, tn, split):
    w13, w2, gu, hid, og = refs[-5:]
    F = w1_ref.shape[2]
    rows = x_ref.shape[0]
    w13[:, :F] = w1_ref[0].astype(jnp.bfloat16)
    w13[:, F:] = w3_ref[0].astype(jnp.bfloat16)
    w2[...] = w2_ref[0].astype(jnp.bfloat16)
    pick = lax.broadcasted_iota(jnp.int32, r_ref.shape, 0) == head(s_ref)
    rate = jnp.sum(jnp.where(pick, r_ref[...], 0.0), axis=0, keepdims=True)
    rate = jnp.transpose(jnp.broadcast_to(rate, (8, rows)))[:, :1]
    og[...] = (-rate * v_ref[...].astype(jnp.float32)).astype(jnp.bfloat16)
    n = rows // tm

    def products(i):
        r = slice(i * tm, (i + 1) * tm)
        return mm(x_ref[r, :], w13[...]), mm(og[r, :], w2[...], NT)

    def finish(i, pre, hg):
        r = slice(i * tm, (i + 1) * tm)
        pg, pu = pre[:, :F], pre[:, F:]
        sg = jax.nn.sigmoid(pg)
        act = pg * sg
        gu[r, :F] = (hg * pu * (sg * (1.0 + pg * (1.0 - sg)))).astype(jnp.bfloat16)
        gu[r, F:] = (hg * act).astype(jnp.bfloat16)
        hid[r, :] = (act * pu).astype(jnp.bfloat16)

    cur = products(0)
    for i in range(n):
        nxt = products(i + 1) if i + 1 < n else None
        finish(i, *cur)
        cur = nxt
    x = x_ref[...]
    hd = hid[...]
    x1, y1 = at_x(s_ref), at_y(s_ref)
    block_rows = 3 * F // 4
    segments = owned_rows(F) if split else []

    def put(lo, grad):
        if not split:
            refs[0][lo : lo + grad.shape[0], :] = grad.astype(refs[0].dtype)
            return
        grad = grad + refs[0][lo : lo + grad.shape[0], :].astype(jnp.float32)
        for a, b, to in segments:
            a, b, to = max(lo, a), min(lo + grad.shape[0], b), to + max(lo - a, 0)
            if a < b:
                block, row = divmod(to, block_rows)
                slot = jnp.where((x1 if block < 2 else y1) == block % 2, 0, 1)
                part = grad[a - lo : b - lo].astype(jnp.bfloat16)
                refs[1 + block // 2][slot, row : row + b - a, :] = part

    for j in range(2 * F // tn):
        put(j * tn, mm(gu[:, j * tn : (j + 1) * tn], x, TN))
    for j in range(F // HD):
        put(2 * F + j * HD, mm(og[:, j * HD : (j + 1) * HD], hd, TN))
    if split:
        for o in range(2):
            refs[3 + 2 * o][...] = refs[1 + o][0]
            refs[4 + 2 * o][...] = refs[1 + o][1]


def gradients(position, head, fk, fv, rates_t, w1, w3, w2, received=None):
    rows = fk.shape[0]
    F = w1.shape[1]
    tm = min(256, rows)
    tn = 256 if 2 * F % 256 == 0 else HD
    once = dict(pipeline_mode=pl.Buffered(1))
    col = pl.BlockSpec((rows, F), lambda i, s: (0, head(s)), **once)
    weight = pl.BlockSpec((1, F, F), lambda i, s: (head(s), 0, 0), **once)
    whole = lambda *shape: pl.BlockSpec(shape, lambda i, s: (0,) * len(shape), **once)
    bf = jnp.bfloat16
    args = [position, fk, fv, rates_t, w1, w3, w2]
    specs = [col, col, whole(*rates_t.shape), weight, weight, weight]
    scratch = [
        pltpu.VMEM((F, 2 * F), bf),
        pltpu.VMEM((F, F), bf),
        pltpu.VMEM((rows, 2 * F), bf),
        pltpu.VMEM((rows, F), bf),
        pltpu.VMEM((rows, F), bf),
    ]
    if received is None:
        shapes = [(3 * F, F)]
    else:
        shapes = [(3 * F // 4, F)] * 4
        args.append(received)
        specs.append(whole(3 * F, F))
        scratch = [pltpu.VMEM((2, 3 * F // 4, F), bf)] * 2 + scratch
    kernel = functools.partial(grad_kernel, head=head, tm=tm, tn=tn, split=received is not None)

    def body(*refs):
        if received is None:
            return kernel(*refs)
        ins, outs, halves, rest = refs[:8], refs[8:12], refs[12:14], refs[14:]
        return kernel(*ins, *halves, *outs, *rest)

    return pl.pallas_call(
        body,
        grid_spec=pltpu.PrefetchScalarGridSpec(
            num_scalar_prefetch=1,
            grid=(1,),
            in_specs=specs,
            out_specs=[whole(*shape) for shape in shapes],
            scratch_shapes=scratch,
        ),
        out_shape=[jax.ShapeDtypeStruct(shape, bf) for shape in shapes],
        cost_estimate=pl.CostEstimate(
            flops=12 * rows * F * F, bytes_accessed=rows * F * 4 + F * F * 18, transcendentals=rows * F
        ),
        name="grads",
        compiler_params=room(40 if received is None else 36),
    )(*args)


def turn_kernel(s_ref, w1, w3, w2, o_ref, *scratch, parts):
    F = w1.shape[2]
    all_ref = scratch[0] if scratch else o_ref
    all_ref[:F, :] = w1[0].T
    all_ref[F : 2 * F, :] = w3[0].T
    all_ref[2 * F :, :] = w2[0].T
    at = 0
    for n, start in parts:
        o_ref[at : at + n, :] = all_ref[pl.ds(pl.multiple_of(start(s_ref), 8), n), :]
        at += n


def turned(position, head, w1, w3, w2, parts=()):
    F = w1.shape[1]
    weight = pl.BlockSpec((1, F, F), lambda i, s: (head(s), 0, 0))
    shape = (sum(n for n, _ in parts), F) if parts else (3 * F, F)
    return pl.pallas_call(
        functools.partial(turn_kernel, parts=parts),
        grid_spec=pltpu.PrefetchScalarGridSpec(
            num_scalar_prefetch=1,
            grid=(1,),
            in_specs=[weight] * 3,
            out_specs=pl.BlockSpec(shape, lambda i, s: (0, 0)),
            scratch_shapes=[pltpu.VMEM((3 * F, F), jnp.float32)] if parts else [],
        ),
        out_shape=jax.ShapeDtypeStruct(shape, jnp.float32),
        cost_estimate=pl.CostEstimate(flops=3 * F * F, bytes_accessed=24 * F * F, transcendentals=0),
        name="turned",
        compiler_params=room(20),
    )(position, w1, w3, w2)


def renormed(old, grad):
    new = old - grad
    old_sq = jnp.sum(old * old, axis=-1, keepdims=True)
    new_sq = jnp.sum(new * new, axis=-1, keepdims=True)
    return (new * (jnp.sqrt(old_sq) / jnp.sqrt(new_sq + EPS))).astype(jnp.bfloat16)


def renorm_kernel(s_ref, old_ref, *refs):
    out = refs[-1]
    at = 0
    for i in range(2):
        a, b, c = (ref[...].astype(jnp.float32) for ref in refs[3 * i : 3 * i + 3])
        rows = slice(at, at + a.shape[0])
        out[rows, :] = renormed(old_ref[rows, :], a + b + c)
        at += a.shape[0]


def renorm_units(position, old, upper, lower):
    rows, F = old.shape
    specs = [pl.BlockSpec((rows, F), lambda i, s: (0, 0))]
    for group in (upper, lower):
        size = group[2][0].shape[0]
        specs += [pl.BlockSpec((size, F), lambda i, s, at=at: (at(s), 0)) for _, at in group]
    return pl.pallas_call(
        renorm_kernel,
        grid_spec=pltpu.PrefetchScalarGridSpec(
            num_scalar_prefetch=1,
            grid=(1,),
            in_specs=specs,
            out_specs=pl.BlockSpec((rows, F), lambda i, s: (0, 0)),
        ),
        out_shape=jax.ShapeDtypeStruct((rows, F), jnp.bfloat16),
        cost_estimate=pl.CostEstimate(flops=10 * rows * F, bytes_accessed=12 * rows * F, transcendentals=0),
        name="renorm",
        compiler_params=room(12),
    )(position, old, *[array for array, _ in upper + lower])


def merge_kernel(s_ref, own_ref, far_ref, own_log, far_log, *rest, stride, head_of):
    o_ref = rest[-1]
    lane = lax.broadcasted_iota(jnp.int32, own_log.shape, 1)
    heads = o_ref.shape[1] // HD
    for j in range(heads):
        cs = slice(j * HD, (j + 1) * HD)
        at = pl.program_id(0) * heads + j
        pick = lambda ref, of: jnp.sum(
            jnp.where(of, ref[...].astype(jnp.float32), 0.0), axis=1, keepdims=True
        )
        own = pick(own_log, lane == at)
        far = pick(far_log, (lane == at) | (lane == at + stride) | (lane == at + 2 * stride))
        far = jnp.where(s_ref[0] == 0, -jnp.inf, far)
        top = jnp.maximum(own, far)
        own, far = jnp.exp2(own - top), jnp.exp2(far - top)
        share = own / (own + far)
        a, b = own_ref[:, cs].astype(jnp.float32), far_ref[:, cs].astype(jnp.float32)
        out = a * share + b * (1.0 - share)
        if head_of:
            per = rest[0].shape[1] // HD
            cols = pl.ds(pl.multiple_of(lax.rem(at, per) * HD, HD), HD)
            added = rest[0][:, cols]
            for ref, head in zip(rest[1 : len(head_of)], head_of[1:]):
                added = jnp.where(head(s_ref) == lax.div(at, per), ref[:, cols], added)
            out = out + added
        o_ref[:, cs] = out.astype(o_ref.dtype)


def merged(position, own, far, own_log, width, tile, head_of=(), added=(), into=None):
    rows, cols = far.shape[0], own.shape[1]
    w = width * HD
    mine = pl.BlockSpec((rows, w), lambda g, s: (tile, g))
    col = pl.BlockSpec((rows, w), lambda g, s: (0, g))
    own_logs = pl.BlockSpec((rows, HD), lambda g, s: (tile, 0))
    far_logs = pl.BlockSpec((rows, HD), lambda g, s: (0, cols // HD))
    args = [position, own, far, own_log, far, *added]
    specs = [mine, col, own_logs, far_logs] + [pl.BlockSpec(a.shape, lambda g, s: (0, 0)) for a in added]
    shape, aliases = (rows, cols), {}
    if into is not None:
        shape, aliases = into.shape, {len(args): 0}
        args.append(into)
        specs.append(ANY)
    kernel = functools.partial(merge_kernel, stride=log_stride_of(cols), head_of=head_of)
    return pl.pallas_call(
        kernel,
        grid_spec=pltpu.PrefetchScalarGridSpec(
            num_scalar_prefetch=1,
            grid=(cols // w,),
            in_specs=specs,
            out_specs=mine if into is not None else col,
        ),
        out_shape=jax.ShapeDtypeStruct(shape, jnp.bfloat16),
        input_output_aliases=aliases,
        cost_estimate=pl.CostEstimate(
            flops=8 * rows * cols, bytes_accessed=6 * rows * cols, transcendentals=rows * cols // HD
        ),
        name="merge",
        compiler_params=room(10),
    )(*args)


def gated(h, n):
    g = h[:, :n]
    return (g * jax.nn.sigmoid(g) * h[:, n:]).astype(jnp.bfloat16)


def staggered(n, first, second):
    cur = first(0)
    for i in range(n):
        nxt = first(i + 1) if i + 1 < n else None
        second(i, cur)
        cur = nxt


def for_each_chip(s_ref, body):
    chip = 2 * at_x(s_ref) + at_y(s_ref)
    for k in range(4):
        pl.when(chip == k)(functools.partial(body, k))


NEIGHBOURS = (0, 2, 1, 3)


def hidden_kernel(s_ref, q_ref, own_ref, over_x, over_y, o_ref, w_ref, *, tm, head):
    F = own_ref.shape[1]
    n = F // 4
    for i, ref in enumerate((own_ref, over_x, over_y)):
        w_ref[i * n : (i + 1) * n, :] = ref[:n, :]
        w_ref[(3 + i) * n : (4 + i) * n, :] = ref[n : 2 * n, :]
    cols = pl.ds(pl.multiple_of(head(s_ref) * F, HD), F)

    def first(i):
        return mm(q_ref[i * tm : (i + 1) * tm, cols], w_ref[...], NT)

    def second(i, h):
        o_ref[i * tm : (i + 1) * tm, : 3 * n] = gated(h, 3 * n)

    staggered(q_ref.shape[0] // tm, first, second)


VMEM = pl.BlockSpec(memory_space=pltpu.VMEM)
SMEM = pl.BlockSpec(memory_space=pltpu.SMEM)
ANY = pl.BlockSpec(memory_space=pl.ANY)


def hidden_part(position, head, fq, pieces):
    rows = fq.shape[0]
    F = pieces[0].shape[1]
    bf = jnp.bfloat16
    return pl.pallas_call(
        functools.partial(hidden_kernel, tm=min(256, rows), head=head),
        in_specs=[SMEM] + [VMEM] * 4,
        out_specs=VMEM,
        scratch_shapes=[pltpu.VMEM((3 * F // 2, F), bf)],
        out_shape=jax.ShapeDtypeStruct((rows, F), bf),
        cost_estimate=pl.CostEstimate(
            flops=3 * rows * F * F, bytes_accessed=rows * F * 4 + F * F * 3, transcendentals=rows * F
        ),
        name="hidden",
        compiler_params=room(24),
    )(position, fq, *pieces[:3])


def apply_kernel(s_ref, q_ref, *rest, tm, head, split, tiles, sources):
    attended, rest = rest[:sources], rest[sources:]
    o_ref, x_ref, n_ref, w_ref, h_ref, r_ref, sems = rest[-7:]
    F = n_ref.shape[1]
    n, m = F // 4, F // 8
    cols = pl.ds(pl.multiple_of(head(s_ref) * F, HD), F)
    if split:
        own, over_x, over_y, upper, lower = rest[1:6]
        w_ref[: n + m, :] = upper[...]
        w_ref[n + m :, :] = lower[:m, :]
    else:
        w_ref[...] = rest[0][: 2 * F, :]
        n_ref[...] = rest[0][2 * F :, :]

    def copy_out(i):
        to = pl.ds(tiles[i][0] * tm, tm)
        return pltpu.make_async_copy(r_ref.at[pl.ds(i * tm, tm), :], o_ref.at[to, cols], sems.at[i])

    def place(k):
        rows_of = ((own, 2 * n), (over_x, 2 * n), (over_y, 2 * n), (lower, m))
        for flip, (ref, row) in zip(NEIGHBOURS, rows_of):
            for j, from_flip in enumerate(NEIGHBOURS):
                to, at = (k ^ flip) * n, (k ^ from_flip) * n
                n_ref[to : to + n, j * n : (j + 1) * n] = ref[row : row + n, at : at + n]

    if split:
        for_each_chip(s_ref, place)

    def first(i):
        at = tiles[i][0] * tm
        return mm(q_ref[at : at + tm, cols], w_ref[...], NT)

    def second(i, h):
        tile, source, at = tiles[i]
        r = slice(i * tm, (i + 1) * tm)
        if split:
            h_ref[r, : 3 * n] = rest[0][tile * tm : (tile + 1) * tm, : 3 * n]
            h_ref[r, 3 * n :] = gated(h, n)
            hid = h_ref[r, :]
        else:
            hid = gated(h, F)
        out = mm(hid, n_ref[...], NT)
        if source is None:
            x_ref[...] = out
        else:
            a = attended[source][at : at + tm, cols].astype(jnp.float32)
            r_ref[r, :] = (a + out).astype(r_ref.dtype)
            copy_out(i).start()

    staggered(len(tiles), first, second)
    for i in range(len(tiles)):
        if tiles[i][1] is not None:
            copy_out(i).wait()


def apply_head(position, head, fq, hidden, pieces, attended, tiles, tm, into=None):
    rows, cols = fq.shape
    F = pieces[0].shape[1]
    split = hidden is not None
    args = [position, fq, *attended] + ([hidden] if split else []) + list(pieces)
    specs = [SMEM] + [VMEM] * (len(args) - 1)
    aliases = {}
    if into is not None:
        aliases = {len(args): 0}
        args.append(into)
        specs.append(ANY)
    bf = jnp.bfloat16
    mine = len(tiles) * tm
    return pl.pallas_call(
        functools.partial(
            apply_kernel, tm=tm, head=head, split=split, tiles=tiles, sources=len(attended)
        ),
        in_specs=specs,
        out_specs=[ANY, VMEM],
        scratch_shapes=[
            pltpu.VMEM((F, F), bf),
            pltpu.VMEM((F // 2 if split else 2 * F, F), bf),
            pltpu.VMEM((mine, F), bf),
            pltpu.VMEM((mine, F), bf),
            pltpu.SemaphoreType.DMA((len(tiles),)),
        ],
        out_shape=[jax.ShapeDtypeStruct((rows, cols), bf), jax.ShapeDtypeStruct((tm, F), jnp.float32)],
        input_output_aliases=aliases,
        cost_estimate=pl.CostEstimate(
            flops=3 * mine * F * F, bytes_accessed=mine * F * 8 + F * F * 6, transcendentals=mine * F
        ),
        name="apply",
        compiler_params=room(24),
    )(*args)


def exchange(block, bit):
    size = lax.axis_size("seq")
    return lax.ppermute(block, "seq", [(i, i ^ (1 << bit)) for i in range(size)])


def shifted(block, by):
    size = lax.axis_size("seq")
    return lax.ppermute(block, "seq", [(i, i + by) for i in range(size) if 0 <= i + by < size])


def synced(total, old, bits, position):
    offset = 0
    for bit in bits:
        half = total.shape[0] // 2
        mine = (position >> bit) & 1
        away = lax.dynamic_slice_in_dim(total, (1 - mine) * half, half, 0).astype(jnp.bfloat16)
        kept = lax.dynamic_slice_in_dim(total, mine * half, half, 0)
        total = kept + exchange(away, bit).astype(jnp.float32)
        offset = offset + mine * half
    part = renormed(lax.dynamic_slice_in_dim(old, offset, total.shape[0], 0), total)
    for bit in reversed(bits):
        mine = (position >> bit) & 1
        other = exchange(part, bit)
        part = jnp.concatenate(
            [jnp.where(mine == 0, part, other), jnp.where(mine == 0, other, part)], axis=0
        )
    return part


def synced_square(position, blocks, old):
    x, y = (position[0] >> 1) & 1, (position[0] >> 2) & 1
    keep_x, send_x, keep_y, send_y = blocks
    top0, bottom0 = exchange(send_x, 1), exchange(send_y, 2)

    def fold(a, b, at):
        n = a.shape[0] // 2
        a, b = (lax.dynamic_slice_in_dim(v, at * n, n, 0).astype(jnp.float32) for v in (a, b))
        return (a + b).astype(jnp.bfloat16)

    top1 = exchange(fold(keep_x, top0, 1 - y), 2)
    bottom1 = exchange(fold(keep_y, bottom0, 1 - x), 1)
    zero = lambda s: 0
    part = renorm_units(
        position,
        old,
        [(keep_x, at_y), (top0, at_y), (top1, zero)],
        [(keep_y, at_x), (bottom0, at_x), (bottom1, zero)],
    )
    n = top1.shape[0]
    over_x, over_y = exchange(part, 1), exchange(part, 2)
    top2, bottom2 = exchange(over_y[:n], 1), exchange(over_x[n:], 2)
    return [part, over_x, over_y, top2, bottom2]


def quarter(F, flip_x=0, flip_y=0):
    return lambda s: (2 * (at_x(s) ^ flip_x) + (at_y(s) ^ flip_y)) * (F // 4)


def shards(attn_q, attn_k, attn_v, fast_q, fast_k, fast_v, rates, fast_gate, fast_up, fast_down):
    position = lax.axis_index("seq").astype(jnp.int32).reshape(1)
    count = lax.axis_size("seq")
    heads = fast_gate.shape[0]
    rows = attn_q.shape[0]
    half = rows // 2
    width = 2 if attn_q.shape[1] // HD % 2 == 0 else 1
    prev = shifted(jnp.concatenate([attn_k[half:], attn_v[half:]], axis=0), 1)
    guests = shifted(attn_q[:half], -1)
    rates_t = rates.T
    stay = lambda a: pltpu.with_memory_space_constraint(a, pltpu.HBM)
    attn_q, attn_k, attn_v = stay(attn_q), stay(attn_k), stay(attn_v)
    fast_k, fast_v = stay(fast_k), stay(fast_v)
    weights = (stay(fast_gate), stay(fast_up), stay(fast_down))

    def grads(head, received=None):
        return gradients(position, head, fast_k, fast_v, rates_t, *weights, received)

    if heads == 2 and count == 8:
        near, far = (lambda s: s[0] & 1), (lambda s: 1 - (s[0] & 1))
        received = exchange(grads(far)[0], 0)
        F = fast_gate.shape[1]
        mine = quarter(F)
        starts = [(F // 4, lambda s, at=i * F: at + mine(s)) for i in range(3)]
        old = turned(position, near, *weights, parts=tuple(starts))
        blocks = grads(near, received)
        pieces = synced_square(position, blocks, old)
        other = [exchange(p, 0) for p in pieces]
        news = []
        for head, new in ((near, pieces), (far, other)):
            news.append((head, hidden_part(position, head, fast_q, new), new))
    else:
        news = []
        bits = list(range(count.bit_length() - 1))
        for h in range(heads):
            head = lambda s, h=h: h
            old = turned(position, head, *weights)
            new = synced(grads(head)[0].astype(jnp.float32), old, bits, position[0])
            news.append((head, None, [new]))
    bq = min(256, half)
    tiles = half // bq
    late = [
        [(0, t * bq, half, 1), (1, 0, half + (t + 1) * bq, -1)] for t in range(tiles)
    ]
    early = [[(0, 0, (t + 1) * bq, -1)] for t in range(tiles)]
    guest = [[(0, t * bq, rows, 1)] for t in range(tiles)]
    here = (attn_k, 0, attn_v, 0, rows)
    jobs = [(guests, t, guest[t : t + 1], 2) for t in range(tiles)] + [(attn_q, 0, early, 1)]
    *returned, own_out, own_log = attention(position, jobs, [here], bq, width)
    far_outs = [shifted(part, 1) for part in returned]
    (high,) = attention(position, [(attn_q, 1, late, 0)], [(prev, 0, prev, 1, half), here], bq, width)
    lows = []
    for t, part in enumerate(far_outs[:-1]):
        lows.append(merged(position, own_out, part, own_log, width, t))
    rows_of = [(t, t, 0) for t in range(tiles - 1)] + [(tiles + t, tiles - 1, t * bq) for t in range(tiles)]
    rows_of.append((tiles - 1, None, 0))
    mixed, added = None, []
    for head, hidden, new in news:
        mixed, extra = apply_head(
            position, head, fast_q, hidden, new, [*lows, high], rows_of, bq, mixed
        )
        added.append(extra)
    head_of = [head for head, _, _ in news]
    return merged(position, own_out, far_outs[-1], own_log, width, tiles - 1, head_of, added, mixed)


def solution(mesh):
    placed = (P("seq", "head"),) * 7 + (P("head", None, None),) * 3
    return jax.shard_map(shards, mesh=mesh, in_specs=placed, out_specs=P("seq", "head"), check_vma=False)
```

```python
import functools
import math

import jax
import jax.numpy as jnp
from jax import lax
from jax.experimental import pallas as pl
from jax.experimental.pallas import tpu as pltpu
from jax.sharding import PartitionSpec as P


HD = 128
EPS = 1e-06
NN = (((1,), (0,)), ((), ()))
NT = (((1,), (1,)), ((), ()))
TN = (((0,), (0,)), ((), ()))


def room(mib):
    return pltpu.CompilerParams(vmem_limit_bytes=mib << 20)


def mm(a, b, dims=NN):
    return lax.dot_general(a, b, dims, preferred_element_type=jnp.float32)


def attn_kernel(position_ref, *refs, bq, jobs, sources, log_stride):
    queries = refs[: len(jobs)]
    keys = refs[len(jobs) : len(jobs) + sources]
    values = refs[len(jobs) + sources : len(jobs) + 2 * sources]
    rest = list(refs[len(jobs) + 2 * sources :])
    outs = []
    for _, sums in jobs:
        outs.append((rest.pop(0), rest.pop(0) if sums == 1 else None))
    bufs = (rest.pop(0), rest.pop(0))
    logs = [rest.pop(0) if sums else None for _, sums in jobs]
    group = pl.program_id(0)
    heads = queries[0].shape[1] // HD
    c = math.log2(math.e) / math.sqrt(HD)
    ri = lax.broadcasted_iota(jnp.int32, (bq, bq), 0)
    ci = lax.broadcasted_iota(jnp.int32, (bq, bq), 1)
    absent = position_ref[0] == 0
    units = [(h, j, t) for h in range(heads) for j in range(len(jobs)) for t in range(len(jobs[j][0]))]

    def scores(i):
        h, j, t = units[i]
        hs = slice(h * HD, (h + 1) * HD)
        buf = bufs[i % 2]
        q = queries[j][t * bq : (t + 1) * bq, hs]
        tops = []
        at = 0
        for source, lo, hi, edge in jobs[j][0][t]:
            s = mm(q, keys[source][lo:hi, hs], NT)
            n = hi - lo
            if edge == 1:
                kept = jnp.where(ci >= ri, s[:, :bq], -jnp.inf)
                s = jnp.concatenate([kept, s[:, bq:]], axis=1) if n > bq else kept
            elif edge == -1:
                kept = jnp.where(ci <= ri, s[:, n - bq :], -jnp.inf)
                s = jnp.concatenate([s[:, : n - bq], kept], axis=1) if n > bq else kept
            buf[:, at : at + n] = s
            tops.append(jnp.max(s, axis=1, keepdims=True))
            at += n
        if len(tops) == 1:
            return [tops[0] * c]
        m = jnp.maximum(tops[1], jnp.where(absent, -jnp.inf, tops[0])) * c
        return [jnp.where(absent, 1e30, m), m]

    def finish(i, ms):
        h, j, t = units[i]
        plan, sums = jobs[j]
        hs = slice(h * HD, (h + 1) * HD)
        buf = bufs[i % 2]
        out = total = None
        at = 0
        for (source, lo, hi, _), m in zip(plan[t], ms):
            p = jnp.exp2(buf[:, at : at + hi - lo] * c - m)
            part = jnp.sum(p, axis=1, keepdims=True)
            o = mm(p.astype(jnp.bfloat16), values[source][lo:hi, hs])
            total = part if total is None else total + part
            out = o if out is None else out + o
            at += hi - lo
        rows = slice(t * bq, (t + 1) * bq)
        out = (out / total).astype(jnp.bfloat16)
        head = group * heads + h
        if sums == 2:
            outs[j][0][rows, pl.ds(pl.multiple_of(head * HD, HD), HD)] = out
        else:
            outs[j][0][rows, hs] = out
        if sums:
            lane = lax.broadcasted_iota(jnp.int32, (bq, HD), 1)
            log = ms[-1] + jnp.log(total) * math.log2(math.e)
            logs[j][rows, :] = jnp.where(lane == head, log, logs[j][rows, :])

    if any(sums for _, sums in jobs):

        @pl.when(group == 0)
        def _():
            for log in logs:
                if log is not None:
                    log[...] = jnp.zeros(log.shape, log.dtype)

    ms = scores(0)
    for i in range(len(units)):
        nxt = scores(i + 1) if i + 1 < len(units) else None
        finish(i, ms)
        ms = nxt
    if any(sums for _, sums in jobs):

        @pl.when(group == pl.num_programs(0) - 1)
        def _():
            for (_, sums), (out, log_out), log in zip(jobs, outs, logs):
                if sums == 1:
                    log_out[...] = log[...]
                if sums == 2:
                    x = log[...]
                    a = x.astype(jnp.bfloat16).astype(jnp.float32)
                    b = (x - a).astype(jnp.bfloat16).astype(jnp.float32)
                    x = a + pltpu.roll(b, log_stride, 1) + pltpu.roll(x - a - b, 2 * log_stride, 1)
                    out[:, out.shape[1] - HD :] = x.astype(jnp.bfloat16)


def log_stride_of(cols):
    return 16 * pl.cdiv(cols // HD, 16)


def attention(position, jobs, sources, bq, width):
    cols = jobs[0][0].shape[1]
    w = width * HD
    ranges = [r for _, _, plan, _ in jobs for tile in plan for r in tile]
    span = max(sum(hi - lo for _, lo, hi, _ in tile) for _, _, plan, _ in jobs for tile in plan)
    pairs = bq * sum(hi - lo for _, lo, hi, _ in ranges) * cols // HD
    block = lambda n, at: pl.BlockSpec((n, w), lambda g, f: (at, g))
    whole = lambda *shape: pl.BlockSpec(shape, lambda g, f: (0, 0))
    outs, out_specs, logs = [], [], []
    for _, _, plan, sums in jobs:
        rows = len(plan) * bq
        if sums == 2:
            outs.append(jax.ShapeDtypeStruct((rows, cols + HD), jnp.bfloat16))
            out_specs.append(whole(rows, cols + HD))
        else:
            outs.append(jax.ShapeDtypeStruct((rows, cols), jnp.bfloat16))
            out_specs.append(block(rows, 0))
        if sums == 1:
            outs.append(jax.ShapeDtypeStruct((rows, HD), jnp.float32))
            out_specs.append(whole(rows, HD))
        if sums:
            logs.append(pltpu.VMEM((rows, HD), jnp.float32))
    specs = [block(len(plan) * bq, at) for _, at, plan, _ in jobs]
    specs += [block(n, at) for _, at, _, _, n in sources] + [block(n, at) for _, _, _, at, n in sources]
    kernel = functools.partial(
        attn_kernel,
        bq=bq,
        jobs=[(plan, sums) for _, _, plan, sums in jobs],
        sources=len(sources),
        log_stride=log_stride_of(cols),
    )
    return pl.pallas_call(
        kernel,
        grid_spec=pltpu.PrefetchScalarGridSpec(
            num_scalar_prefetch=1,
            grid=(cols // w,),
            in_specs=specs,
            out_specs=out_specs,
            scratch_shapes=[pltpu.VMEM((bq, span), jnp.float32)] * 2 + logs,
        ),
        out_shape=outs,
        cost_estimate=pl.CostEstimate(
            flops=4 * pairs * HD, bytes_accessed=8 * bq * cols * len(ranges), transcendentals=pairs
        ),
        compiler_params=room(14),
    )(position, *[job[0] for job in jobs], *[x[0] for x in sources], *[x[2] for x in sources])


def owned_rows(F):
    n, m, half = F // 4, F // 8, 3 * F // 2
    unit = 3 * F // 8
    segments = []
    for k in range(4):
        upper, lower = k * unit, half + (2 * (k % 2) + k // 2) * unit
        segments += [
            (k * n, (k + 1) * n, upper),
            (F + k * n, F + k * n + m, upper + n),
            (F + k * n + m, F + (k + 1) * n, lower),
            (2 * F + k * n, 2 * F + (k + 1) * n, lower + m),
        ]
    return segments


def at_x(s):
    return (s[0] >> 1) & 1


def at_y(s):
    return (s[0] >> 2) & 1


def grad_kernel(s_ref, x_ref, v_ref, r_ref, w1_ref, w3_ref, w2_ref, *refs, head, tm, tn, split):
    w13, w2, gu, hid, og = refs[-5:]
    F = w1_ref.shape[2]
    rows = x_ref.shape[0]
    w13[:, :F] = w1_ref[0].astype(jnp.bfloat16)
    w13[:, F:] = w3_ref[0].astype(jnp.bfloat16)
    w2[...] = w2_ref[0].astype(jnp.bfloat16)
    pick = lax.broadcasted_iota(jnp.int32, r_ref.shape, 0) == head(s_ref)
    rate = jnp.sum(jnp.where(pick, r_ref[...], 0.0), axis=0, keepdims=True)
    rate = jnp.transpose(jnp.broadcast_to(rate, (8, rows)))[:, :1]
    og[...] = (-rate * v_ref[...].astype(jnp.float32)).astype(jnp.bfloat16)
    n = rows // tm

    def products(i):
        r = slice(i * tm, (i + 1) * tm)
        return mm(x_ref[r, :], w13[...]), mm(og[r, :], w2[...], NT)

    def finish(i, pre, hg):
        r = slice(i * tm, (i + 1) * tm)
        pg, pu = pre[:, :F], pre[:, F:]
        sg = jax.nn.sigmoid(pg)
        act = pg * sg
        gu[r, :F] = (hg * pu * (sg * (1.0 + pg * (1.0 - sg)))).astype(jnp.bfloat16)
        gu[r, F:] = (hg * act).astype(jnp.bfloat16)
        hid[r, :] = (act * pu).astype(jnp.bfloat16)

    cur = products(0)
    for i in range(n):
        nxt = products(i + 1) if i + 1 < n else None
        finish(i, *cur)
        cur = nxt
    x = x_ref[...]
    hd = hid[...]
    x1, y1 = at_x(s_ref), at_y(s_ref)
    block_rows = 3 * F // 4
    segments = owned_rows(F) if split else []

    def put(lo, grad):
        if not split:
            refs[0][lo : lo + grad.shape[0], :] = grad.astype(refs[0].dtype)
            return
        grad = grad + refs[0][lo : lo + grad.shape[0], :].astype(jnp.float32)
        for a, b, to in segments:
            a, b, to = max(lo, a), min(lo + grad.shape[0], b), to + max(lo - a, 0)
            if a < b:
                block, row = divmod(to, block_rows)
                slot = jnp.where((x1 if block < 2 else y1) == block % 2, 0, 1)
                part = grad[a - lo : b - lo].astype(jnp.bfloat16)
                refs[1 + block // 2][slot, row : row + b - a, :] = part

    for j in range(2 * F // tn):
        put(j * tn, mm(gu[:, j * tn : (j + 1) * tn], x, TN))
    for j in range(F // HD):
        put(2 * F + j * HD, mm(og[:, j * HD : (j + 1) * HD], hd, TN))
    if split:
        for o in range(2):
            refs[3 + 2 * o][...] = refs[1 + o][0]
            refs[4 + 2 * o][...] = refs[1 + o][1]


def gradients(position, head, fk, fv, rates_t, w1, w3, w2, received=None):
    rows = fk.shape[0]
    F = w1.shape[1]
    tm = min(256, rows)
    tn = 256 if 2 * F % 256 == 0 else HD
    once = dict(pipeline_mode=pl.Buffered(1))
    col = pl.BlockSpec((rows, F), lambda i, s: (0, head(s)), **once)
    weight = pl.BlockSpec((1, F, F), lambda i, s: (head(s), 0, 0), **once)
    whole = lambda *shape: pl.BlockSpec(shape, lambda i, s: (0,) * len(shape), **once)
    bf = jnp.bfloat16
    args = [position, fk, fv, rates_t, w1, w3, w2]
    specs = [col, col, whole(*rates_t.shape), weight, weight, weight]
    scratch = [
        pltpu.VMEM((F, 2 * F), bf),
        pltpu.VMEM((F, F), bf),
        pltpu.VMEM((rows, 2 * F), bf),
        pltpu.VMEM((rows, F), bf),
        pltpu.VMEM((rows, F), bf),
    ]
    if received is None:
        shapes = [(3 * F, F)]
    else:
        shapes = [(3 * F // 4, F)] * 4
        args.append(received)
        specs.append(whole(3 * F, F))
        scratch = [pltpu.VMEM((2, 3 * F // 4, F), bf)] * 2 + scratch
    kernel = functools.partial(grad_kernel, head=head, tm=tm, tn=tn, split=received is not None)

    def body(*refs):
        if received is None:
            return kernel(*refs)
        ins, outs, halves, rest = refs[:8], refs[8:12], refs[12:14], refs[14:]
        return kernel(*ins, *halves, *outs, *rest)

    return pl.pallas_call(
        body,
        grid_spec=pltpu.PrefetchScalarGridSpec(
            num_scalar_prefetch=1,
            grid=(1,),
            in_specs=specs,
            out_specs=[whole(*shape) for shape in shapes],
            scratch_shapes=scratch,
        ),
        out_shape=[jax.ShapeDtypeStruct(shape, bf) for shape in shapes],
        cost_estimate=pl.CostEstimate(
            flops=12 * rows * F * F, bytes_accessed=rows * F * 4 + F * F * 18, transcendentals=rows * F
        ),
        name="grads",
        compiler_params=room(40 if received is None else 36),
    )(*args)


def turn_kernel(s_ref, w1, w3, w2, o_ref, *scratch, parts):
    F = w1.shape[2]
    all_ref = scratch[0] if scratch else o_ref
    all_ref[:F, :] = w1[0].T
    all_ref[F : 2 * F, :] = w3[0].T
    all_ref[2 * F :, :] = w2[0].T
    at = 0
    for n, start in parts:
        o_ref[at : at + n, :] = all_ref[pl.ds(pl.multiple_of(start(s_ref), 8), n), :]
        at += n


def turned(position, head, w1, w3, w2, parts=()):
    F = w1.shape[1]
    weight = pl.BlockSpec((1, F, F), lambda i, s: (head(s), 0, 0))
    shape = (sum(n for n, _ in parts), F) if parts else (3 * F, F)
    return pl.pallas_call(
        functools.partial(turn_kernel, parts=parts),
        grid_spec=pltpu.PrefetchScalarGridSpec(
            num_scalar_prefetch=1,
            grid=(1,),
            in_specs=[weight] * 3,
            out_specs=pl.BlockSpec(shape, lambda i, s: (0, 0)),
            scratch_shapes=[pltpu.VMEM((3 * F, F), jnp.float32)] if parts else [],
        ),
        out_shape=jax.ShapeDtypeStruct(shape, jnp.float32),
        cost_estimate=pl.CostEstimate(flops=3 * F * F, bytes_accessed=24 * F * F, transcendentals=0),
        name="turned",
        compiler_params=room(20),
    )(position, w1, w3, w2)


def renormed(old, grad):
    new = old - grad
    old_sq = jnp.sum(old * old, axis=-1, keepdims=True)
    new_sq = jnp.sum(new * new, axis=-1, keepdims=True)
    return (new * (jnp.sqrt(old_sq) / jnp.sqrt(new_sq + EPS))).astype(jnp.bfloat16)


def renorm_kernel(s_ref, old_ref, *refs):
    out = refs[-1]
    at = 0
    for i in range(2):
        a, b, c = (ref[...].astype(jnp.float32) for ref in refs[3 * i : 3 * i + 3])
        rows = slice(at, at + a.shape[0])
        out[rows, :] = renormed(old_ref[rows, :], a + b + c)
        at += a.shape[0]


def renorm_units(position, old, upper, lower):
    rows, F = old.shape
    specs = [pl.BlockSpec((rows, F), lambda i, s: (0, 0))]
    for group in (upper, lower):
        size = group[2][0].shape[0]
        specs += [pl.BlockSpec((size, F), lambda i, s, at=at: (at(s), 0)) for _, at in group]
    return pl.pallas_call(
        renorm_kernel,
        grid_spec=pltpu.PrefetchScalarGridSpec(
            num_scalar_prefetch=1,
            grid=(1,),
            in_specs=specs,
            out_specs=pl.BlockSpec((rows, F), lambda i, s: (0, 0)),
        ),
        out_shape=jax.ShapeDtypeStruct((rows, F), jnp.bfloat16),
        cost_estimate=pl.CostEstimate(flops=10 * rows * F, bytes_accessed=12 * rows * F, transcendentals=0),
        name="renorm",
        compiler_params=room(12),
    )(position, old, *[array for array, _ in upper + lower])


def merge_kernel(s_ref, own_ref, far_ref, own_log, far_log, *rest, stride, head_of):
    o_ref = rest[-1]
    lane = lax.broadcasted_iota(jnp.int32, own_log.shape, 1)
    heads = o_ref.shape[1] // HD
    for j in range(heads):
        cs = slice(j * HD, (j + 1) * HD)
        at = pl.program_id(0) * heads + j
        pick = lambda ref, of: jnp.sum(
            jnp.where(of, ref[...].astype(jnp.float32), 0.0), axis=1, keepdims=True
        )
        own = pick(own_log, lane == at)
        far = pick(far_log, (lane == at) | (lane == at + stride) | (lane == at + 2 * stride))
        far = jnp.where(s_ref[0] == 0, -jnp.inf, far)
        top = jnp.maximum(own, far)
        own, far = jnp.exp2(own - top), jnp.exp2(far - top)
        share = own / (own + far)
        a, b = own_ref[:, cs].astype(jnp.float32), far_ref[:, cs].astype(jnp.float32)
        out = a * share + b * (1.0 - share)
        if head_of:
            per = rest[0].shape[1] // HD
            cols = pl.ds(pl.multiple_of(lax.rem(at, per) * HD, HD), HD)
            added = rest[0][:, cols]
            for ref, head in zip(rest[1 : len(head_of)], head_of[1:]):
                added = jnp.where(head(s_ref) == lax.div(at, per), ref[:, cols], added)
            out = out + added
        o_ref[:, cs] = out.astype(o_ref.dtype)


def merged(position, own, far, own_log, width, tile, head_of=(), added=(), into=None):
    rows, cols = far.shape[0], own.shape[1]
    w = width * HD
    mine = pl.BlockSpec((rows, w), lambda g, s: (tile, g))
    col = pl.BlockSpec((rows, w), lambda g, s: (0, g))
    own_logs = pl.BlockSpec((rows, HD), lambda g, s: (tile, 0))
    far_logs = pl.BlockSpec((rows, HD), lambda g, s: (0, cols // HD))
    args = [position, own, far, own_log, far, *added]
    specs = [mine, col, own_logs, far_logs] + [pl.BlockSpec(a.shape, lambda g, s: (0, 0)) for a in added]
    shape, aliases = (rows, cols), {}
    if into is not None:
        shape, aliases = into.shape, {len(args): 0}
        args.append(into)
        specs.append(ANY)
    kernel = functools.partial(merge_kernel, stride=log_stride_of(cols), head_of=head_of)
    return pl.pallas_call(
        kernel,
        grid_spec=pltpu.PrefetchScalarGridSpec(
            num_scalar_prefetch=1,
            grid=(cols // w,),
            in_specs=specs,
            out_specs=mine if into is not None else col,
        ),
        out_shape=jax.ShapeDtypeStruct(shape, jnp.bfloat16),
        input_output_aliases=aliases,
        cost_estimate=pl.CostEstimate(
            flops=8 * rows * cols, bytes_accessed=6 * rows * cols, transcendentals=rows * cols // HD
        ),
        name="merge",
        compiler_params=room(12),
    )(*args)


def gated(h, n):
    g = h[:, :n]
    return (g * jax.nn.sigmoid(g) * h[:, n:]).astype(jnp.bfloat16)


def staggered(n, first, second):
    cur = first(0)
    for i in range(n):
        nxt = first(i + 1) if i + 1 < n else None
        second(i, cur)
        cur = nxt


def for_each_chip(s_ref, body):
    chip = 2 * at_x(s_ref) + at_y(s_ref)
    for k in range(4):
        pl.when(chip == k)(functools.partial(body, k))


NEIGHBOURS = (0, 2, 1, 3)


def hidden_kernel(s_ref, q_ref, own_ref, over_x, over_y, o_ref, w_ref, *, tm, head):
    F = own_ref.shape[1]
    n = F // 4
    for i, ref in enumerate((own_ref, over_x, over_y)):
        w_ref[i * n : (i + 1) * n, :] = ref[:n, :]
        w_ref[(3 + i) * n : (4 + i) * n, :] = ref[n : 2 * n, :]
    cols = pl.ds(pl.multiple_of(head(s_ref) * F, HD), F)

    def first(i):
        return mm(q_ref[i * tm : (i + 1) * tm, cols], w_ref[...], NT)

    def second(i, h):
        o_ref[i * tm : (i + 1) * tm, : 3 * n] = gated(h, 3 * n)

    staggered(q_ref.shape[0] // tm, first, second)


VMEM = pl.BlockSpec(memory_space=pltpu.VMEM)
SMEM = pl.BlockSpec(memory_space=pltpu.SMEM)
ANY = pl.BlockSpec(memory_space=pl.ANY)


def hidden_part(position, head, fq, pieces):
    rows = fq.shape[0]
    F = pieces[0].shape[1]
    bf = jnp.bfloat16
    return pl.pallas_call(
        functools.partial(hidden_kernel, tm=min(256, rows), head=head),
        in_specs=[SMEM] + [VMEM] * 4,
        out_specs=VMEM,
        scratch_shapes=[pltpu.VMEM((3 * F // 2, F), bf)],
        out_shape=jax.ShapeDtypeStruct((rows, F), bf),
        cost_estimate=pl.CostEstimate(
            flops=3 * rows * F * F, bytes_accessed=rows * F * 4 + F * F * 3, transcendentals=rows * F
        ),
        name="hidden",
        compiler_params=room(24),
    )(position, fq, *pieces[:3])


def apply_kernel(s_ref, q_ref, *rest, tm, head, split, tiles, sources):
    attended, rest = rest[:sources], rest[sources:]
    o_ref, x_ref, n_ref, w_ref, h_ref, r_ref, sems = rest[-7:]
    F = n_ref.shape[1]
    n, m = F // 4, F // 8
    cols = pl.ds(pl.multiple_of(head(s_ref) * F, HD), F)
    if split:
        own, over_x, over_y, upper, lower = rest[1:6]
        w_ref[: n + m, :] = upper[...]
        w_ref[n + m :, :] = lower[:m, :]
    else:
        w_ref[...] = rest[0][: 2 * F, :]
        n_ref[...] = rest[0][2 * F :, :]

    def copy_out(i):
        to = pl.ds(tiles[i][0] * tm, tm)
        return pltpu.make_async_copy(r_ref.at[pl.ds(i * tm, tm), :], o_ref.at[to, cols], sems.at[i])

    def place(k):
        rows_of = ((own, 2 * n), (over_x, 2 * n), (over_y, 2 * n), (lower, m))
        for flip, (ref, row) in zip(NEIGHBOURS, rows_of):
            for j, from_flip in enumerate(NEIGHBOURS):
                to, at = (k ^ flip) * n, (k ^ from_flip) * n
                n_ref[to : to + n, j * n : (j + 1) * n] = ref[row : row + n, at : at + n]

    if split:
        for_each_chip(s_ref, place)

    def first(i):
        at = tiles[i][0] * tm
        return mm(q_ref[at : at + tm, cols], w_ref[...], NT)

    def second(i, h):
        tile, source, at = tiles[i]
        r = slice(i * tm, (i + 1) * tm)
        if split:
            h_ref[r, : 3 * n] = rest[0][tile * tm : (tile + 1) * tm, : 3 * n]
            h_ref[r, 3 * n :] = gated(h, n)
            hid = h_ref[r, :]
        else:
            hid = gated(h, F)
        out = mm(hid, n_ref[...], NT)
        if source is None:
            x_ref[...] = out
        else:
            a = attended[source][at : at + tm, cols].astype(jnp.float32)
            r_ref[r, :] = (a + out).astype(r_ref.dtype)
            copy_out(i).start()

    staggered(len(tiles), first, second)
    for i in range(len(tiles)):
        if tiles[i][1] is not None:
            copy_out(i).wait()


def apply_head(position, head, fq, hidden, pieces, attended, tiles, tm, into=None):
    rows, cols = fq.shape
    F = pieces[0].shape[1]
    split = hidden is not None
    args = [position, fq, *attended] + ([hidden] if split else []) + list(pieces)
    specs = [SMEM] + [VMEM] * (len(args) - 1)
    aliases = {}
    if into is not None:
        aliases = {len(args): 0}
        args.append(into)
        specs.append(ANY)
    bf = jnp.bfloat16
    mine = len(tiles) * tm
    return pl.pallas_call(
        functools.partial(
            apply_kernel, tm=tm, head=head, split=split, tiles=tiles, sources=len(attended)
        ),
        in_specs=specs,
        out_specs=[ANY, VMEM],
        scratch_shapes=[
            pltpu.VMEM((F, F), bf),
            pltpu.VMEM((F // 2 if split else 2 * F, F), bf),
            pltpu.VMEM((mine, F), bf),
            pltpu.VMEM((mine, F), bf),
            pltpu.SemaphoreType.DMA((len(tiles),)),
        ],
        out_shape=[jax.ShapeDtypeStruct((rows, cols), bf), jax.ShapeDtypeStruct((tm, F), jnp.float32)],
        input_output_aliases=aliases,
        cost_estimate=pl.CostEstimate(
            flops=3 * mine * F * F, bytes_accessed=mine * F * 8 + F * F * 6, transcendentals=mine * F
        ),
        name="apply",
        compiler_params=room(24),
    )(*args)


def exchange(block, bit):
    size = lax.axis_size("seq")
    return lax.ppermute(block, "seq", [(i, i ^ (1 << bit)) for i in range(size)])


def shifted(block, by):
    size = lax.axis_size("seq")
    return lax.ppermute(block, "seq", [(i, i + by) for i in range(size) if 0 <= i + by < size])


def synced(total, old, bits, position):
    offset = 0
    for bit in bits:
        half = total.shape[0] // 2
        mine = (position >> bit) & 1
        away = lax.dynamic_slice_in_dim(total, (1 - mine) * half, half, 0).astype(jnp.bfloat16)
        kept = lax.dynamic_slice_in_dim(total, mine * half, half, 0)
        total = kept + exchange(away, bit).astype(jnp.float32)
        offset = offset + mine * half
    part = renormed(lax.dynamic_slice_in_dim(old, offset, total.shape[0], 0), total)
    for bit in reversed(bits):
        mine = (position >> bit) & 1
        other = exchange(part, bit)
        part = jnp.concatenate(
            [jnp.where(mine == 0, part, other), jnp.where(mine == 0, other, part)], axis=0
        )
    return part


def synced_square(position, blocks, old):
    x, y = (position[0] >> 1) & 1, (position[0] >> 2) & 1
    keep_x, send_x, keep_y, send_y = blocks
    top0, bottom0 = exchange(send_x, 1), exchange(send_y, 2)

    def fold(a, b, at):
        n = a.shape[0] // 2
        a, b = (lax.dynamic_slice_in_dim(v, at * n, n, 0).astype(jnp.float32) for v in (a, b))
        return (a + b).astype(jnp.bfloat16)

    top1 = exchange(fold(keep_x, top0, 1 - y), 2)
    bottom1 = exchange(fold(keep_y, bottom0, 1 - x), 1)
    zero = lambda s: 0
    part = renorm_units(
        position,
        old,
        [(keep_x, at_y), (top0, at_y), (top1, zero)],
        [(keep_y, at_x), (bottom0, at_x), (bottom1, zero)],
    )
    n = top1.shape[0]
    over_x, over_y = exchange(part, 1), exchange(part, 2)
    top2, bottom2 = exchange(over_y[:n], 1), exchange(over_x[n:], 2)
    return [part, over_x, over_y, top2, bottom2]


def quarter(F, flip_x=0, flip_y=0):
    return lambda s: (2 * (at_x(s) ^ flip_x) + (at_y(s) ^ flip_y)) * (F // 4)


def shards(attn_q, attn_k, attn_v, fast_q, fast_k, fast_v, rates, fast_gate, fast_up, fast_down):
    position = lax.axis_index("seq").astype(jnp.int32).reshape(1)
    count = lax.axis_size("seq")
    heads = fast_gate.shape[0]
    rows = attn_q.shape[0]
    half = rows // 2
    width = 2 if attn_q.shape[1] // HD % 2 == 0 else 1
    prev = shifted(jnp.concatenate([attn_k[half:], attn_v[half:]], axis=0), 1)
    guests = shifted(attn_q[:half], -1)
    rates_t = rates.T
    stay = lambda a: pltpu.with_memory_space_constraint(a, pltpu.HBM)
    attn_q, attn_k, attn_v = stay(attn_q), stay(attn_k), stay(attn_v)
    fast_k, fast_v = stay(fast_k), stay(fast_v)
    weights = (stay(fast_gate), stay(fast_up), stay(fast_down))

    def grads(head, received=None):
        return gradients(position, head, fast_k, fast_v, rates_t, *weights, received)

    if heads == 2 and count == 8:
        near, far = (lambda s: s[0] & 1), (lambda s: 1 - (s[0] & 1))
        received = exchange(grads(far)[0], 0)
        F = fast_gate.shape[1]
        mine = quarter(F)
        starts = [(F // 4, lambda s, at=i * F: at + mine(s)) for i in range(3)]
        old = turned(position, near, *weights, parts=tuple(starts))
        blocks = grads(near, received)
        pieces = synced_square(position, blocks, old)
        other = [exchange(p, 0) for p in pieces]
        news = []
        for head, new in ((near, pieces), (far, other)):
            news.append((head, hidden_part(position, head, fast_q, new), new))
    else:
        news = []
        bits = list(range(count.bit_length() - 1))
        for h in range(heads):
            head = lambda s, h=h: h
            old = turned(position, head, *weights)
            new = synced(grads(head)[0].astype(jnp.float32), old, bits, position[0])
            news.append((head, None, [new]))
    bq = min(256, half)
    tiles = half // bq
    late = [
        [(0, t * bq, half, 1), (1, 0, half + (t + 1) * bq, -1)] for t in range(tiles)
    ]
    early = [[(0, 0, (t + 1) * bq, -1)] for t in range(tiles)]
    guest = [[(0, t * bq, rows, 1)] for t in range(tiles)]
    here = (attn_k, 0, attn_v, 0, rows)
    jobs = [(guests, t, guest[t : t + 1], 2) for t in range(tiles)] + [(attn_q, 0, early, 1)]
    *returned, own_out, own_log = attention(position, jobs, [here], bq, width)
    far_outs = [shifted(part, 1) for part in returned]
    (high,) = attention(position, [(attn_q, 1, late, 0)], [(prev, 0, prev, 1, half), here], bq, width)
    lows = []
    for t, part in enumerate(far_outs[:-1]):
        lows.append(merged(position, own_out, part, own_log, width, t))
    rows_of = [(t, t, 0) for t in range(tiles - 1)] + [(tiles + t, tiles - 1, t * bq) for t in range(tiles)]
    rows_of.append((tiles - 1, None, 0))
    mixed, added = None, []
    for head, hidden, new in news:
        mixed, extra = apply_head(
            position, head, fast_q, hidden, new, [*lows, high], rows_of, bq, mixed
        )
        added.append(extra)
    head_of = [head for head, _, _ in news]
    span = attn_q.shape[1] // HD
    wide = span // 2 if span % 2 == 0 else 1
    return merged(position, own_out, far_outs[-1], own_log, wide, tiles - 1, head_of, added, mixed)


def solution(mesh):
    placed = (P("seq", "head"),) * 7 + (P("head", None, None),) * 3
    return jax.shard_map(shards, mesh=mesh, in_specs=placed, out_specs=P("seq", "head"), check_vma=False)
```

```python
import functools
import math

import jax
import jax.numpy as jnp
from jax import lax
from jax.experimental import pallas as pl
from jax.experimental.pallas import tpu as pltpu
from jax.sharding import PartitionSpec as P


HD = 128
EPS = 1e-06
NN = (((1,), (0,)), ((), ()))
NT = (((1,), (1,)), ((), ()))
TN = (((0,), (0,)), ((), ()))


def room(mib):
    return pltpu.CompilerParams(vmem_limit_bytes=mib << 20)


def mm(a, b, dims=NN):
    return lax.dot_general(a, b, dims, preferred_element_type=jnp.float32)


def attn_kernel(position_ref, *refs, bq, jobs, sources, log_stride):
    queries = refs[: len(jobs)]
    keys = refs[len(jobs) : len(jobs) + sources]
    values = refs[len(jobs) + sources : len(jobs) + 2 * sources]
    rest = list(refs[len(jobs) + 2 * sources :])
    outs = []
    for _, sums in jobs:
        outs.append((rest.pop(0), rest.pop(0) if sums == 1 else None))
    bufs = (rest.pop(0), rest.pop(0))
    logs = [rest.pop(0) if sums else None for _, sums in jobs]
    group = pl.program_id(0)
    heads = queries[0].shape[1] // HD
    c = math.log2(math.e) / math.sqrt(HD)
    ri = lax.broadcasted_iota(jnp.int32, (bq, bq), 0)
    ci = lax.broadcasted_iota(jnp.int32, (bq, bq), 1)
    absent = position_ref[0] == 0
    units = [(h, j, t) for h in range(heads) for j in range(len(jobs)) for t in range(len(jobs[j][0]))]

    def scores(i):
        h, j, t = units[i]
        hs = slice(h * HD, (h + 1) * HD)
        buf = bufs[i % 2]
        q = queries[j][t * bq : (t + 1) * bq, hs]
        tops = []
        at = 0
        for source, lo, hi, edge in jobs[j][0][t]:
            s = mm(q, keys[source][lo:hi, hs], NT)
            n = hi - lo
            if edge == 1:
                kept = jnp.where(ci >= ri, s[:, :bq], -jnp.inf)
                s = jnp.concatenate([kept, s[:, bq:]], axis=1) if n > bq else kept
            elif edge == -1:
                kept = jnp.where(ci <= ri, s[:, n - bq :], -jnp.inf)
                s = jnp.concatenate([s[:, : n - bq], kept], axis=1) if n > bq else kept
            buf[:, at : at + n] = s
            tops.append(jnp.max(s, axis=1, keepdims=True))
            at += n
        if len(tops) == 1:
            return [tops[0] * c]
        m = jnp.maximum(tops[1], jnp.where(absent, -jnp.inf, tops[0])) * c
        return [jnp.where(absent, 1e30, m), m]

    def finish(i, ms):
        h, j, t = units[i]
        plan, sums = jobs[j]
        hs = slice(h * HD, (h + 1) * HD)
        buf = bufs[i % 2]
        out = total = None
        at = 0
        for (source, lo, hi, _), m in zip(plan[t], ms):
            p = jnp.exp2(buf[:, at : at + hi - lo] * c - m)
            part = jnp.sum(p, axis=1, keepdims=True)
            o = mm(p.astype(jnp.bfloat16), values[source][lo:hi, hs])
            total = part if total is None else total + part
            out = o if out is None else out + o
            at += hi - lo
        rows = slice(t * bq, (t + 1) * bq)
        out = (out / total).astype(jnp.bfloat16)
        head = group * heads + h
        if sums == 2:
            outs[j][0][rows, pl.ds(pl.multiple_of(head * HD, HD), HD)] = out
        else:
            outs[j][0][rows, hs] = out
        if sums:
            lane = lax.broadcasted_iota(jnp.int32, (bq, HD), 1)
            log = ms[-1] + jnp.log(total) * math.log2(math.e)
            logs[j][rows, :] = jnp.where(lane == head, log, logs[j][rows, :])

    if any(sums for _, sums in jobs):

        @pl.when(group == 0)
        def _():
            for log in logs:
                if log is not None:
                    log[...] = jnp.zeros(log.shape, log.dtype)

    ms = scores(0)
    for i in range(len(units)):
        nxt = scores(i + 1) if i + 1 < len(units) else None
        finish(i, ms)
        ms = nxt
    if any(sums for _, sums in jobs):

        @pl.when(group == pl.num_programs(0) - 1)
        def _():
            for (_, sums), (out, log_out), log in zip(jobs, outs, logs):
                if sums == 1:
                    log_out[...] = log[...]
                if sums == 2:
                    x = log[...]
                    a = x.astype(jnp.bfloat16).astype(jnp.float32)
                    b = (x - a).astype(jnp.bfloat16).astype(jnp.float32)
                    x = a + pltpu.roll(b, log_stride, 1) + pltpu.roll(x - a - b, 2 * log_stride, 1)
                    out[:, out.shape[1] - HD :] = x.astype(jnp.bfloat16)


def log_stride_of(cols):
    return 16 * pl.cdiv(cols // HD, 16)


def attention(position, jobs, sources, bq, width):
    cols = jobs[0][0].shape[1]
    w = width * HD
    ranges = [r for _, _, plan, _ in jobs for tile in plan for r in tile]
    span = max(sum(hi - lo for _, lo, hi, _ in tile) for _, _, plan, _ in jobs for tile in plan)
    pairs = bq * sum(hi - lo for _, lo, hi, _ in ranges) * cols // HD
    block = lambda n, at: pl.BlockSpec((n, w), lambda g, f: (at, g))
    whole = lambda *shape: pl.BlockSpec(shape, lambda g, f: (0, 0))
    outs, out_specs, logs = [], [], []
    for _, _, plan, sums in jobs:
        rows = len(plan) * bq
        if sums == 2:
            outs.append(jax.ShapeDtypeStruct((rows, cols + HD), jnp.bfloat16))
            out_specs.append(whole(rows, cols + HD))
        else:
            outs.append(jax.ShapeDtypeStruct((rows, cols), jnp.bfloat16))
            out_specs.append(block(rows, 0))
        if sums == 1:
            outs.append(jax.ShapeDtypeStruct((rows, HD), jnp.float32))
            out_specs.append(whole(rows, HD))
        if sums:
            logs.append(pltpu.VMEM((rows, HD), jnp.float32))
    specs = [block(len(plan) * bq, at) for _, at, plan, _ in jobs]
    specs += [block(n, at) for _, at, _, _, n in sources] + [block(n, at) for _, _, _, at, n in sources]
    kernel = functools.partial(
        attn_kernel,
        bq=bq,
        jobs=[(plan, sums) for _, _, plan, sums in jobs],
        sources=len(sources),
        log_stride=log_stride_of(cols),
    )
    return pl.pallas_call(
        kernel,
        grid_spec=pltpu.PrefetchScalarGridSpec(
            num_scalar_prefetch=1,
            grid=(cols // w,),
            in_specs=specs,
            out_specs=out_specs,
            scratch_shapes=[pltpu.VMEM((bq, span), jnp.float32)] * 2 + logs,
        ),
        out_shape=outs,
        cost_estimate=pl.CostEstimate(
            flops=4 * pairs * HD, bytes_accessed=8 * bq * cols * len(ranges), transcendentals=pairs
        ),
        compiler_params=room(14),
    )(position, *[job[0] for job in jobs], *[x[0] for x in sources], *[x[2] for x in sources])


def owned_rows(F):
    n, m, half = F // 4, F // 8, 3 * F // 2
    unit = 3 * F // 8
    segments = []
    for k in range(4):
        upper, lower = k * unit, half + (2 * (k % 2) + k // 2) * unit
        segments += [
            (k * n, (k + 1) * n, upper),
            (F + k * n, F + k * n + m, upper + n),
            (F + k * n + m, F + (k + 1) * n, lower),
            (2 * F + k * n, 2 * F + (k + 1) * n, lower + m),
        ]
    return segments


def at_x(s):
    return (s[0] >> 1) & 1


def at_y(s):
    return (s[0] >> 2) & 1


def grad_kernel(s_ref, x_ref, v_ref, r_ref, w1_ref, w3_ref, w2_ref, *refs, head, tm, tn, split):
    w13, w2, gu, hid, og = refs[-5:]
    F = w1_ref.shape[2]
    rows = x_ref.shape[0]
    w13[:, :F] = w1_ref[0].astype(jnp.bfloat16)
    w13[:, F:] = w3_ref[0].astype(jnp.bfloat16)
    w2[...] = w2_ref[0].astype(jnp.bfloat16)
    pick = lax.broadcasted_iota(jnp.int32, r_ref.shape, 0) == head(s_ref)
    rate = jnp.sum(jnp.where(pick, r_ref[...], 0.0), axis=0, keepdims=True)
    rate = jnp.transpose(jnp.broadcast_to(rate, (8, rows)))[:, :1]
    og[...] = (-rate * v_ref[...].astype(jnp.float32)).astype(jnp.bfloat16)
    n = rows // tm

    def products(i):
        r = slice(i * tm, (i + 1) * tm)
        return mm(x_ref[r, :], w13[...]), mm(og[r, :], w2[...], NT)

    def finish(i, pre, hg):
        r = slice(i * tm, (i + 1) * tm)
        pg, pu = pre[:, :F], pre[:, F:]
        sg = jax.nn.sigmoid(pg)
        act = pg * sg
        gu[r, :F] = (hg * pu * (sg * (1.0 + pg * (1.0 - sg)))).astype(jnp.bfloat16)
        gu[r, F:] = (hg * act).astype(jnp.bfloat16)
        hid[r, :] = (act * pu).astype(jnp.bfloat16)

    cur = products(0)
    for i in range(n):
        nxt = products(i + 1) if i + 1 < n else None
        finish(i, *cur)
        cur = nxt
    x = x_ref[...]
    hd = hid[...]
    x1, y1 = at_x(s_ref), at_y(s_ref)
    block_rows = 3 * F // 4
    segments = owned_rows(F) if split else []

    def put(lo, grad):
        if not split:
            refs[0][lo : lo + grad.shape[0], :] = grad.astype(refs[0].dtype)
            return
        grad = grad + refs[0][lo : lo + grad.shape[0], :].astype(jnp.float32)
        for a, b, to in segments:
            a, b, to = max(lo, a), min(lo + grad.shape[0], b), to + max(lo - a, 0)
            if a < b:
                block, row = divmod(to, block_rows)
                slot = jnp.where((x1 if block < 2 else y1) == block % 2, 0, 1)
                part = grad[a - lo : b - lo].astype(jnp.bfloat16)
                refs[1 + block // 2][slot, row : row + b - a, :] = part

    for j in range(2 * F // tn):
        put(j * tn, mm(gu[:, j * tn : (j + 1) * tn], x, TN))
    for j in range(F // HD):
        put(2 * F + j * HD, mm(og[:, j * HD : (j + 1) * HD], hd, TN))
    if split:
        for o in range(2):
            refs[3 + 2 * o][...] = refs[1 + o][0]
            refs[4 + 2 * o][...] = refs[1 + o][1]


def gradients(position, head, fk, fv, rates_t, w1, w3, w2, received=None):
    rows = fk.shape[0]
    F = w1.shape[1]
    tm = min(256, rows)
    tn = 256 if 2 * F % 256 == 0 else HD
    once = dict(pipeline_mode=pl.Buffered(1))
    col = pl.BlockSpec((rows, F), lambda i, s: (0, head(s)), **once)
    weight = pl.BlockSpec((1, F, F), lambda i, s: (head(s), 0, 0), **once)
    whole = lambda *shape: pl.BlockSpec(shape, lambda i, s: (0,) * len(shape), **once)
    bf = jnp.bfloat16
    args = [position, fk, fv, rates_t, w1, w3, w2]
    specs = [col, col, whole(*rates_t.shape), weight, weight, weight]
    scratch = [
        pltpu.VMEM((F, 2 * F), bf),
        pltpu.VMEM((F, F), bf),
        pltpu.VMEM((rows, 2 * F), bf),
        pltpu.VMEM((rows, F), bf),
        pltpu.VMEM((rows, F), bf),
    ]
    if received is None:
        shapes = [(3 * F, F)]
    else:
        shapes = [(3 * F // 4, F)] * 4
        args.append(received)
        specs.append(whole(3 * F, F))
        scratch = [pltpu.VMEM((2, 3 * F // 4, F), bf)] * 2 + scratch
    kernel = functools.partial(grad_kernel, head=head, tm=tm, tn=tn, split=received is not None)

    def body(*refs):
        if received is None:
            return kernel(*refs)
        ins, outs, halves, rest = refs[:8], refs[8:12], refs[12:14], refs[14:]
        return kernel(*ins, *halves, *outs, *rest)

    return pl.pallas_call(
        body,
        grid_spec=pltpu.PrefetchScalarGridSpec(
            num_scalar_prefetch=1,
            grid=(1,),
            in_specs=specs,
            out_specs=[whole(*shape) for shape in shapes],
            scratch_shapes=scratch,
        ),
        out_shape=[jax.ShapeDtypeStruct(shape, bf) for shape in shapes],
        cost_estimate=pl.CostEstimate(
            flops=12 * rows * F * F, bytes_accessed=rows * F * 4 + F * F * 18, transcendentals=rows * F
        ),
        name="grads",
        compiler_params=room(40 if received is None else 36),
    )(*args)


def turn_kernel(s_ref, w1, w3, w2, o_ref, *scratch, parts):
    F = w1.shape[2]
    all_ref = scratch[0] if scratch else o_ref
    all_ref[:F, :] = w1[0].T
    all_ref[F : 2 * F, :] = w3[0].T
    all_ref[2 * F :, :] = w2[0].T
    at = 0
    for n, start in parts:
        o_ref[at : at + n, :] = all_ref[pl.ds(pl.multiple_of(start(s_ref), 8), n), :]
        at += n


def turned(position, head, w1, w3, w2, parts=()):
    F = w1.shape[1]
    weight = pl.BlockSpec((1, F, F), lambda i, s: (head(s), 0, 0))
    shape = (sum(n for n, _ in parts), F) if parts else (3 * F, F)
    return pl.pallas_call(
        functools.partial(turn_kernel, parts=parts),
        grid_spec=pltpu.PrefetchScalarGridSpec(
            num_scalar_prefetch=1,
            grid=(1,),
            in_specs=[weight] * 3,
            out_specs=pl.BlockSpec(shape, lambda i, s: (0, 0)),
            scratch_shapes=[pltpu.VMEM((3 * F, F), jnp.float32)] if parts else [],
        ),
        out_shape=jax.ShapeDtypeStruct(shape, jnp.float32),
        cost_estimate=pl.CostEstimate(flops=3 * F * F, bytes_accessed=24 * F * F, transcendentals=0),
        name="turned",
        compiler_params=room(20),
    )(position, w1, w3, w2)


def renormed(old, grad):
    new = old - grad
    old_sq = jnp.sum(old * old, axis=-1, keepdims=True)
    new_sq = jnp.sum(new * new, axis=-1, keepdims=True)
    return (new * (jnp.sqrt(old_sq) / jnp.sqrt(new_sq + EPS))).astype(jnp.bfloat16)


def renorm_kernel(s_ref, old_ref, *refs):
    out = refs[-1]
    at = 0
    for i in range(2):
        a, b, c = (ref[...].astype(jnp.float32) for ref in refs[3 * i : 3 * i + 3])
        rows = slice(at, at + a.shape[0])
        out[rows, :] = renormed(old_ref[rows, :], a + b + c)
        at += a.shape[0]


def renorm_units(position, old, upper, lower):
    rows, F = old.shape
    specs = [pl.BlockSpec((rows, F), lambda i, s: (0, 0))]
    for group in (upper, lower):
        size = group[2][0].shape[0]
        specs += [pl.BlockSpec((size, F), lambda i, s, at=at: (at(s), 0)) for _, at in group]
    return pl.pallas_call(
        renorm_kernel,
        grid_spec=pltpu.PrefetchScalarGridSpec(
            num_scalar_prefetch=1,
            grid=(1,),
            in_specs=specs,
            out_specs=pl.BlockSpec((rows, F), lambda i, s: (0, 0)),
        ),
        out_shape=jax.ShapeDtypeStruct((rows, F), jnp.bfloat16),
        cost_estimate=pl.CostEstimate(flops=10 * rows * F, bytes_accessed=12 * rows * F, transcendentals=0),
        name="renorm",
        compiler_params=room(12),
    )(position, old, *[array for array, _ in upper + lower])


def merge_kernel(s_ref, own_ref, far_ref, own_log, far_log, *rest, stride, head_of):
    o_ref = rest[-1]
    lane = lax.broadcasted_iota(jnp.int32, own_log.shape, 1)
    heads = o_ref.shape[1] // HD
    for j in range(heads):
        cs = slice(j * HD, (j + 1) * HD)
        at = pl.program_id(0) * heads + j
        pick = lambda ref, of: jnp.sum(
            jnp.where(of, ref[...].astype(jnp.float32), 0.0), axis=1, keepdims=True
        )
        own = pick(own_log, lane == at)
        far = pick(far_log, (lane == at) | (lane == at + stride) | (lane == at + 2 * stride))
        far = jnp.where(s_ref[0] == 0, -jnp.inf, far)
        top = jnp.maximum(own, far)
        own, far = jnp.exp2(own - top), jnp.exp2(far - top)
        share = own / (own + far)
        a, b = own_ref[:, cs].astype(jnp.float32), far_ref[:, cs].astype(jnp.float32)
        out = a * share + b * (1.0 - share)
        if head_of:
            per = rest[0].shape[1] // HD
            cols = pl.ds(pl.multiple_of(lax.rem(at, per) * HD, HD), HD)
            added = rest[0][:, cols]
            for ref, head in zip(rest[1 : len(head_of)], head_of[1:]):
                added = jnp.where(head(s_ref) == lax.div(at, per), ref[:, cols], added)
            out = out + added
        o_ref[:, cs] = out.astype(o_ref.dtype)


def merged(position, own, far, own_log, width, tile, head_of=(), added=(), into=None):
    rows, cols = far.shape[0], own.shape[1]
    w = width * HD
    mine = pl.BlockSpec((rows, w), lambda g, s: (tile, g))
    col = pl.BlockSpec((rows, w), lambda g, s: (0, g))
    own_logs = pl.BlockSpec((rows, HD), lambda g, s: (tile, 0))
    far_logs = pl.BlockSpec((rows, HD), lambda g, s: (0, cols // HD))
    args = [position, own, far, own_log, far, *added]
    specs = [mine, col, own_logs, far_logs] + [pl.BlockSpec(a.shape, lambda g, s: (0, 0)) for a in added]
    shape, aliases = (rows, cols), {}
    if into is not None:
        shape, aliases = into.shape, {len(args): 0}
        args.append(into)
        specs.append(ANY)
    kernel = functools.partial(merge_kernel, stride=log_stride_of(cols), head_of=head_of)
    return pl.pallas_call(
        kernel,
        grid_spec=pltpu.PrefetchScalarGridSpec(
            num_scalar_prefetch=1,
            grid=(cols // w,),
            in_specs=specs,
            out_specs=mine if into is not None else col,
        ),
        out_shape=jax.ShapeDtypeStruct(shape, jnp.bfloat16),
        input_output_aliases=aliases,
        cost_estimate=pl.CostEstimate(
            flops=8 * rows * cols, bytes_accessed=6 * rows * cols, transcendentals=rows * cols // HD
        ),
        name="merge",
        compiler_params=room(12),
    )(*args)


def gated(h, n):
    g = h[:, :n]
    return (g * jax.nn.sigmoid(g) * h[:, n:]).astype(jnp.bfloat16)


def staggered(n, first, second):
    cur = first(0)
    for i in range(n):
        nxt = first(i + 1) if i + 1 < n else None
        second(i, cur)
        cur = nxt


def for_each_chip(s_ref, body):
    chip = 2 * at_x(s_ref) + at_y(s_ref)
    for k in range(4):
        pl.when(chip == k)(functools.partial(body, k))


NEIGHBOURS = (0, 2, 1, 3)


def hidden_kernel(s_ref, q_ref, own_ref, over_x, over_y, o_ref, w_ref, *, tm, head):
    F = own_ref.shape[1]
    n = F // 4
    for i, ref in enumerate((own_ref, over_x, over_y)):
        w_ref[i * n : (i + 1) * n, :] = ref[:n, :]
        w_ref[(3 + i) * n : (4 + i) * n, :] = ref[n : 2 * n, :]
    cols = pl.ds(pl.multiple_of(head(s_ref) * F, HD), F)

    def first(i):
        return mm(q_ref[i * tm : (i + 1) * tm, cols], w_ref[...], NT)

    def second(i, h):
        o_ref[i * tm : (i + 1) * tm, : 3 * n] = gated(h, 3 * n)

    staggered(q_ref.shape[0] // tm, first, second)


VMEM = pl.BlockSpec(memory_space=pltpu.VMEM)
SMEM = pl.BlockSpec(memory_space=pltpu.SMEM)
ANY = pl.BlockSpec(memory_space=pl.ANY)


def hidden_part(position, head, fq, pieces):
    rows = fq.shape[0]
    F = pieces[0].shape[1]
    bf = jnp.bfloat16
    return pl.pallas_call(
        functools.partial(hidden_kernel, tm=min(256, rows), head=head),
        in_specs=[SMEM] + [VMEM] * 4,
        out_specs=VMEM,
        scratch_shapes=[pltpu.VMEM((3 * F // 2, F), bf)],
        out_shape=jax.ShapeDtypeStruct((rows, F), bf),
        cost_estimate=pl.CostEstimate(
            flops=3 * rows * F * F, bytes_accessed=rows * F * 4 + F * F * 3, transcendentals=rows * F
        ),
        name="hidden",
        compiler_params=room(24),
    )(position, fq, *pieces[:3])


def apply_kernel(s_ref, q_ref, *rest, tm, head, split, tiles, sources):
    attended, rest = rest[:sources], rest[sources:]
    o_ref, x_ref, n_ref, w_ref, h_ref, r_ref, sems = rest[-7:]
    F = n_ref.shape[1]
    n, m = F // 4, F // 8
    cols = pl.ds(pl.multiple_of(head(s_ref) * F, HD), F)
    if split:
        own, over_x, over_y, upper, lower = rest[1:6]
        w_ref[: n + m, :] = upper[...]
        w_ref[n + m :, :] = lower[:m, :]
    else:
        w_ref[...] = rest[0][: 2 * F, :]
        n_ref[...] = rest[0][2 * F :, :]

    def copy_out(i):
        to = pl.ds(tiles[i][0] * tm, tm)
        return pltpu.make_async_copy(r_ref.at[pl.ds(i * tm, tm), :], o_ref.at[to, cols], sems.at[i])

    def place(k):
        rows_of = ((own, 2 * n), (over_x, 2 * n), (over_y, 2 * n), (lower, m))
        for flip, (ref, row) in zip(NEIGHBOURS, rows_of):
            for j, from_flip in enumerate(NEIGHBOURS):
                to, at = (k ^ flip) * n, (k ^ from_flip) * n
                n_ref[to : to + n, j * n : (j + 1) * n] = ref[row : row + n, at : at + n]

    if split:
        for_each_chip(s_ref, place)

    def first(i):
        at = tiles[i][0] * tm
        return mm(q_ref[at : at + tm, cols], w_ref[...], NT)

    def second(i, h):
        tile, source, at = tiles[i]
        r = slice(i * tm, (i + 1) * tm)
        if split:
            h_ref[r, : 3 * n] = rest[0][tile * tm : (tile + 1) * tm, : 3 * n]
            h_ref[r, 3 * n :] = gated(h, n)
            hid = h_ref[r, :]
        else:
            hid = gated(h, F)
        out = mm(hid, n_ref[...], NT)
        if source is None:
            x_ref[...] = out
        else:
            a = attended[source][at : at + tm, cols].astype(jnp.float32)
            r_ref[r, :] = (a + out).astype(r_ref.dtype)
            copy_out(i).start()

    staggered(len(tiles), first, second)
    for i in range(len(tiles)):
        if tiles[i][1] is not None:
            copy_out(i).wait()


def apply_head(position, head, fq, hidden, pieces, attended, tiles, tm, into=None):
    rows, cols = fq.shape
    F = pieces[0].shape[1]
    split = hidden is not None
    args = [position, fq, *attended] + ([hidden] if split else []) + list(pieces)
    specs = [SMEM] + [VMEM] * (len(args) - 1)
    aliases = {}
    if into is not None:
        aliases = {len(args): 0}
        args.append(into)
        specs.append(ANY)
    bf = jnp.bfloat16
    mine = len(tiles) * tm
    return pl.pallas_call(
        functools.partial(
            apply_kernel, tm=tm, head=head, split=split, tiles=tiles, sources=len(attended)
        ),
        in_specs=specs,
        out_specs=[ANY, VMEM],
        scratch_shapes=[
            pltpu.VMEM((F, F), bf),
            pltpu.VMEM((F // 2 if split else 2 * F, F), bf),
            pltpu.VMEM((mine, F), bf),
            pltpu.VMEM((mine, F), bf),
            pltpu.SemaphoreType.DMA((len(tiles),)),
        ],
        out_shape=[jax.ShapeDtypeStruct((rows, cols), bf), jax.ShapeDtypeStruct((tm, F), jnp.float32)],
        input_output_aliases=aliases,
        cost_estimate=pl.CostEstimate(
            flops=3 * mine * F * F, bytes_accessed=mine * F * 8 + F * F * 6, transcendentals=mine * F
        ),
        name="apply",
        compiler_params=room(24),
    )(*args)


def exchange(block, bit):
    size = lax.axis_size("seq")
    return lax.ppermute(block, "seq", [(i, i ^ (1 << bit)) for i in range(size)])


def shifted(block, by):
    size = lax.axis_size("seq")
    return lax.ppermute(block, "seq", [(i, i + by) for i in range(size) if 0 <= i + by < size])


def synced(total, old, bits, position):
    offset = 0
    for bit in bits:
        half = total.shape[0] // 2
        mine = (position >> bit) & 1
        away = lax.dynamic_slice_in_dim(total, (1 - mine) * half, half, 0).astype(jnp.bfloat16)
        kept = lax.dynamic_slice_in_dim(total, mine * half, half, 0)
        total = kept + exchange(away, bit).astype(jnp.float32)
        offset = offset + mine * half
    part = renormed(lax.dynamic_slice_in_dim(old, offset, total.shape[0], 0), total)
    for bit in reversed(bits):
        mine = (position >> bit) & 1
        other = exchange(part, bit)
        part = jnp.concatenate(
            [jnp.where(mine == 0, part, other), jnp.where(mine == 0, other, part)], axis=0
        )
    return part


def synced_square(position, blocks, old):
    x, y = (position[0] >> 1) & 1, (position[0] >> 2) & 1
    keep_x, send_x, keep_y, send_y = blocks
    top0, bottom0 = exchange(send_x, 1), exchange(send_y, 2)

    def fold(a, b, at):
        n = a.shape[0] // 2
        a, b = (lax.dynamic_slice_in_dim(v, at * n, n, 0).astype(jnp.float32) for v in (a, b))
        return (a + b).astype(jnp.bfloat16)

    top1 = exchange(fold(keep_x, top0, 1 - y), 2)
    bottom1 = exchange(fold(keep_y, bottom0, 1 - x), 1)
    zero = lambda s: 0
    part = renorm_units(
        position,
        old,
        [(keep_x, at_y), (top0, at_y), (top1, zero)],
        [(keep_y, at_x), (bottom0, at_x), (bottom1, zero)],
    )
    n = top1.shape[0]
    over_x, over_y = exchange(part, 1), exchange(part, 2)
    top2, bottom2 = exchange(over_y[:n], 1), exchange(over_x[n:], 2)
    return [part, over_x, over_y, top2, bottom2]


def quarter(F, flip_x=0, flip_y=0):
    return lambda s: (2 * (at_x(s) ^ flip_x) + (at_y(s) ^ flip_y)) * (F // 4)


def shards(attn_q, attn_k, attn_v, fast_q, fast_k, fast_v, rates, fast_gate, fast_up, fast_down):
    position = lax.axis_index("seq").astype(jnp.int32).reshape(1)
    count = lax.axis_size("seq")
    heads = fast_gate.shape[0]
    rows = attn_q.shape[0]
    half = rows // 2
    width = 2 if attn_q.shape[1] // HD % 2 == 0 else 1
    asked = attn_q[:half]
    guests = shifted(asked, -1)
    later_k, later_v, _ = lax.optimization_barrier((attn_k, attn_v, asked))
    prev = shifted(jnp.concatenate([later_k[half:], later_v[half:]], axis=0), 1)
    rates_t = rates.T
    stay = lambda a: pltpu.with_memory_space_constraint(a, pltpu.HBM)
    attn_q, attn_k, attn_v = stay(attn_q), stay(attn_k), stay(attn_v)
    fast_k, fast_v = stay(fast_k), stay(fast_v)
    weights = (stay(fast_gate), stay(fast_up), stay(fast_down))

    def grads(head, received=None):
        return gradients(position, head, fast_k, fast_v, rates_t, *weights, received)

    if heads == 2 and count == 8:
        near, far = (lambda s: s[0] & 1), (lambda s: 1 - (s[0] & 1))
        received = exchange(grads(far)[0], 0)
        F = fast_gate.shape[1]
        mine = quarter(F)
        starts = [(F // 4, lambda s, at=i * F: at + mine(s)) for i in range(3)]
        old = turned(position, near, *weights, parts=tuple(starts))
        blocks = grads(near, received)
        pieces = synced_square(position, blocks, old)
        other = [exchange(p, 0) for p in pieces]
        news = []
        for head, new in ((near, pieces), (far, other)):
            news.append((head, hidden_part(position, head, fast_q, new), new))
    else:
        news = []
        bits = list(range(count.bit_length() - 1))
        for h in range(heads):
            head = lambda s, h=h: h
            old = turned(position, head, *weights)
            new = synced(grads(head)[0].astype(jnp.float32), old, bits, position[0])
            news.append((head, None, [new]))
    bq = min(256, half)
    tiles = half // bq
    late = [
        [(0, t * bq, half, 1), (1, 0, half + (t + 1) * bq, -1)] for t in range(tiles)
    ]
    early = [[(0, 0, (t + 1) * bq, -1)] for t in range(tiles)]
    guest = [[(0, t * bq, rows, 1)] for t in range(tiles)]
    here = (attn_k, 0, attn_v, 0, rows)
    jobs = [(guests, t, guest[t : t + 1], 2) for t in range(tiles)] + [(attn_q, 0, early, 1)]
    *returned, own_out, own_log = attention(position, jobs, [here], bq, width)
    far_outs = [shifted(part, 1) for part in returned]
    (high,) = attention(position, [(attn_q, 1, late, 0)], [(prev, 0, prev, 1, half), here], bq, width)
    lows = []
    for t, part in enumerate(far_outs[:-1]):
        lows.append(merged(position, own_out, part, own_log, width, t))
    rows_of = [(t, t, 0) for t in range(tiles - 1)] + [(tiles + t, tiles - 1, t * bq) for t in range(tiles)]
    rows_of.append((tiles - 1, None, 0))
    mixed, added = None, []
    for head, hidden, new in news:
        mixed, extra = apply_head(
            position, head, fast_q, hidden, new, [*lows, high], rows_of, bq, mixed
        )
        added.append(extra)
    head_of = [head for head, _, _ in news]
    span = attn_q.shape[1] // HD
    wide = span // 2 if span % 2 == 0 else 1
    return merged(position, own_out, far_outs[-1], own_log, wide, tiles - 1, head_of, added, mixed)


def solution(mesh):
    placed = (P("seq", "head"),) * 7 + (P("head", None, None),) * 3
    return jax.shard_map(shards, mesh=mesh, in_specs=placed, out_specs=P("seq", "head"), check_vma=False)
```
